256 devices in a mesh: mem: 4 (over z_lo), hor: 16 (over y, x), grp: 4 (over z_hi, core).
Axes of the slice: x: 4, y: 4, z: 8 (z_hi: 2, z_lo: 4; z = z_hi * 4 + z_lo), core: 2. Of those that a mesh axis runs over, the one named last changes fastest.
Arguments:
- ensemble: float32 [128, 2, 32, 8192], P(('mem', 'grp'), None, None, 'hor'), may hold values from -1 to 1
- coupling: float32 [32, 32], replicated, may hold values from -1 to 1
- obs_column: int32 [2, 16, 16, 512], P(None, ('mem', 'grp'), 'hor'), may hold values from 0 to 511
- obs_level: int32 [2, 16, 16, 512], P(None, ('mem', 'grp'), 'hor'), may hold values from 0 to 1
- obs_value: float32 [2, 16, 16, 512], P(None, ('mem', 'grp'), 'hor'), may hold values from -6 to 6
- obs_error: float32 [2, 16, 16, 512], P(None, ('mem', 'grp'), 'hor'), may hold values from 0.25 to 4
- obs_live: int32 [2, 16, 16, 512], P(None, ('mem', 'grp'), 'hor'), may hold values 0 or 1
- partners: int32 [16, 16, 2], P(('mem', 'grp'), 'hor'), may hold values from 0 to 15, as said below
Outputs:
- analysed: float32 [128, 2, 32, 8192], P(('mem', 'grp'), None, None, 'hor')
The draws below stay inside these ranges and needn't reach their ends.
Inputs may be any that keep to these rules, and one draw needn't show every extreme that they name: `partners`: each row holds 2 different slab numbers, none of them the row's own slab.
All inputs are finite; a program needn't handle non-finite values. No bound on the sum of `obs_live` on one device may be relied on, other than what follows from the above.
Results may differ from the reference program's by a relative error of at most 0.0003.
Values sent between devices are 32-bit elements; how exact they have to be, the bound alone decides.
No kernel may reach another device: no remote copies, remote signals or barrier semaphores. Data moves between devices by JAX's collectives and lax.ppermute only.
A program may use at most 64 MiB of HBM per device.

```python
import math
import jax
import jax.numpy as jnp
from jax import lax

MEMBERS = 128
LEVELS = 32
COL_DEV = 512
OBS_SLOTS = 512
SUBSTEPS = 4
CYCLES = 2
ROOT_STEPS = 8
PARTNER_COUNT = 2
SLABS = 16
TILES = 16
SLAB_LEVELS = 2
COLUMNS = 8192


def draw_partners(key, part):
    first_key, second_key = jax.random.split(jax.random.fold_in(key, 7))
    first = jax.random.randint(first_key, (SLABS, TILES), 1, SLABS)
    second = jax.random.randint(second_key, (SLABS, TILES), 1, SLABS - 1)
    second = second + (second >= first).astype(jnp.int32)
    own_slab = jnp.arange(SLABS, dtype=jnp.int32)[:, None]
    chosen = jnp.stack([(own_slab + first) % SLABS, (own_slab + second) % SLABS], axis=-1)
    return chosen.astype(jnp.int32)


def place_ends(drawn, own_key, smallest, top_value):
    spot = [jax.random.randint(jax.random.fold_in(own_key, axis), (), 0, length) for axis, length in enumerate(drawn.shape)]
    main_axis = drawn.shape.index(max(drawn.shape))
    neighbour = spot[:main_axis] + [(spot[main_axis] + 1) % drawn.shape[main_axis]] + spot[main_axis + 1:]
    return drawn.at[tuple(spot)].set(smallest).at[tuple(neighbour)].set(top_value)


def block_levels(key, extent, cuts, least, top_value):
    gain = 1.0
    for axis_at, shards_of in cuts:
        draws = jax.random.uniform(jax.random.fold_in(jax.random.fold_in(key, 6), axis_at), (shards_of,), jnp.float32, least / len(cuts), top_value / len(cuts))
        gain = gain * jnp.repeat(jnp.exp(draws), extent[axis_at] // shards_of).reshape((-1,) + (1,) * (len(extent) - 1 - axis_at))
    return gain


def gaussian(stream_key, dims, scale, bound, pieces=(), held_as=jnp.bfloat16):
    array = jax.random.normal(stream_key, dims, jnp.float32) * scale
    if len(pieces) > 0:
        array = block_levels(stream_key, dims, pieces, -0.22, 0.18) * array
    return jnp.clip(array, min=-bound, max=bound).astype(held_as)


def setup_inputs(seed: int = 0) -> dict:
    streams_of = jax.random.split(jax.random.key(seed), 9)
    ensemble = gaussian(streams_of[0], (MEMBERS, 2, LEVELS, COLUMNS), 0.25, 1.0, ((0, 16), (3, 16)), jnp.float32)
    coupling = gaussian(streams_of[1], (LEVELS, LEVELS), LEVELS ** -0.5, 1.0, (), jnp.float32)
    obs_column = place_ends(jax.random.randint(streams_of[2], (CYCLES, SLABS, TILES, OBS_SLOTS), 0, COL_DEV), jax.random.fold_in(streams_of[2], 1), 0, COL_DEV - 1).astype(jnp.int32)
    obs_level = place_ends(jax.random.randint(streams_of[3], (CYCLES, SLABS, TILES, OBS_SLOTS), 0, SLAB_LEVELS), jax.random.fold_in(streams_of[3], 1), 0, SLAB_LEVELS - 1).astype(jnp.int32)
    obs_value = gaussian(streams_of[4], (CYCLES, SLABS, TILES, OBS_SLOTS), 1.0, 6.0, ((1, 16), (2, 16)), jnp.float32)
    obs_error = jnp.clip(jnp.exp(math.log(4.0) - 2.7725887 * jax.random.uniform(streams_of[5], (CYCLES, SLABS, TILES, OBS_SLOTS), jnp.float32) ** block_levels(streams_of[5], (CYCLES, SLABS, TILES, OBS_SLOTS), ((1, 16), (2, 16)), -0.2, 0.2)), 0.25, 4.0)
    obs_live = place_ends((jax.random.randint(streams_of[6], (CYCLES, SLABS, TILES, OBS_SLOTS), 0, 4) < 3).astype(jnp.int32), jax.random.fold_in(streams_of[6], 1), 0, 1)
    partners = draw_partners(jax.random.fold_in(streams_of[8], 71), 0)
    return {"ensemble": ensemble, "coupling": coupling, "obs_column": obs_column, "obs_level": obs_level, "obs_value": obs_value, "obs_error": obs_error, "obs_live": obs_live, "partners": partners}


time_step = 0.2

def centred(field):
    return (jnp.roll(field, -1, axis=-1) - jnp.roll(field, 1, axis=-1)) * 0.5

def substep(velocity, height, coupling):
    pressure = jnp.einsum('lk,mkc->mlc', coupling, height, precision=lax.Precision.HIGHEST)
    moved = velocity - time_step * (velocity * centred(velocity) + centred(pressure))
    fluxes = moved * height
    height_new = height - time_step * centred(fluxes)
    return (moved, height_new)

def observe(patch, column, level, value, error, live):
    width = patch.shape[0]
    cells = patch.shape[-1]
    heights = patch[:, 1].reshape(width, -1)
    position = (level * cells + column).astype(jnp.int32)
    observed = jnp.take(heights, position, axis=1)
    average = lax.optimization_barrier(jnp.mean(observed, axis=0))
    anomalies = observed - average
    weight = live.astype(jnp.float32) / error
    gram_matrix = jnp.dot(anomalies * weight, anomalies.T, precision=lax.Precision.HIGHEST)
    innovation = jnp.dot(anomalies, weight * (value - average), precision=lax.Precision.HIGHEST)
    return (gram_matrix, innovation)

def analyse(patch, gram_sum, vector_sum, count):
    width = patch.shape[0]
    identity = jnp.eye(width, dtype=jnp.float32)
    blended = (width - 1.0) * identity + gram_sum / (count + 1.0)
    bvector = vector_sum / (count + 1.0)
    frobenius = jnp.sqrt(jnp.sum(blended * blended))
    iterate = blended / frobenius
    inverse_root = identity
    for step_index in range(ROOT_STEPS):
        newton = 1.5 * identity - 0.5 * jnp.dot(inverse_root, iterate, precision=lax.Precision.HIGHEST)
        iterate = jnp.dot(iterate, newton, precision=lax.Precision.HIGHEST)
        inverse_root = jnp.dot(newton, inverse_root, precision=lax.Precision.HIGHEST)
    spread = inverse_root * (jnp.sqrt(width - 1.0) / jnp.sqrt(frobenius))
    inner = jnp.dot(inverse_root, bvector, precision=lax.Precision.HIGHEST)
    mean_weight = jnp.dot(inverse_root, inner, precision=lax.Precision.HIGHEST) / frobenius
    transform = mean_weight[:, None] + spread
    flat = patch.reshape(width, -1)
    average = lax.optimization_barrier(jnp.mean(flat, axis=0))
    anomalies = flat - average
    result = average + jnp.dot(transform.T, anomalies, precision=lax.Precision.HIGHEST)
    return result.reshape(patch.shape)

def reference(ensemble, coupling, obs_column, obs_level, obs_value, obs_error, obs_live, partners):
    members = ensemble
    tile_index = jnp.arange(TILES, dtype=jnp.int32)[None, :]
    for cycle_index in range(CYCLES):
        velocity, height = (members[:, 0], members[:, 1])
        for step_index in range(SUBSTEPS):
            velocity, height = substep(velocity, height, coupling)
        members = jnp.stack([velocity, height], axis=1)
        patches = members.reshape(MEMBERS, 2, SLABS, SLAB_LEVELS, TILES, COL_DEV).transpose(2, 4, 0, 1, 3, 5)
        flat_patches = patches.reshape(SLABS * TILES, MEMBERS, 2, SLAB_LEVELS, COL_DEV)

        def observe_one(items):
            return observe(items[0], items[1], items[2], items[3], items[4], items[5])
        grams, vectors = lax.map(observe_one, (flat_patches, obs_column[cycle_index].reshape(-1, OBS_SLOTS), obs_level[cycle_index].reshape(-1, OBS_SLOTS), obs_value[cycle_index].reshape(-1, OBS_SLOTS), obs_error[cycle_index].reshape(-1, OBS_SLOTS), obs_live[cycle_index].reshape(-1, OBS_SLOTS)))
        grams = grams.reshape(SLABS, TILES, MEMBERS, MEMBERS)
        vectors = vectors.reshape(SLABS, TILES, MEMBERS)
        gram_sum = grams
        vector_sum = vectors
        for which in range(PARTNER_COUNT):
            gram_sum = gram_sum + grams[partners[:, :, which], tile_index]
            vector_sum = vector_sum + vectors[partners[:, :, which], tile_index]

        def analyse_one(items):
            return analyse(items[0], items[1], items[2], PARTNER_COUNT)
        updated = lax.map(analyse_one, (flat_patches, gram_sum.reshape(-1, MEMBERS, MEMBERS), vector_sum.reshape(-1, MEMBERS)))
        members = updated.reshape(SLABS, TILES, MEMBERS, 2, SLAB_LEVELS, COL_DEV).transpose(2, 3, 0, 4, 1, 5).reshape(MEMBERS, 2, LEVELS, COLUMNS)
    return members
```

```python
import functools
import math

import jax
import jax.numpy as jnp
from jax import lax
from jax.experimental import pallas as pl
from jax.experimental.pallas import tpu as pltpu
from jax.sharding import Mesh, PartitionSpec as P

SUBSTEPS = 4
ROOT_STEPS = 8
TIME_STEP = 0.2
GROUP = 16
WIDTH = 128
LEVELS = 32
COLS = 512
MINE = COLS // GROUP
HALO = 2 * SUBSTEPS
WIDE = MINE + 2 * HALO
FOLD = 72
F32 = jnp.float32
BF16 = jnp.bfloat16
VMEM_LIMIT = 48 * 1024 * 1024
ALL = ("mem", "hor", "zh", "core")
TILE = ("mem", "zh", "core")
CHIPS = ("mem", "zh")


def block_of(g):
    return ((g >> 1) & 1) * 8 + (g >> 2) * 2 + (g & 1)


MEMBER_AT = {block_of(g): g for g in range(GROUP)}


def split(a):
    high = a.astype(BF16)
    return high, (a - high.astype(F32)).astype(BF16)


def dot_split(a, b, dims=((1,), (0,))):
    dims = (dims, ((), ()))
    dot = functools.partial(lax.dot_general, dimension_numbers=dims, preferred_element_type=F32)
    return dot(a[0], b[0]) + (dot(a[0], b[1]) + dot(a[1], b[0]))


def iota(shape, dim):
    return lax.broadcasted_iota(jnp.int32, shape, dim)


def chunk_transpose(rows):
    lane = iota(rows[0].shape, 1)
    out = []
    for p in range(4):
        total = None
        for q in range(4):
            piece = rows[q] if p == q else pltpu.roll(rows[q], (32 * (q - p)) % 128, 1)
            total = piece if total is None else jnp.where(lane >= 32 * q, piece, total)
        out.append(total)
    return out


def pack_kernel(ens, column, level, value, error, live, partner, out, tiles):
    for t in range(4):
        tiles[pl.ds(512 * t, 512), :] = ens[:, pl.ds(128 * t, 128)]
    for m in range(8):
        for t in range(4):
            rows = []
            for f in range(2):
                for j in range(2):
                    rows.append(tiles[pl.ds(512 * t + (m * 2 + f) * LEVELS + j, 16, stride=2), :])
            for p, block in enumerate(chunk_transpose(rows)):
                g = MEMBER_AT[4 * t + p]
                out[pl.ds(g * 136 + m, 16, stride=8), :] = block
    member = iota((GROUP, COLS), 0)
    place = ((member >> 1) & 1) * 8 + (member >> 2) * 2 + (member & 1)
    spot = iota((64, COLS), 0)
    zero = jnp.zeros((64, COLS), F32)
    for cycle in range(2):
        col = column[cycle : cycle + 1, :]
        weight = live[cycle : cycle + 1, :].astype(F32) / error[cycle : cycle + 1, :]
        weighted = weight * value[cycle : cycle + 1, :]
        here = (col >> 5) == place
        left = jnp.concatenate([jnp.where(here, weight, 0.0), jnp.where(here, weighted, 0.0)], axis=1)
        hit = jnp.where(level[cycle : cycle + 1, :] * 32 + (col & 31) == spot, 1.0, 0.0)
        right = jnp.concatenate(
            [jnp.concatenate([hit, zero], axis=1), jnp.concatenate([zero, hit], axis=1)], axis=0
        )
        sums = lax.dot_general(
            left, right, (((1,), (1,)), ((), ())), precision=lax.Precision.HIGHEST, preferred_element_type=F32
        )
        out[pl.ds(128 + cycle, GROUP, stride=136), :] = sums
    lane = iota((GROUP, 128), 1)
    first = partner[0].astype(F32)
    second = partner[1].astype(F32)
    out[pl.ds(130, GROUP, stride=136), :] = jnp.where(lane == 0, first, second)


def unpack_kernel(got, state, low, high, hist, table):
    for s in range(GROUP):
        square = jnp.concatenate([got[pl.ds(g * 136 + s * 8, 8), :] for g in range(GROUP)], axis=0).T
        for f in range(2):
            for j in range(2):
                at = (f * 2 + j) * 32
                state[pl.ds(f * MINE * LEVELS + 2 * s + j, MINE, stride=LEVELS), :] = square[at : at + 32, :]
    for f in range(2):
        edge = HALO * LEVELS
        low[pl.ds(f * edge, edge), :] = state[pl.ds(f * MINE * LEVELS, edge), :]
        high[pl.ds(f * edge, edge), :] = state[pl.ds((f + 1) * MINE * LEVELS - edge, edge), :]
    for cycle in range(2):
        rows = got[pl.ds(128 + cycle, GROUP, stride=136), :]
        hist[pl.ds(cycle * 128, 128), :] = jnp.concatenate([rows, jnp.zeros((128 - GROUP, 128), F32)], axis=0).T
    table[...] = got[pl.ds(130, GROUP, stride=136), :].astype(jnp.int32)


def fold(top, bottom, vector):
    row, lane = iota((64, 128), 0), iota((64, 128), 1)
    body = jnp.where((lane >= 64) | (row <= lane), top, pltpu.roll(bottom, 64, 1))
    diagonal = jnp.sum(jnp.where(lane == row + 64, bottom, 0.0), axis=0, keepdims=True)
    tail = jnp.where(iota((8, 128), 0) == 0, diagonal, vector)
    return body, tail


def unfold(body, tail):
    row, lane = iota((64, 128), 0), iota((64, 128), 1)
    top = jnp.where((lane >= 64) | (row < lane), body, jnp.where(row == lane, 0.5 * body, 0.0))
    moved = pltpu.roll(body, 64, 1)
    bottom = jnp.where(row > lane - 64, moved, jnp.where(row == lane - 64, 0.5 * tail[0:1, :], 0.0))
    bottom = jnp.where(lane >= 64, bottom, 0.0)
    half = jnp.concatenate([top, bottom], axis=0)
    return half + half.T, tail[1:2, :]


def forecast_kernel(cycle, table, core, state, low, high, hist, mixing, out, keep, send, us, hs, ps, fs):
    edge = HALO * LEVELS
    span = MINE * LEVELS
    for f, ref in enumerate((us, hs)):
        ref[pl.ds(0, edge), :] = low[pl.ds(f * edge, edge), :]
        ref[pl.ds(edge, span), :] = state[pl.ds(f * span, span), :]
        ref[pl.ds(edge + span, edge), :] = high[pl.ds(f * edge, edge), :]
    rate = 0.5 * TIME_STEP
    mix = (mixing[pl.ds(0, 256), :].astype(BF16), mixing[pl.ds(256, 256), :].astype(BF16))

    def col(ref, c):
        return ref[pl.ds(c * LEVELS, LEVELS), :]

    for step in range(SUBSTEPS):
        lo, hi = 2 * step, WIDE - 2 * step
        for pair in range(3):
            block = jnp.concatenate(
                [hs[pl.ds(pair * 512, 256), :], hs[pl.ds(pair * 512 + 256, 256), :]], axis=1
            )
            pressure = dot_split(mix, split(block))
            ps[pl.ds(pair * 512, 256), :] = pressure[:, :128]
            ps[pl.ds(pair * 512 + 256, 256), :] = pressure[:, 128:]
        before, here = col(us, lo), col(us, lo + 1)
        flux_two, flux_one, height_one = None, None, None
        for c in range(lo + 1, hi - 1):
            after = col(us, c + 1)
            moved = here - rate * (here * (after - before) + (col(ps, c + 1) - col(ps, c - 1)))
            height = col(hs, c)
            flux = moved * height
            if c >= lo + 3:
                hs[pl.ds((c - 1) * LEVELS, LEVELS), :] = height_one - rate * (flux - flux_two)
            us[pl.ds(c * LEVELS, LEVELS), :] = moved
            before, here = here, after
            flux_two, flux_one, height_one = flux_one, flux, height
    out[pl.ds(0, span), :] = us[pl.ds(edge, span), :]
    out[pl.ds(span, span), :] = hs[pl.ds(edge, span), :]

    for q in range(GROUP):
        field = jnp.concatenate(
            [hs[pl.ds(edge + 2 * q + j, MINE, stride=LEVELS), :] for j in range(2)], axis=0
        )
        mean = jnp.mean(field, axis=1, keepdims=True)
        anomaly = field - mean
        weight = hist[pl.ds(cycle * 128, 64), q : q + 1]
        pull = hist[pl.ds(cycle * 128 + 64, 64), q : q + 1] - weight * mean
        vector = jnp.sum(anomaly * pull, axis=0, keepdims=True)
        flipped = split(anomaly.T)
        gram = dot_split(flipped, split(anomaly * weight))
        body, tail = fold(gram[:64], gram[64:], vector)
        fs[q, pl.ds(0, 64), :] = body
        fs[q, pl.ds(64, 8), :] = tail
    mine = core[0]
    for j in range(GROUP // 2):
        for which, ref in ((mine, keep), (1 - mine, send)):
            s = 2 * j + which
            ref[j] = fs[s] + fs[table[s, 0]] + fs[table[s, 1]]


def root_kernel(got, out):
    total = got[0]
    for j in range(1, 8):
        total = total + got[j]
    gram, vector = unfold(total[:64], total[64:])
    eye = jnp.where(iota((WIDTH, WIDTH), 0) == iota((WIDTH, WIDTH), 1), 1.0, 0.0)
    third = 1.0 / 3.0
    blended = (WIDTH - 1.0) * eye + gram * third
    pull = vector * third
    squared = jnp.sum(jnp.sum(blended * blended, axis=0, keepdims=True), axis=1, keepdims=True)
    norm = jnp.sqrt(squared)
    a = blended / norm
    newton = 1.5 * eye - 0.5 * a
    s = split(newton)
    a = dot_split(split(a), s)
    z = newton
    for step in range(1, ROOT_STEPS):
        newton = 1.5 * eye - 0.5 * dot_split(split(z), split(a))
        s = split(newton)
        if step < ROOT_STEPS - 1:
            a = dot_split(split(a), s)
        z = dot_split(s, split(z))
    halves = split(z)
    wide = jnp.broadcast_to(pull, (8, WIDTH))
    inner = dot_split(split(wide), halves, ((1,), (1,)))
    shift = dot_split(split(inner), halves, ((1,), (1,)))[0:1, :] / norm
    spread = z * (math.sqrt(WIDTH - 1.0) / jnp.sqrt(norm))
    body, tail = fold(spread[:64], spread[64:], shift)
    for j in range(8):
        out[j, pl.ds(0, 64), :] = body
        out[j, pl.ds(64, 8), :] = tail


def apply_kernel(last, core, state, same, other, *outs):
    mine = core[0]
    both = outs[-1]
    for j in range(GROUP // 2):
        both[2 * j + mine] = same[j]
        both[2 * j + 1 - mine] = other[j]
    span = MINE * LEVELS
    for s in range(GROUP):
        spread, shift = unfold(both[s, pl.ds(0, 64), :], both[s, pl.ds(64, 8), :])
        field = jnp.concatenate(
            [
                state[pl.ds(f * span + 2 * s + j, MINE, stride=LEVELS), :]
                for f in range(2)
                for j in range(2)
            ],
            axis=0,
        )
        mean = jnp.mean(field, axis=1, keepdims=True)
        anomaly = field - mean
        centre = mean + jnp.sum(anomaly * shift, axis=1, keepdims=True)
        result = centre + dot_split(split(anomaly), split(spread))
        if last:
            result = result.T
            for g in range(GROUP):
                outs[0][pl.ds((g * GROUP + s) * 8, 8), :] = result[g * 8 : g * 8 + 8, :]
        else:
            for f in range(2):
                for j in range(2):
                    at = (f * 2 + j) * 32
                    outs[0][pl.ds(f * span + 2 * s + j, MINE, stride=LEVELS), :] = result[at : at + 32, :]
    if not last:
        edge = HALO * LEVELS
        for f in range(2):
            outs[1][pl.ds(f * edge, edge), :] = outs[0][pl.ds(f * span, edge), :]
            outs[2][pl.ds(f * edge, edge), :] = outs[0][pl.ds((f + 1) * span - edge, edge), :]


def place_kernel(got, out, tiles):
    for n in range(8):
        for t in range(4):
            rows = [got[pl.ds(MEMBER_AT[4 * t + p] * 128 + n, 16, stride=8), :] for p in range(4)]
            for fj, block in enumerate(chunk_transpose(rows)):
                f, j = fj // 2, fj % 2
                tiles[pl.ds(512 * t + (n * 2 + f) * LEVELS + j, 16, stride=2), :] = block
    for t in range(4):
        out[:, pl.ds(128 * t, 128)] = tiles[pl.ds(512 * t, 512), :]


def vmem():
    return pl.BlockSpec(memory_space=pltpu.VMEM)


def smem():
    return pl.BlockSpec(memory_space=pltpu.SMEM)


def call(kernel, out, ins, name, scratch=()):
    return pl.pallas_call(
        kernel,
        out_shape=out,
        in_specs=ins,
        out_specs=jax.tree.map(lambda _: vmem(), out),
        scratch_shapes=scratch,
        compiler_params=pltpu.CompilerParams(vmem_limit_bytes=VMEM_LIMIT),
        name=name,
    )


def arr(*shape, dtype=F32):
    return jax.ShapeDtypeStruct(shape, dtype)


def across(x, forward):
    pairs = []
    for hor in range(16):
        for block in range(GROUP):
            here = MEMBER_AT[block]
            nxt = MEMBER_AT[(block + 1) % GROUP]
            nhor = (hor + (block + 1) // GROUP) % 16

            def flat(g, h):
                return ((g >> 2) * 16 + h) * 4 + (g & 3)

            pair = (flat(here, hor), flat(nxt, nhor))
            pairs.append(pair if forward else pair[::-1])
    return lax.ppermute(x, ALL, pairs)


def swap(x):
    return lax.ppermute(x, "core", [(0, 1), (1, 0)])


def exchange(x, axes):
    return lax.all_to_all(x, axes, split_axis=0, concat_axis=0, tiled=True)


def shards(ensemble, coupling, obs_column, obs_level, obs_value, obs_error, obs_live, partners):
    rows = MINE * LEVELS
    edges = 2 * HALO * LEVELS
    core = lax.axis_index("core").astype(jnp.int32).reshape(1)
    blocks = jnp.kron(jnp.eye(8, dtype=F32), coupling)
    blocks_high = lax.reduce_precision(blocks, 8, 7)
    mixing = jnp.concatenate([blocks_high, blocks - blocks_high], axis=0)
    packed = call(
        pack_kernel,
        arr(GROUP * 136, 128),
        [vmem()] * 6 + [smem()],
        "pack",
        [pltpu.VMEM((2048, 128), F32)],
    )(
        ensemble.reshape(512, 512),
        obs_column.reshape(2, COLS),
        obs_level.reshape(2, COLS),
        obs_value.reshape(2, COLS),
        obs_error.reshape(2, COLS),
        obs_live.reshape(2, COLS),
        partners.reshape(2),
    )
    got = exchange(packed.reshape(GROUP, 136, 128), TILE).reshape(GROUP * 136, 128)
    state, low, high, hist, table = call(
        unpack_kernel,
        (
            arr(2 * rows, WIDTH),
            arr(edges, WIDTH),
            arr(edges, WIDTH),
            arr(256, 128),
            arr(GROUP, 128, dtype=jnp.int32),
        ),
        [vmem()],
        "unpack",
    )(got)
    for cycle in range(2):
        from_low = across(high, True)
        from_high = across(low, False)
        state, keep, send = call(
            functools.partial(forecast_kernel, cycle),
            (arr(2 * rows, WIDTH), arr(8, FOLD, 128), arr(8, FOLD, 128)),
            [smem(), smem()] + [vmem()] * 5,
            "forecast",
            [
                pltpu.VMEM((WIDE * LEVELS, WIDTH), F32),
                pltpu.VMEM((WIDE * LEVELS, WIDTH), F32),
                pltpu.VMEM((WIDE * LEVELS, WIDTH), F32),
                pltpu.VMEM((GROUP, FOLD, 128), F32),
            ],
        )(table, core, state, from_low, from_high, hist, mixing)
        parts = exchange(keep + swap(send), CHIPS)
        copies = call(root_kernel, arr(8, FOLD, 128), [vmem()], "root")(parts)
        same = exchange(copies, CHIPS)
        other = swap(same)
        last = cycle == 1
        scratch = [pltpu.VMEM((GROUP, FOLD, 128), F32)]
        if last:
            outs = (arr(GROUP * 128, 128),)
        else:
            outs = (arr(2 * rows, WIDTH), arr(edges, WIDTH), arr(edges, WIDTH))
        result = call(
            functools.partial(apply_kernel, last), outs, [smem()] + [vmem()] * 3, "apply", scratch
        )(core, state, same, other)
        if not last:
            state, low, high = result
    got = exchange(result[0].reshape(GROUP, 128, 128), TILE).reshape(GROUP * 128, 128)
    placed = call(place_kernel, arr(512, 512), [vmem()], "place", [pltpu.VMEM((2048, 128), F32)])(got)
    return placed.reshape(ensemble.shape)


def solution(mesh):
    fine = Mesh(mesh.devices.reshape(4, 16, 2, 2), ALL)
    group = TILE
    in_specs = (
        P(group, None, None, "hor"),
        P(),
        P(None, group, "hor", None),
        P(None, group, "hor", None),
        P(None, group, "hor", None),
        P(None, group, "hor", None),
        P(None, group, "hor", None),
        P(group, "hor", None),
    )
    out_specs = P(group, None, None, "hor")
    return jax.shard_map(shards, mesh=fine, in_specs=in_specs, out_specs=out_specs, check_vma=False)
```

```python
import functools
import math

import jax
import jax.numpy as jnp
from jax import lax
from jax.experimental import pallas as pl
from jax.experimental.pallas import tpu as pltpu
from jax.sharding import Mesh, PartitionSpec as P

SUBSTEPS = 4
ROOT_STEPS = 8
TIME_STEP = 0.2
GROUP = 16
WIDTH = 128
LEVELS = 32
COLS = 512
MINE = COLS // GROUP
HALO = 2 * SUBSTEPS
WIDE = MINE + 2 * HALO
FOLD = 72
F32 = jnp.float32
BF16 = jnp.bfloat16
VMEM_LIMIT = 48 * 1024 * 1024
ALL = ("mem", "hor", "zh", "core")
TILE = ("mem", "zh", "core")
CHIPS = ("mem", "zh")


def block_of(g):
    return ((g >> 1) & 1) * 8 + (g >> 2) * 2 + (g & 1)


MEMBER_AT = {block_of(g): g for g in range(GROUP)}


def split(a):
    high = a.astype(BF16)
    return high, (a - high.astype(F32)).astype(BF16)


def dot_split(a, b, dims=((1,), (0,))):
    dims = (dims, ((), ()))
    dot = functools.partial(lax.dot_general, dimension_numbers=dims, preferred_element_type=F32)
    return dot(a[0], b[0]) + (dot(a[0], b[1]) + dot(a[1], b[0]))


def iota(shape, dim):
    return lax.broadcasted_iota(jnp.int32, shape, dim)


def chunk_transpose(rows):
    lane = iota(rows[0].shape, 1)
    out = []
    for p in range(4):
        total = None
        for q in range(4):
            piece = rows[q] if p == q else pltpu.roll(rows[q], (32 * (q - p)) % 128, 1)
            total = piece if total is None else jnp.where(lane >= 32 * q, piece, total)
        out.append(total)
    return out


def edges_kernel(left, right, first, last):
    first[...] = left[...].T[0:HALO, :]
    last[...] = right[...].T[128 - HALO :, :]


def observe_kernel(info, partner, column, level, value, error, live, coupling, out, mixing):
    member = jnp.bitwise_xor(iota((GROUP, COLS), 0), info[1])
    place = ((member >> 1) & 1) * 8 + (member >> 2) * 2 + (member & 1)
    spot = iota((64, COLS), 0)
    zero = jnp.zeros((64, COLS), F32)
    for cycle in range(2):
        col = column[cycle, 0]
        weight = live[cycle, 0].astype(F32) / error[cycle, 0]
        weighted = weight * value[cycle, 0]
        here = (col >> 5) == place
        left = jnp.concatenate([jnp.where(here, weight, 0.0), jnp.where(here, weighted, 0.0)], axis=1)
        hit = jnp.where(level[cycle, 0] * 32 + (col & 31) == spot, 1.0, 0.0)
        right = jnp.concatenate(
            [jnp.concatenate([hit, zero], axis=1), jnp.concatenate([zero, hit], axis=1)], axis=0
        )
        sums = lax.dot_general(
            left, right, (((1,), (1,)), ((), ())), precision=lax.Precision.HIGHEST, preferred_element_type=F32
        )
        out[pl.ds(cycle, GROUP, stride=8), :] = sums
    lane = iota((GROUP, 128), 1)
    first = partner[0, 0, 0].astype(F32)
    second = partner[0, 0, 1].astype(F32)
    out[pl.ds(2, GROUP, stride=8), :] = jnp.where(lane == 0, first, second)
    wide = jnp.concatenate([coupling[...]] * 8, axis=1)
    wide = jnp.concatenate([wide] * 8, axis=0)
    wide = jnp.where((iota((256, 256), 0) >> 5) == (iota((256, 256), 1) >> 5), wide, 0.0)
    high, rest = split(wide)
    mixing[pl.ds(0, 256), :] = high
    mixing[pl.ds(256, 256), :] = rest


def first_kernel(info, ens, before, after, sums, mixing, heights, speeds, us, hs, tiles):
    ring = COLS + 128
    middle = jnp.zeros((128 - 2 * HALO, COLS), F32)
    halo = jnp.concatenate([after[...], middle, before[...]], axis=0).T
    for m in range(8):
        for f, ref in enumerate((us, hs)):
            at = (m * 2 + f) * LEVELS
            ref[pl.ds(m * LEVELS, LEVELS), pl.ds(0, COLS)] = ens[pl.ds(at, LEVELS), :]
            ref[pl.ds(m * LEVELS, LEVELS), pl.ds(COLS, 128)] = halo[at : at + LEVELS, :]
    rate = 0.5 * TIME_STEP
    mix = (mixing[pl.ds(0, 256), :], mixing[pl.ds(256, 256), :])

    def slope(x):
        return pltpu.roll(x, ring - 1, 1) - pltpu.roll(x, 1, 1)

    for step in range(SUBSTEPS):
        pressure = dot_split(mix, split(hs[...]))
        for r in range(32):
            rows = pl.ds(8 * r, 8)
            u, h = us[rows, :], hs[rows, :]
            moved = u - rate * (u * slope(u) + slope(pressure[8 * r : 8 * r + 8, :]))
            height = h - rate * slope(moved * h)
            if step < SUBSTEPS - 1:
                us[rows, :] = moved
                hs[rows, :] = height
            else:
                for t in range(4):
                    for f, done in enumerate((moved, height)):
                        tiles[pl.ds((f * 4 + t) * 256 + 8 * r, 8), :] = done[:, 128 * t : 128 * t + 128]
    for f, (ref, size) in enumerate(((speeds, 64), (heights, 72))):
        for t in range(4):
            for m in range(8):
                at = (f * 4 + t) * 256 + m * LEVELS
                rows = [tiles[pl.ds(at + i, 8, stride=4), :] for i in range(4)]
                for p, block in enumerate(chunk_transpose(rows)):
                    g = jnp.bitwise_xor(MEMBER_AT[4 * t + p], info[1])
                    ref[pl.ds(g * size + m, 8, stride=8), :] = block
    for g in range(GROUP):
        heights[pl.ds(g * 72 + 64, 8), :] = sums[pl.ds(g * 8, 8), :]


def square_of(ref, at, size):
    return jnp.concatenate([ref[pl.ds(g * size + at * 8, 8), :] for g in range(GROUP)], axis=0)


def blend(fs, table, core, keep, send):
    mine = core
    for j in range(GROUP // 2):
        for which, ref in ((mine, keep), (1 - mine, send)):
            s = 2 * j + which
            ref[j] = fs[s] + fs[table[s, 0]] + fs[table[s, 1]]


def partial_gram(fs, q, flipped, anomaly, mean, weight, total):
    pull = total - weight * mean
    vector = jnp.sum(anomaly * pull, axis=0, keepdims=True)
    gram = dot_split(split(flipped), split(anomaly * weight))
    body, tail = fold(gram[:64], gram[64:], vector)
    fs[q, pl.ds(0, 64), :] = body
    fs[q, pl.ds(64, 8), :] = tail


def first_gram_kernel(info, got, keep, send, later, table_out, fs, table, sem):
    rows = got[pl.ds(66, GROUP, stride=72), :].astype(jnp.int32)
    table_out[...] = rows
    copy = pltpu.make_async_copy(table_out, table, sem)
    copy.start()
    hist = []
    for cycle in range(2):
        lines = got[pl.ds(64 + cycle, GROUP, stride=72), :]
        hist.append(jnp.concatenate([lines, jnp.zeros((128 - GROUP, 128), F32)], axis=0).T)
    later[...] = hist[1]
    for four in range(8):
        square = square_of(got, four, 72)
        square = square - jnp.mean(square, axis=0, keepdims=True)
        mean = jnp.mean(square_of(got, four, 72).T, axis=1, keepdims=True)
        turned = square.T
        for half in range(2):
            q = 2 * four + half
            at = slice(64 * half, 64 * half + 64)
            partial_gram(
                fs, q, square[:, at], turned[at, :], mean[at], hist[0][:64, q : q + 1], hist[0][64:, q : q + 1]
            )
    copy.wait()
    blend(fs, table, info[0], keep, send)


def fold(top, bottom, vector):
    row, lane = iota((64, 128), 0), iota((64, 128), 1)
    body = jnp.where((lane >= 64) | (row <= lane), top, pltpu.roll(bottom, 64, 1))
    diagonal = jnp.sum(jnp.where(lane == row + 64, bottom, 0.0), axis=0, keepdims=True)
    tail = jnp.where(iota((8, 128), 0) == 0, diagonal, vector)
    return body, tail


def unfold(body, tail):
    row, lane = iota((64, 128), 0), iota((64, 128), 1)
    top = jnp.where((lane >= 64) | (row < lane), body, jnp.where(row == lane, 0.5 * body, 0.0))
    moved = pltpu.roll(body, 64, 1)
    bottom = jnp.where(row > lane - 64, moved, jnp.where(row == lane - 64, 0.5 * tail[0:1, :], 0.0))
    bottom = jnp.where(lane >= 64, bottom, 0.0)
    half = jnp.concatenate([top, bottom], axis=0)
    return half + half.T, tail[1:2, :]


def forecast_kernel(table, info, state, low, high, hist, mixing, out, keep, send, us, hs, ps, fs):
    edge = HALO * LEVELS
    span = MINE * LEVELS
    for f, ref in enumerate((us, hs)):
        ref[pl.ds(0, edge), :] = low[pl.ds(f * edge, edge), :]
        ref[pl.ds(edge, span), :] = state[pl.ds(f * span, span), :]
        ref[pl.ds(edge + span, edge), :] = high[pl.ds(f * edge, edge), :]
    rate = 0.5 * TIME_STEP
    mix = (mixing[pl.ds(0, 256), :], mixing[pl.ds(256, 256), :])

    def col(ref, c):
        return ref[pl.ds(c * LEVELS, LEVELS), :]

    for step in range(SUBSTEPS):
        lo, hi = 2 * step, WIDE - 2 * step
        for pair in range(3):
            block = jnp.concatenate(
                [hs[pl.ds(pair * 512, 256), :], hs[pl.ds(pair * 512 + 256, 256), :]], axis=1
            )
            pressure = dot_split(mix, split(block))
            ps[pl.ds(pair * 512, 256), :] = pressure[:, :128]
            ps[pl.ds(pair * 512 + 256, 256), :] = pressure[:, 128:]
        before, here = col(us, lo), col(us, lo + 1)
        flux_two, flux_one, height_one = None, None, None
        for c in range(lo + 1, hi - 1):
            after = col(us, c + 1)
            moved = here - rate * (here * (after - before) + (col(ps, c + 1) - col(ps, c - 1)))
            height = col(hs, c)
            flux = moved * height
            if c >= lo + 3:
                hs[pl.ds((c - 1) * LEVELS, LEVELS), :] = height_one - rate * (flux - flux_two)
            us[pl.ds(c * LEVELS, LEVELS), :] = moved
            before, here = here, after
            flux_two, flux_one, height_one = flux_one, flux, height
    out[pl.ds(0, span), :] = us[pl.ds(edge, span), :]
    out[pl.ds(span, span), :] = hs[pl.ds(edge, span), :]

    for q in range(GROUP):
        field = jnp.concatenate(
            [hs[pl.ds(edge + 2 * q + j, MINE, stride=LEVELS), :] for j in range(2)], axis=0
        )
        mean = jnp.mean(field, axis=1, keepdims=True)
        anomaly = field - mean
        partial_gram(fs, q, anomaly.T, anomaly, mean, hist[pl.ds(0, 64), q : q + 1], hist[pl.ds(64, 64), q : q + 1])
    blend(fs, table, info[0], keep, send)


def root_kernel(got, out):
    total = got[0]
    for j in range(1, 8):
        total = total + got[j]
    gram, vector = unfold(total[:64], total[64:])
    eye = jnp.where(iota((WIDTH, WIDTH), 0) == iota((WIDTH, WIDTH), 1), 1.0, 0.0)
    third = 1.0 / 3.0
    blended = (WIDTH - 1.0) * eye + gram * third
    pull = vector * third
    squared = jnp.sum(jnp.sum(blended * blended, axis=0, keepdims=True), axis=1, keepdims=True)
    norm = jnp.sqrt(squared)
    a = blended / norm
    newton = 1.5 * eye - 0.5 * a
    s = split(newton)
    a = dot_split(split(a), s)
    z = newton
    for step in range(1, ROOT_STEPS):
        newton = 1.5 * eye - 0.5 * dot_split(split(z), split(a))
        s = split(newton)
        if step < ROOT_STEPS - 1:
            a = dot_split(split(a), s)
        z = dot_split(s, split(z))
    halves = split(z)
    wide = jnp.broadcast_to(pull, (8, WIDTH))
    inner = dot_split(split(wide), halves, ((1,), (1,)))
    shift = dot_split(split(inner), halves, ((1,), (1,)))[0:1, :] / norm
    spread = z * (math.sqrt(WIDTH - 1.0) / jnp.sqrt(norm))
    body, tail = fold(spread[:64], spread[64:], shift)
    for j in range(8):
        out[j, pl.ds(0, 64), :] = body
        out[j, pl.ds(64, 8), :] = tail


def gather_roots(info, same, other, both):
    for j in range(GROUP // 2):
        both[2 * j + info[0]] = same[j]
        both[2 * j + 1 - info[0]] = other[j]


def first_apply_kernel(info, heights, speeds, same, other, out, low, high, both):
    gather_roots(info, same, other, both)
    span = MINE * LEVELS
    edge = HALO * LEVELS
    for four in range(8):
        fields = (square_of(speeds, four, 64), square_of(heights, four, 72))
        for half in range(2):
            s = 2 * four + half
            spread, shift = unfold(both[s, pl.ds(0, 64), :], both[s, pl.ds(64, 8), :])
            field = jnp.concatenate([x[:, 64 * half : 64 * half + 64] for x in fields], axis=1)
            mean = jnp.mean(field, axis=0, keepdims=True)
            result = mean + dot_split(split(spread + shift), split(field - mean))
            result = result.T
            for f in range(2):
                for j in range(2):
                    at = (f * 2 + j) * 32
                    out[pl.ds(f * span + 2 * s + j, MINE, stride=LEVELS), :] = result[at : at + 32, :]
    for f in range(2):
        low[pl.ds(f * edge, edge), :] = out[pl.ds(f * span, edge), :]
        high[pl.ds(f * edge, edge), :] = out[pl.ds((f + 1) * span - edge, edge), :]


def last_apply_kernel(info, state, same, other, out, both):
    gather_roots(info, same, other, both)
    span = MINE * LEVELS
    for s in range(GROUP):
        spread, shift = unfold(both[s, pl.ds(0, 64), :], both[s, pl.ds(64, 8), :])
        field = jnp.concatenate(
            [
                state[pl.ds(f * span + 2 * s + j, MINE, stride=LEVELS), :]
                for f in range(2)
                for j in range(2)
            ],
            axis=0,
        ).T
        mean = jnp.mean(field, axis=0, keepdims=True)
        result = mean + dot_split(split(spread + shift), split(field - mean))
        for g in range(GROUP):
            out[pl.ds((g * GROUP + s) * 8, 8), :] = result[g * 8 : g * 8 + 8, :]


def place_kernel(info, got, out, tiles):
    for n in range(8):
        for t in range(4):
            members = [jnp.bitwise_xor(MEMBER_AT[4 * t + p], info[1]) for p in range(4)]
            rows = [got[pl.ds(g * 128 + n, 16, stride=8), :] for g in members]
            for fj, block in enumerate(chunk_transpose(rows)):
                f, j = fj // 2, fj % 2
                tiles[pl.ds(512 * t + (n * 2 + f) * LEVELS + j, 16, stride=2), :] = block
    for t in range(4):
        out[:, pl.ds(128 * t, 128)] = tiles[pl.ds(512 * t, 512), :]


def vmem():
    return pl.BlockSpec(memory_space=pltpu.VMEM)


def smem():
    return pl.BlockSpec(memory_space=pltpu.SMEM)


def call(kernel, out, ins, name, scratch=()):
    return pl.pallas_call(
        kernel,
        out_shape=out,
        in_specs=ins,
        out_specs=jax.tree.map(lambda _: vmem(), out),
        scratch_shapes=scratch,
        compiler_params=pltpu.CompilerParams(vmem_limit_bytes=VMEM_LIMIT),
        name=name,
    )


def arr(*shape, dtype=F32):
    return jax.ShapeDtypeStruct(shape, dtype)


def across(x, forward):
    pairs = []
    for hor in range(16):
        for block in range(GROUP):
            here = MEMBER_AT[block]
            nxt = MEMBER_AT[(block + 1) % GROUP]
            nhor = (hor + (block + 1) // GROUP) % 16

            def flat(g, h):
                return ((g >> 2) * 16 + h) * 4 + (g & 3)

            pair = (flat(here ^ (15 * (hor & 1)), hor), flat(nxt ^ (15 * (nhor & 1)), nhor))
            pairs.append(pair if forward else pair[::-1])
    return lax.ppermute(x, ALL, pairs)


def swap(x):
    return lax.ppermute(x, "core", [(0, 1), (1, 0)])


def exchange(x, axes):
    return lax.all_to_all(x, axes, split_axis=0, concat_axis=0, tiled=True)


def shards(ensemble, coupling, obs_column, obs_level, obs_value, obs_error, obs_live, partners):
    rows = MINE * LEVELS
    edges = 2 * HALO * LEVELS
    members = ensemble.reshape(512, COLS)
    info = jnp.stack([lax.axis_index("core"), 15 * (lax.axis_index("hor") & 1)]).astype(jnp.int32)
    first, last = pl.pallas_call(
        edges_kernel,
        grid=(1,),
        out_shape=(arr(HALO, COLS), arr(HALO, COLS)),
        in_specs=[pl.BlockSpec((512, 128), lambda i: (0, 0)), pl.BlockSpec((512, 128), lambda i: (0, 3))],
        out_specs=(pl.BlockSpec((HALO, COLS), lambda i: (0, 0)),) * 2,
        name="edges",
    )(members, members)
    ring = [(i, (i + 1) % 16) for i in range(16)]
    before = lax.ppermute(last, "hor", ring)
    after = lax.ppermute(first, "hor", [(b, a) for a, b in ring])
    sums, mixing = call(
        observe_kernel, (arr(128, 128), arr(512, 256, dtype=BF16)), [smem()] * 2 + [vmem()] * 6, "observe"
    )(info, partners, obs_column, obs_level, obs_value, obs_error, obs_live, coupling)
    heights, speeds = call(
        first_kernel,
        (arr(GROUP * 72, 128), arr(GROUP * 64, 128)),
        [smem()] + [vmem()] * 5,
        "first",
        [pltpu.VMEM((256, COLS + 128), F32), pltpu.VMEM((256, COLS + 128), F32), pltpu.VMEM((2048, 128), F32)],
    )(info, members, before, after, sums, mixing)
    heights = exchange(heights.reshape(GROUP, 72, 128), TILE)
    speeds, heights = lax.optimization_barrier((speeds, heights))
    heights = heights.reshape(GROUP * 72, 128)
    speeds = exchange(speeds.reshape(GROUP, 64, 128), TILE).reshape(GROUP * 64, 128)
    folded = pltpu.VMEM((GROUP, FOLD, 128), F32)
    keep, send, hist, table = call(
        first_gram_kernel,
        (arr(8, FOLD, 128), arr(8, FOLD, 128), arr(128, 128), arr(GROUP, 128, dtype=jnp.int32)),
        [smem(), vmem()],
        "gram",
        [folded, pltpu.SMEM((GROUP, 128), jnp.int32), pltpu.SemaphoreType.DMA(())],
    )(info, heights)

    def roots(keep, send):
        parts = exchange(keep + swap(send), CHIPS)
        copies = call(root_kernel, arr(8, FOLD, 128), [vmem()], "root")(parts)
        same = exchange(copies, CHIPS)
        return same, swap(same)

    same, other = roots(keep, send)
    state, low, high = call(
        first_apply_kernel,
        (arr(2 * rows, WIDTH), arr(edges, WIDTH), arr(edges, WIDTH)),
        [smem()] + [vmem()] * 4,
        "apply",
        [folded],
    )(info, heights, speeds, same, other)
    from_low = across(high, True)
    from_high = across(low, False)
    wide = pltpu.VMEM((WIDE * LEVELS, WIDTH), F32)
    state, keep, send = call(
        forecast_kernel,
        (arr(2 * rows, WIDTH), arr(8, FOLD, 128), arr(8, FOLD, 128)),
        [smem(), smem()] + [vmem()] * 5,
        "forecast",
        [wide, wide, wide, folded],
    )(table, info, state, from_low, from_high, hist, mixing)
    same, other = roots(keep, send)
    analysed = call(
        last_apply_kernel, arr(GROUP * 128, 128), [smem()] + [vmem()] * 3, "analyse", [folded]
    )(info, state, same, other)
    got = exchange(analysed.reshape(GROUP, 128, 128), TILE).reshape(GROUP * 128, 128)
    placed = call(place_kernel, arr(512, 512), [smem(), vmem()], "place", [pltpu.VMEM((2048, 128), F32)])(info, got)
    return placed.reshape(ensemble.shape)


def solution(mesh):
    fine = Mesh(mesh.devices.reshape(4, 16, 2, 2), ALL)
    group = TILE
    in_specs = (
        P(group, None, None, "hor"),
        P(),
        P(None, group, "hor", None),
        P(None, group, "hor", None),
        P(None, group, "hor", None),
        P(None, group, "hor", None),
        P(None, group, "hor", None),
        P(group, "hor", None),
    )
    out_specs = P(group, None, None, "hor")
    return jax.shard_map(shards, mesh=fine, in_specs=in_specs, out_specs=out_specs, check_vma=False)
```

```python
import functools
import math

import jax
import jax.numpy as jnp
from jax import lax
from jax.experimental import pallas as pl
from jax.experimental.pallas import tpu as pltpu
from jax.sharding import Mesh, PartitionSpec as P

SUBSTEPS = 4
ROOT_STEPS = 8
TIME_STEP = 0.2
GROUP = 16
WIDTH = 128
LEVELS = 32
COLS = 512
MINE = COLS // GROUP
HALO = 2 * SUBSTEPS
WIDE = MINE + 2 * HALO
FOLD = 72
F32 = jnp.float32
BF16 = jnp.bfloat16
VMEM_LIMIT = 48 * 1024 * 1024
ALL = ("mem", "hor", "zh", "core")
TILE = ("mem", "zh", "core")
CHIPS = ("mem", "zh")


def block_of(g):
    return ((g >> 1) & 1) * 8 + (g >> 2) * 2 + (g & 1)


MEMBER_AT = {block_of(g): g for g in range(GROUP)}


def split(a):
    high = a.astype(BF16)
    return high, (a - high.astype(F32)).astype(BF16)


def dot_split(a, b, turned=False):
    left = jnp.concatenate([a[0], a[0], a[1]], axis=1)
    right = jnp.concatenate([b[0], b[1], b[0]], axis=1 if turned else 0)
    dims = (((1,), (1 if turned else 0,)), ((), ()))
    return lax.dot_general(left, right, dims, preferred_element_type=F32)


def iota(shape, dim):
    return lax.broadcasted_iota(jnp.int32, shape, dim)


def chunk_transpose(rows):
    lane = iota(rows[0].shape, 1)
    out = []
    for p in range(4):
        total = None
        for q in range(4):
            piece = rows[q] if p == q else pltpu.roll(rows[q], (32 * (q - p)) % 128, 1)
            total = piece if total is None else jnp.where(lane >= 32 * q, piece, total)
        out.append(total)
    return out


def edges_kernel(left, right, first, last):
    first[...] = left[...].T[0:HALO, :]
    last[...] = right[...].T[128 - HALO :, :]


def prepare_kernel(
    info, partner, ens, column, level, value, error, live, coupling, state, out, mixing, tiles, blocks
):
    for t in range(4):
        tiles[pl.ds(512 * t, 512), :] = ens[:, pl.ds(128 * t, 128)]
    for f in range(2):
        for t in range(4):
            for m in range(8):
                at = t * 512 + (m * 2 + f) * LEVELS
                rows = [tiles[pl.ds(at + i, 8, stride=4), :] for i in range(4)]
                for p, block in enumerate(chunk_transpose(rows)):
                    blocks[pl.ds(f * 1024 + (4 * t + p) * 8 + m, 8, stride=128), :] = block
        for four in range(8):
            turned = blocks[pl.ds(f * 1024 + four * 128, 128), :].T
            for i in range(4):
                at = f * MINE * LEVELS + 4 * four + i
                state[pl.ds(at, MINE, stride=LEVELS), :] = turned[32 * i : 32 * i + 32, :]
    member = jnp.bitwise_xor(iota((GROUP, COLS), 0), info[1])
    place = ((member >> 1) & 1) * 8 + (member >> 2) * 2 + (member & 1)
    spot = iota((64, COLS), 0)
    zero = jnp.zeros((64, COLS), F32)
    for cycle in range(2):
        col = column[cycle, 0]
        weight = live[cycle, 0].astype(F32) / error[cycle, 0]
        weighted = weight * value[cycle, 0]
        here = (col >> 5) == place
        left = jnp.concatenate([jnp.where(here, weight, 0.0), jnp.where(here, weighted, 0.0)], axis=1)
        hit = jnp.where(level[cycle, 0] * 32 + (col & 31) == spot, 1.0, 0.0)
        right = jnp.concatenate(
            [jnp.concatenate([hit, zero], axis=1), jnp.concatenate([zero, hit], axis=1)], axis=0
        )
        sums = lax.dot_general(
            left, right, (((1,), (1,)), ((), ())), precision=lax.Precision.HIGHEST, preferred_element_type=F32
        )
        out[pl.ds(cycle, GROUP, stride=8), :] = sums
    lane = iota((GROUP, 128), 1)
    first = partner[0, 0, 0].astype(F32)
    second = partner[0, 0, 1].astype(F32)
    out[pl.ds(2, GROUP, stride=8), :] = jnp.where(lane == 0, first, second)
    wide = jnp.concatenate([coupling[...]] * 8, axis=1)
    wide = jnp.concatenate([wide] * 8, axis=0)
    wide = jnp.where((iota((256, 256), 0) >> 5) == (iota((256, 256), 1) >> 5), wide, 0.0)
    high, rest = split(wide)
    mixing[pl.ds(0, 256), :] = high
    mixing[pl.ds(256, 256), :] = rest


def substeps(us, hs, ps, mixing):
    rate = 0.5 * TIME_STEP
    mix = (mixing[pl.ds(0, 256), :], mixing[pl.ds(256, 256), :])

    def col(ref, c):
        return ref[pl.ds(c * LEVELS, LEVELS), :]

    for step in range(SUBSTEPS):
        lo, hi = 2 * step, WIDE - 2 * step
        for pair in range(3):
            block = jnp.concatenate(
                [hs[pl.ds(pair * 512, 256), :], hs[pl.ds(pair * 512 + 256, 256), :]], axis=1
            )
            pressure = dot_split(mix, split(block))
            ps[pl.ds(pair * 512, 256), :] = pressure[:, :128]
            ps[pl.ds(pair * 512 + 256, 256), :] = pressure[:, 128:]
        before, here = col(us, lo), col(us, lo + 1)
        flux_two, flux_one, height_one = None, None, None
        for c in range(lo + 1, hi - 1):
            after = col(us, c + 1)
            moved = here - rate * (here * (after - before) + (col(ps, c + 1) - col(ps, c - 1)))
            height = col(hs, c)
            flux = moved * height
            if c >= lo + 3:
                hs[pl.ds((c - 1) * LEVELS, LEVELS), :] = height_one - rate * (flux - flux_two)
            us[pl.ds(c * LEVELS, LEVELS), :] = moved
            before, here = here, after
            flux_two, flux_one, height_one = flux_one, flux, height


def four_levels(ref, at, four):
    rows = [ref[pl.ds(at + 4 * four + i, MINE, stride=LEVELS), :] for i in range(4)]
    return jnp.concatenate(rows, axis=0)


def first_kernel(info, state, before, after, sums, mixing, packed, us, hs, ps, spare):
    span = MINE * LEVELS
    edge = HALO * LEVELS
    pieces = []
    for ref in (before, after):
        for m in range(8):
            line = ref[:, pl.ds(128 * (m // 2), 128)]
            spare[pl.ds(8 * m, 8), :] = line if m % 2 == 0 else pltpu.roll(line, 64, 1)
        pieces += [spare[pl.ds(c, 8, stride=8), :] for c in range(8)]
    halo = jnp.concatenate(pieces, axis=0).T
    lane = iota((LEVELS, 128), 1)
    for f, ref in enumerate((us, hs)):
        ref[pl.ds(edge, span), :] = state[pl.ds(f * span, span), :]
        line = halo[f * LEVELS : (f + 1) * LEVELS, :]
        for c in range(HALO):
            inner = pltpu.roll(state[pl.ds(f * span + (MINE - HALO + c) * LEVELS, LEVELS), :], 8, 1)
            outer = pltpu.roll(line, (128 - 8 * c) % 128, 1)
            ref[pl.ds(c * LEVELS, LEVELS), :] = jnp.where(lane < 8, outer, inner)
            inner = pltpu.roll(state[pl.ds(f * span + c * LEVELS, LEVELS), :], 120, 1)
            outer = pltpu.roll(line, (56 - 8 * c) % 128, 1)
            ref[pl.ds(edge + span + c * LEVELS, LEVELS), :] = jnp.where(lane >= 120, outer, inner)
    substeps(us, hs, ps, mixing)
    starts = [jnp.bitwise_xor(MEMBER_AT[k], info[1]) * 136 for k in range(GROUP)]
    for base, ref in ((72, us), (0, hs)):
        for four in range(8):
            square = four_levels(ref, edge, four).T
            for k in range(GROUP):
                packed[pl.ds(starts[k] + (base + 8 * four), 8), :] = square[8 * k : 8 * k + 8, :]
    for g in range(GROUP):
        packed[pl.ds(g * 136 + 64, 8), :] = sums[pl.ds(g * 8, 8), :]


def square_of(ref, base, four):
    return jnp.concatenate([ref[pl.ds(g * 136 + base + four * 8, 8), :] for g in range(GROUP)], axis=0)


def blend(fs, table, core, keep, send):
    for j in range(GROUP // 2):
        for which, ref in ((core, keep), (1 - core, send)):
            s = 2 * j + which
            ref[j] = fs[s] + fs[table[s, 0]] + fs[table[s, 1]]


def gram_pair(fs, four, square, lines):
    mean = jnp.mean(square, axis=0, keepdims=True)
    anomaly = square - mean
    halves = split(anomaly)
    lane = iota((1, 128), 1)
    for half in range(2):
        q = 2 * four + half
        line = lines(q)
        swapped = pltpu.roll(line, 64, 1)
        mine = (lane >= 64) if half else (lane < 64)
        weight = jnp.where(mine, swapped if half else line, 0.0)
        pull = jnp.where(mine, line if half else swapped, 0.0) - weight * mean
        left = jnp.concatenate([anomaly * weight, jnp.broadcast_to(pull, (8, 128))], axis=0)
        gram = dot_split(split(left), halves, turned=True)
        body, tail = fold(gram[:64], gram[64:128], gram[128:129])
        fs[q, pl.ds(0, 64), :] = body
        fs[q, pl.ds(64, 8), :] = tail


def first_gram_kernel(info, got, keep, send, later, table_out, fs, table, sem):
    table_out[...] = got[pl.ds(66, GROUP, stride=136), :].astype(jnp.int32)
    copy = pltpu.make_async_copy(table_out, table, sem)
    copy.start()
    later[...] = got[pl.ds(65, GROUP, stride=136), :]
    for four in range(8):
        gram_pair(fs, four, square_of(got, 0, four), lambda q: got[pl.ds(q * 136 + 64, 1), :])
    copy.wait()
    blend(fs, table, info[0], keep, send)


def fold(top, bottom, vector):
    row, lane = iota((64, 128), 0), iota((64, 128), 1)
    body = jnp.where((lane >= 64) | (row <= lane), top, pltpu.roll(bottom, 64, 1))
    diagonal = jnp.sum(jnp.where(lane == row + 64, bottom, 0.0), axis=0, keepdims=True)
    tail = jnp.where(iota((8, 128), 0) == 0, diagonal, vector)
    return body, tail


def unfold(body, tail):
    row, lane = iota((64, 128), 0), iota((64, 128), 1)
    top = jnp.where((lane >= 64) | (row < lane), body, jnp.where(row == lane, 0.5 * body, 0.0))
    moved = pltpu.roll(body, 64, 1)
    bottom = jnp.where(row > lane - 64, moved, jnp.where(row == lane - 64, 0.5 * tail[0:1, :], 0.0))
    bottom = jnp.where(lane >= 64, bottom, 0.0)
    half = jnp.concatenate([top, bottom], axis=0)
    return half + half.T, tail[1:2, :]


def forecast_kernel(table, info, state, low, high, hist, mixing, out, keep, send, us, hs, ps, fs):
    edge = HALO * LEVELS
    span = MINE * LEVELS
    for f, ref in enumerate((us, hs)):
        ref[pl.ds(0, edge), :] = low[pl.ds(f * edge, edge), :]
        ref[pl.ds(edge, span), :] = state[pl.ds(f * span, span), :]
        ref[pl.ds(edge + span, edge), :] = high[pl.ds(f * edge, edge), :]
    substeps(us, hs, ps, mixing)
    out[pl.ds(0, span), :] = us[pl.ds(edge, span), :]
    out[pl.ds(span, span), :] = hs[pl.ds(edge, span), :]
    for four in range(8):
        gram_pair(fs, four, four_levels(hs, edge, four).T, lambda q: hist[pl.ds(q, 1), :])
    blend(fs, table, info[0], keep, send)


def root_kernel(got, out):
    total = got[0]
    for j in range(1, 8):
        total = total + got[j]
    gram, vector = unfold(total[:64], total[64:])
    eye = jnp.where(iota((WIDTH, WIDTH), 0) == iota((WIDTH, WIDTH), 1), 1.0, 0.0)
    third = 1.0 / 3.0
    blended = (WIDTH - 1.0) * eye + gram * third
    pull = vector * third
    squared = jnp.sum(jnp.sum(blended * blended, axis=0, keepdims=True), axis=1, keepdims=True)
    norm = jnp.sqrt(squared)
    a = blended / norm
    newton = 1.5 * eye - 0.5 * a
    a = dot_split(split(a), split(newton))
    z = newton
    for step in range(1, ROOT_STEPS):
        newton = 1.5 * eye - 0.5 * dot_split(split(z), split(a))
        if step < ROOT_STEPS - 1:
            both = dot_split(split(jnp.concatenate([a, z], axis=0)), split(newton))
            a, z = both[:WIDTH], both[WIDTH:]
        else:
            z = dot_split(split(z), split(newton))
    halves = split(z)
    wide = jnp.broadcast_to(pull, (8, WIDTH))
    inner = dot_split(split(wide), halves, turned=True)
    shift = dot_split(split(inner), halves, turned=True)[0:1, :] / norm
    spread = z * (math.sqrt(WIDTH - 1.0) / jnp.sqrt(norm))
    body, tail = fold(spread[:64], spread[64:], shift)
    for j in range(8):
        out[j, pl.ds(0, 64), :] = body
        out[j, pl.ds(64, 8), :] = tail


def gather_roots(info, same, other, both):
    for j in range(GROUP // 2):
        both[2 * j + info[0]] = same[j]
        both[2 * j + 1 - info[0]] = other[j]


def first_apply_kernel(info, got, same, other, out, low, high, both):
    gather_roots(info, same, other, both)
    span = MINE * LEVELS
    edge = HALO * LEVELS
    for four in range(8):
        fields = (square_of(got, 72, four), square_of(got, 0, four))
        for half in range(2):
            s = 2 * four + half
            spread, shift = unfold(both[s, pl.ds(0, 64), :], both[s, pl.ds(64, 8), :])
            field = jnp.concatenate([x[:, 64 * half : 64 * half + 64] for x in fields], axis=1)
            mean = jnp.mean(field, axis=0, keepdims=True)
            result = mean + dot_split(split(spread + shift), split(field - mean))
            result = result.T
            for f in range(2):
                for j in range(2):
                    at = (f * 2 + j) * 32
                    out[pl.ds(f * span + 2 * s + j, MINE, stride=LEVELS), :] = result[at : at + 32, :]
    for f in range(2):
        low[pl.ds(f * edge, edge), :] = out[pl.ds(f * span, edge), :]
        high[pl.ds(f * edge, edge), :] = out[pl.ds((f + 1) * span - edge, edge), :]


def last_apply_kernel(info, state, same, other, out, both):
    gather_roots(info, same, other, both)
    span = MINE * LEVELS
    for s in range(GROUP):
        spread, shift = unfold(both[s, pl.ds(0, 64), :], both[s, pl.ds(64, 8), :])
        field = jnp.concatenate(
            [
                state[pl.ds(f * span + 2 * s + j, MINE, stride=LEVELS), :]
                for f in range(2)
                for j in range(2)
            ],
            axis=0,
        ).T
        mean = jnp.mean(field, axis=0, keepdims=True)
        result = mean + dot_split(split(spread + shift), split(field - mean))
        for g in range(GROUP):
            out[pl.ds((g * GROUP + s) * 8, 8), :] = result[g * 8 : g * 8 + 8, :]


def place_kernel(info, got, out, tiles):
    starts = [jnp.bitwise_xor(MEMBER_AT[k], info[1]) * 128 for k in range(GROUP)]
    for t in range(4):
        for n in range(8):
            rows = [got[pl.ds(starts[4 * t + p] + n, 16, stride=8), :] for p in range(4)]
            for fj, block in enumerate(chunk_transpose(rows)):
                f, j = fj // 2, fj % 2
                tiles[pl.ds(512 * t + (n * 2 + f) * LEVELS + j, 16, stride=2), :] = block
    for t in range(4):
        out[:, pl.ds(128 * t, 128)] = tiles[pl.ds(512 * t, 512), :]


def vmem():
    return pl.BlockSpec(memory_space=pltpu.VMEM)


def smem():
    return pl.BlockSpec(memory_space=pltpu.SMEM)


def call(kernel, out, ins, name, scratch=()):
    return pl.pallas_call(
        kernel,
        out_shape=out,
        in_specs=ins,
        out_specs=jax.tree.map(lambda _: vmem(), out),
        scratch_shapes=scratch,
        compiler_params=pltpu.CompilerParams(vmem_limit_bytes=VMEM_LIMIT),
        name=name,
    )


def arr(*shape, dtype=F32):
    return jax.ShapeDtypeStruct(shape, dtype)


def across(x, forward):
    pairs = []
    for hor in range(16):
        for block in range(GROUP):
            here = MEMBER_AT[block]
            nxt = MEMBER_AT[(block + 1) % GROUP]
            nhor = (hor + (block + 1) // GROUP) % 16

            def flat(g, h):
                return ((g >> 2) * 16 + h) * 4 + (g & 3)

            pair = (flat(here ^ (15 * (hor & 1)), hor), flat(nxt ^ (15 * (nhor & 1)), nhor))
            pairs.append(pair if forward else pair[::-1])
    return lax.ppermute(x, ALL, pairs)


def swap(x):
    return lax.ppermute(x, "core", [(0, 1), (1, 0)])


def exchange(x, axes):
    return lax.all_to_all(x, axes, split_axis=0, concat_axis=0, tiled=True)


def shards(ensemble, coupling, obs_column, obs_level, obs_value, obs_error, obs_live, partners):
    rows = MINE * LEVELS
    edges = 2 * HALO * LEVELS
    members = ensemble.reshape(512, COLS)
    info = jnp.stack([lax.axis_index("core"), 15 * (lax.axis_index("hor") & 1)]).astype(jnp.int32)
    first, last = pl.pallas_call(
        edges_kernel,
        grid=(1,),
        out_shape=(arr(HALO, COLS), arr(HALO, COLS)),
        in_specs=[pl.BlockSpec((512, 128), lambda i: (0, 0)), pl.BlockSpec((512, 128), lambda i: (0, 3))],
        out_specs=(pl.BlockSpec((HALO, COLS), lambda i: (0, 0)),) * 2,
        name="edges",
    )(members, members)
    ring = [(i, (i + 1) % 16) for i in range(16)]
    before = lax.ppermute(last, "hor", ring)
    after = lax.ppermute(first, "hor", [(b, a) for a, b in ring])
    state, sums, mixing = call(
        prepare_kernel,
        (arr(2 * rows, 128), arr(128, 128), arr(512, 256, dtype=BF16)),
        [smem()] * 2 + [vmem()] * 7,
        "prepare",
        [pltpu.VMEM((2048, 128), F32), pltpu.VMEM((2048, 128), F32)],
    )(info, partners, members, obs_column, obs_level, obs_value, obs_error, obs_live, coupling)
    wide = pltpu.VMEM((WIDE * LEVELS, WIDTH), F32)
    packed = call(
        first_kernel,
        arr(GROUP * 136, 128),
        [smem()] + [vmem()] * 5,
        "first",
        [wide, wide, wide, pltpu.VMEM((64, 128), F32)],
    )(info, state, before, after, sums, mixing)
    received = exchange(packed.reshape(GROUP, 136, 128), TILE).reshape(GROUP * 136, 128)
    folded = pltpu.VMEM((GROUP, FOLD, 128), F32)
    keep, send, hist, table = call(
        first_gram_kernel,
        (arr(8, FOLD, 128), arr(8, FOLD, 128), arr(GROUP, 128), arr(GROUP, 128, dtype=jnp.int32)),
        [smem(), vmem()],
        "gram",
        [folded, pltpu.SMEM((GROUP, 128), jnp.int32), pltpu.SemaphoreType.DMA(())],
    )(info, received)

    def roots(keep, send):
        parts = exchange(keep + swap(send), CHIPS)
        copies = call(root_kernel, arr(8, FOLD, 128), [vmem()], "root")(parts)
        same = exchange(copies, CHIPS)
        return same, swap(same)

    same, other = roots(keep, send)
    state, low, high = call(
        first_apply_kernel,
        (arr(2 * rows, WIDTH), arr(edges, WIDTH), arr(edges, WIDTH)),
        [smem()] + [vmem()] * 3,
        "apply",
        [folded],
    )(info, received, same, other)
    from_low = across(high, True)
    from_high = across(low, False)
    state, keep, send = call(
        forecast_kernel,
        (arr(2 * rows, WIDTH), arr(8, FOLD, 128), arr(8, FOLD, 128)),
        [smem(), smem()] + [vmem()] * 5,
        "forecast",
        [wide, wide, wide, folded],
    )(table, info, state, from_low, from_high, hist, mixing)
    same, other = roots(keep, send)
    analysed = call(
        last_apply_kernel, arr(GROUP * 128, 128), [smem()] + [vmem()] * 3, "analyse", [folded]
    )(info, state, same, other)
    got = exchange(analysed.reshape(GROUP, 128, 128), TILE).reshape(GROUP * 128, 128)
    placed = call(place_kernel, arr(512, 512), [smem(), vmem()], "place", [pltpu.VMEM((2048, 128), F32)])(info, got)
    return placed.reshape(ensemble.shape)


def solution(mesh):
    fine = Mesh(mesh.devices.reshape(4, 16, 2, 2), ALL)
    group = TILE
    in_specs = (
        P(group, None, None, "hor"),
        P(),
        P(None, group, "hor", None),
        P(None, group, "hor", None),
        P(None, group, "hor", None),
        P(None, group, "hor", None),
        P(None, group, "hor", None),
        P(group, "hor", None),
    )
    out_specs = P(group, None, None, "hor")
    return jax.shard_map(shards, mesh=fine, in_specs=in_specs, out_specs=out_specs, check_vma=False)
```

```python
import functools
import math

import jax
import jax.numpy as jnp
from jax import lax
from jax.experimental import pallas as pl
from jax.experimental.pallas import tpu as pltpu
from jax.sharding import Mesh, PartitionSpec as P

SUBSTEPS = 4
ROOT_STEPS = 8
TIME_STEP = 0.2
GROUP = 16
WIDTH = 128
LEVELS = 32
COLS = 512
MINE = COLS // GROUP
HALO = 2 * SUBSTEPS
WIDE = MINE + 2 * HALO
FOLD = 72
F32 = jnp.float32
BF16 = jnp.bfloat16
VMEM_LIMIT = 48 * 1024 * 1024
ALL = ("mem", "hor", "zh", "core")
TILE = ("mem", "zh", "core")
CHIPS = ("mem", "zh")


def block_of(g):
    return ((g >> 1) & 1) * 8 + (g >> 2) * 2 + (g & 1)


MEMBER_AT = {block_of(g): g for g in range(GROUP)}


def split(a):
    high = a.astype(BF16)
    return high, (a - high.astype(F32)).astype(BF16)


def dot_split(a, b, turned=False):
    left = jnp.concatenate([a[0], a[0], a[1]], axis=1)
    right = jnp.concatenate([b[0], b[1], b[0]], axis=1 if turned else 0)
    dims = (((1,), (1 if turned else 0,)), ((), ()))
    return lax.dot_general(left, right, dims, preferred_element_type=F32)


def iota(shape, dim):
    return lax.broadcasted_iota(jnp.int32, shape, dim)


def chunk_transpose(rows):
    lane = iota(rows[0].shape, 1)
    out = []
    for p in range(4):
        total = None
        for q in range(4):
            piece = rows[q] if p == q else pltpu.roll(rows[q], (32 * (q - p)) % 128, 1)
            total = piece if total is None else jnp.where(lane >= 32 * q, piece, total)
        out.append(total)
    return out


def edges_kernel(left, right, first, last):
    first[...] = left[...].T[0:HALO, :]
    last[...] = right[...].T[128 - HALO :, :]


def prepare_kernel(
    info, partner, ens, column, level, value, error, live, coupling, state, out, mixing, tiles, blocks
):
    for t in range(4):
        tiles[pl.ds(512 * t, 512), :] = ens[:, pl.ds(128 * t, 128)]
    for f in range(2):
        for t in range(4):
            for m in range(8):
                at = t * 512 + (m * 2 + f) * LEVELS
                rows = [tiles[pl.ds(at + i, 8, stride=4), :] for i in range(4)]
                for p, block in enumerate(chunk_transpose(rows)):
                    blocks[pl.ds(f * 1024 + (4 * t + p) * 8 + m, 8, stride=128), :] = block
        for four in range(8):
            turned = blocks[pl.ds(f * 1024 + four * 128, 128), :].T
            for i in range(4):
                at = f * MINE * LEVELS + 4 * four + i
                state[pl.ds(at, MINE, stride=LEVELS), :] = turned[32 * i : 32 * i + 32, :]
    member = jnp.bitwise_xor(iota((GROUP, COLS), 0), info[1])
    place = ((member >> 1) & 1) * 8 + (member >> 2) * 2 + (member & 1)
    spot = iota((64, COLS), 0)
    zero = jnp.zeros((64, COLS), F32)
    for cycle in range(2):
        col = column[cycle, 0]
        weight = live[cycle, 0].astype(F32) / error[cycle, 0]
        weighted = weight * value[cycle, 0]
        here = (col >> 5) == place
        left = jnp.concatenate([jnp.where(here, weight, 0.0), jnp.where(here, weighted, 0.0)], axis=1)
        hit = jnp.where(level[cycle, 0] * 32 + (col & 31) == spot, 1.0, 0.0)
        right = jnp.concatenate(
            [jnp.concatenate([hit, zero], axis=1), jnp.concatenate([zero, hit], axis=1)], axis=0
        )
        sums = lax.dot_general(
            left, right, (((1,), (1,)), ((), ())), precision=lax.Precision.HIGHEST, preferred_element_type=F32
        )
        out[pl.ds(cycle, GROUP, stride=8), :] = sums
    lane = iota((GROUP, 128), 1)
    first = partner[0, 0, 0].astype(F32)
    second = partner[0, 0, 1].astype(F32)
    out[pl.ds(2, GROUP, stride=8), :] = jnp.where(lane == 0, first, second)
    wide = jnp.concatenate([coupling[...]] * 8, axis=1)
    wide = jnp.concatenate([wide] * 8, axis=0)
    wide = jnp.where((iota((256, 256), 0) >> 5) == (iota((256, 256), 1) >> 5), wide, 0.0)
    high, rest = split(wide)
    mixing[pl.ds(0, 256), :] = high
    mixing[pl.ds(256, 256), :] = rest


def substeps(sources, both, ps, mixing):
    rate = 0.5 * TIME_STEP
    mix = (mixing[pl.ds(0, 256), :], mixing[pl.ds(256, 256), :])
    wide = WIDE * LEVELS
    for c in (0, WIDE - 2):
        both[pl.ds(wide + c * LEVELS, 2 * LEVELS), :] = jnp.zeros((2 * LEVELS, WIDTH), F32)

    def rows(step, f, c, count):
        if step == 0:
            ref, at = sources(f, c)
            return ref[pl.ds(at, count * LEVELS), :]
        return both[pl.ds(f * wide + c * LEVELS, count * LEVELS), :]

    for step in range(SUBSTEPS):
        lo, hi = 2 * step, WIDE - 2 * step
        for pair in range(3):
            block = jnp.concatenate(
                [rows(step, 1, 16 * pair, 8), rows(step, 1, 16 * pair + 8, 8)], axis=1
            )
            pressure = dot_split(mix, split(block))
            ps[pl.ds(pair * 512, 256), :] = pressure[:, :128]
            ps[pl.ds(pair * 512 + 256, 256), :] = pressure[:, 128:]
        before, here = rows(step, 0, lo, 1), rows(step, 0, lo + 1, 1)
        slope_one, slope_two = ps[pl.ds(lo * LEVELS, LEVELS), :], ps[pl.ds((lo + 1) * LEVELS, LEVELS), :]
        flux_two, flux_one, height_one = None, None, None
        for c in range(lo + 1, hi - 1):
            after = rows(step, 0, c + 1, 1)
            slope = ps[pl.ds((c + 1) * LEVELS, LEVELS), :]
            moved = here - rate * (here * (after - before) + (slope - slope_one))
            height = rows(step, 1, c, 1)
            flux = moved * height
            if c >= lo + 3:
                both[pl.ds(wide + (c - 1) * LEVELS, LEVELS), :] = height_one - rate * (flux - flux_two)
            both[pl.ds(c * LEVELS, LEVELS), :] = moved
            before, here = here, after
            slope_one, slope_two = slope_two, slope
            flux_two, flux_one, height_one = flux_one, flux, height


def four_levels(ref, at, four):
    rows = [ref[pl.ds(at + 4 * four + i, MINE, stride=LEVELS), :] for i in range(4)]
    return jnp.concatenate(rows, axis=0)


def slab_rows(ref, at, s):
    rows = [
        ref[pl.ds(f * WIDE * LEVELS + at + 2 * s + j, MINE, stride=LEVELS), :] for f in range(2) for j in range(2)
    ]
    return jnp.concatenate(rows, axis=0)


def first_kernel(info, state, before, after, sums, mixing, packed, both, ps, sides, spare):
    span = MINE * LEVELS
    edge = HALO * LEVELS
    pieces = []
    for ref in (before, after):
        for m in range(8):
            line = ref[:, pl.ds(128 * (m // 2), 128)]
            spare[pl.ds(8 * m, 8), :] = line if m % 2 == 0 else pltpu.roll(line, 64, 1)
        pieces += [spare[pl.ds(c, 8, stride=8), :] for c in range(8)]
    halo = jnp.concatenate(pieces, axis=0).T
    lane = iota((LEVELS, 128), 1)
    for f in range(2):
        line = halo[f * LEVELS : (f + 1) * LEVELS, :]
        for c in range(HALO):
            inner = pltpu.roll(state[pl.ds(f * span + (MINE - HALO + c) * LEVELS, LEVELS), :], 8, 1)
            outer = pltpu.roll(line, (128 - 8 * c) % 128, 1)
            sides[pl.ds((2 * f) * edge + c * LEVELS, LEVELS), :] = jnp.where(lane < 8, outer, inner)
            inner = pltpu.roll(state[pl.ds(f * span + c * LEVELS, LEVELS), :], 120, 1)
            outer = pltpu.roll(line, (56 - 8 * c) % 128, 1)
            sides[pl.ds((2 * f + 1) * edge + c * LEVELS, LEVELS), :] = jnp.where(lane >= 120, outer, inner)

    def sources(f, c):
        if c < HALO:
            return sides, 2 * f * edge + c * LEVELS
        if c < HALO + MINE:
            return state, f * span + (c - HALO) * LEVELS
        return sides, (2 * f + 1) * edge + (c - HALO - MINE) * LEVELS

    substeps(sources, both, ps, mixing)
    starts = [jnp.bitwise_xor(MEMBER_AT[k], info[1]) * 136 for k in range(GROUP)]
    for s in range(GROUP):
        square = slab_rows(both, edge, s).T
        for k in range(GROUP):
            packed[pl.ds(starts[k] + 8 * s, 8), :] = square[8 * k : 8 * k + 8, :]
    for g in range(GROUP):
        packed[pl.ds(g * 136 + 128, 8), :] = sums[pl.ds(g * 8, 8), :]


def square_of(ref, s):
    return jnp.concatenate([ref[pl.ds(g * 136 + s * 8, 8), :] for g in range(GROUP)], axis=0)


def fold(top, bottom, vector, extra=0.0):
    row, lane = iota((64, 128), 0), iota((64, 128), 1)
    body = jnp.where((lane >= 64) | (row <= lane), top, pltpu.roll(bottom, 64, 1))
    diagonal = jnp.sum(jnp.where(lane == row + 64, bottom, 0.0), axis=0, keepdims=True)
    at = iota((8, 128), 0)
    tail = jnp.where(at == 0, diagonal, jnp.where(at == 1, vector, extra))
    return body, tail


def half_of(body, tail):
    row, lane = iota((64, 128), 0), iota((64, 128), 1)
    top = jnp.where((lane >= 64) | (row < lane), body, jnp.where(row == lane, 0.5 * body, 0.0))
    moved = pltpu.roll(body, 64, 1)
    bottom = jnp.where(row > lane - 64, moved, jnp.where(row == lane - 64, 0.5 * tail[0:1, :], 0.0))
    bottom = jnp.where(lane >= 64, bottom, 0.0)
    return jnp.concatenate([top, bottom], axis=0)


def blend(fs, table, core, keep, send):
    for j in range(GROUP // 2):
        for which, ref in ((core, keep), (1 - core, send)):
            s = 2 * j + which
            ref[j] = fs[s] + fs[table[s, 0]] + fs[table[s, 1]]


def gram_of(fs, q, anomaly, halves, mean, line, upper):
    lane = iota((1, 128), 1)
    swapped = pltpu.roll(line, 64, 1)
    mine = (lane >= 64) if upper else (lane < 64)
    weight = jnp.where(mine, swapped if upper else line, 0.0)
    pull = jnp.where(mine, line if upper else swapped, 0.0) - weight * mean
    left = jnp.concatenate([anomaly * weight, jnp.broadcast_to(pull, (8, 128))], axis=0)
    gram = dot_split(split(left), halves, turned=True)
    body, tail = fold(gram[:64], gram[64:128], gram[128:129])
    fs[q, pl.ds(0, 64), :] = body
    fs[q, pl.ds(64, 8), :] = tail


def centred(square):
    mean = jnp.mean(square, axis=0, keepdims=True)
    anomaly = square - mean
    return anomaly, split(anomaly), mean


def first_gram_kernel(info, got, keep, send, later, table_out, fs, table, sem):
    table_out[...] = got[pl.ds(130, GROUP, stride=136), :].astype(jnp.int32)
    copy = pltpu.make_async_copy(table_out, table, sem)
    copy.start()
    later[...] = got[pl.ds(129, GROUP, stride=136), :]
    for q in range(GROUP):
        gram_of(fs, q, *centred(square_of(got, q)), got[pl.ds(q * 136 + 128, 1), :], True)
    copy.wait()
    blend(fs, table, info[0], keep, send)


def forecast_kernel(table, info, state, low, high, hist, mixing, both, keep, send, ps, fs):
    edge = HALO * LEVELS
    span = MINE * LEVELS

    def sources(f, c):
        if c < HALO:
            return low, f * edge + c * LEVELS
        if c < HALO + MINE:
            return state, f * span + (c - HALO) * LEVELS
        return high, f * edge + (c - HALO - MINE) * LEVELS

    substeps(sources, both, ps, mixing)
    for four in range(8):
        parts = centred(four_levels(both, WIDE * LEVELS + edge, four).T)
        for half in range(2):
            q = 2 * four + half
            gram_of(fs, q, *parts, hist[pl.ds(q, 1), :], half == 1)
    blend(fs, table, info[0], keep, send)


def root_kernel(got, out):
    total = got[0]
    for j in range(1, 8):
        total = total + got[j]
    half = half_of(total[:64], total[64:])
    gram, vector = half + half.T, total[65:66]
    eye = jnp.where(iota((WIDTH, WIDTH), 0) == iota((WIDTH, WIDTH), 1), 1.0, 0.0)
    third = 1.0 / 3.0
    blended = (WIDTH - 1.0) * eye + gram * third
    pull = vector * third
    squared = jnp.sum(jnp.sum(blended * blended, axis=0, keepdims=True), axis=1, keepdims=True)
    norm = jnp.sqrt(squared)
    a = blended / norm
    newton = 1.5 * eye - 0.5 * a
    a = dot_split(split(a), split(newton))
    z = newton
    for step in range(1, ROOT_STEPS):
        newton = 1.5 * eye - 0.5 * dot_split(split(z), split(a))
        if step < ROOT_STEPS - 1:
            both = dot_split(split(jnp.concatenate([a, z], axis=0)), split(newton))
            a, z = both[:WIDTH], both[WIDTH:]
        else:
            z = dot_split(split(z), split(newton))
    halves = split(z)
    wide = jnp.broadcast_to(pull, (8, WIDTH))
    inner = dot_split(split(wide), halves, turned=True)
    shift = dot_split(split(inner), halves, turned=True)[0:1, :] / norm
    spread = z * (math.sqrt(WIDTH - 1.0) / jnp.sqrt(norm))
    sums = jnp.sum(spread, axis=0, keepdims=True) + jnp.sum(shift, axis=1, keepdims=True)
    body, tail = fold(spread[:64], spread[64:], shift, (1.0 - sums) * (1.0 / WIDTH))
    for j in range(8):
        out[j, pl.ds(0, 64), :] = body
        out[j, pl.ds(64, 8), :] = tail


def weights_of(roots, j):
    body, tail = roots[j, pl.ds(0, 64), :], roots[j, pl.ds(64, 8), :]
    half = half_of(body, tail)
    return split((half + tail[1:2, :]) + (half + tail[2:3, :]).T)


def first_apply_kernel(second, info, got, roots, *refs):
    out = refs[1] if second else refs[0]
    span = MINE * LEVELS
    edge = HALO * LEVELS
    parity = 1 - info[0] if second else info[0]
    for j in range(8):
        s = 2 * j + parity
        square = jnp.concatenate(
            [got[pl.ds(pl.multiple_of(g * 136 + s * 8, 8), 8), :] for g in range(GROUP)], axis=0
        )
        result = dot_split(weights_of(roots, j), split(square)).T
        for fj in range(4):
            at = (fj // 2) * span + 2 * s + fj % 2
            out[pl.ds(at, MINE, stride=LEVELS), :] = result[fj * 32 : fj * 32 + 32, :]
    if second:
        low, high = refs[2:]
        for f in range(2):
            low[pl.ds(f * edge, edge), :] = out[pl.ds(f * span, edge), :]
            high[pl.ds(f * edge, edge), :] = out[pl.ds((f + 1) * span - edge, edge), :]


def last_apply_kernel(second, info, both, roots, *refs):
    out = refs[-1]
    parity = 1 - info[0] if second else info[0]
    starts = []
    for chunk in range(4):
        fj = (chunk + 4 - info[2]) & 3
        starts.append((fj >> 1) * (WIDE * LEVELS) + (fj & 1) + HALO * LEVELS)
    for j in range(8):
        s = 2 * j + parity
        field = jnp.concatenate(
            [both[pl.ds(at + 2 * s, MINE, stride=LEVELS), :] for at in starts], axis=0
        )
        result = dot_split(weights_of(roots, j), split(field), turned=True)
        for g in range(GROUP):
            out[pl.ds(pl.multiple_of((g * GROUP + s) * 8, 8), 8), :] = result[g * 8 : g * 8 + 8, :]


def place_kernel(info, got, out, tiles):
    starts = [jnp.bitwise_xor(MEMBER_AT[k], info[1]) * 128 for k in range(GROUP)]
    lane = iota((16, 128), 1)
    for t in range(4):
        for n in range(8):
            rows = [got[pl.ds(starts[4 * t + p] + n, 16, stride=8), :] for p in range(4)]
            for fj in range(4):
                block = rows[(0 - fj) % 4]
                for chunk in range(1, 4):
                    block = jnp.where(lane >= 32 * chunk, rows[(chunk - fj) % 4], block)
                if fj > 0:
                    block = pltpu.roll(block, 128 - 32 * fj, 1)
                tiles[pl.ds(512 * t + (n * 2 + fj // 2) * LEVELS + fj % 2, 16, stride=2), :] = block
    for t in range(4):
        out[:, pl.ds(128 * t, 128)] = tiles[pl.ds(512 * t, 512), :]


def vmem():
    return pl.BlockSpec(memory_space=pltpu.VMEM)


def smem():
    return pl.BlockSpec(memory_space=pltpu.SMEM)


def call(kernel, out, ins, name, scratch=(), aliases=None, cost=None):
    return pl.pallas_call(
        kernel,
        out_shape=out,
        in_specs=ins,
        out_specs=jax.tree.map(lambda _: vmem(), out),
        scratch_shapes=scratch,
        input_output_aliases=aliases or {},
        cost_estimate=cost,
        compiler_params=pltpu.CompilerParams(vmem_limit_bytes=VMEM_LIMIT),
        name=name,
    )


def arr(*shape, dtype=F32):
    return jax.ShapeDtypeStruct(shape, dtype)


def across(x, forward):
    pairs = []
    for hor in range(16):
        for block in range(GROUP):
            here = MEMBER_AT[block]
            nxt = MEMBER_AT[(block + 1) % GROUP]
            nhor = (hor + (block + 1) // GROUP) % 16

            def flat(g, h):
                return ((g >> 2) * 16 + h) * 4 + (g & 3)

            pair = (flat(here ^ (15 * (hor & 1)), hor), flat(nxt ^ (15 * (nhor & 1)), nhor))
            pairs.append(pair if forward else pair[::-1])
    return lax.ppermute(x, ALL, pairs)


def swap(x):
    return lax.ppermute(x, "core", [(0, 1), (1, 0)])


def exchange(x, axes):
    return lax.all_to_all(x, axes, split_axis=0, concat_axis=0, tiled=True)


def shards(ensemble, coupling, obs_column, obs_level, obs_value, obs_error, obs_live, partners):
    rows = MINE * LEVELS
    edges = 2 * HALO * LEVELS
    members = ensemble.reshape(512, COLS)
    flip = 15 * (lax.axis_index("hor") & 1)
    block = block_of(lax.axis_index(TILE) ^ flip)
    info = jnp.stack([lax.axis_index("core"), flip, block & 3]).astype(jnp.int32)
    first, last = pl.pallas_call(
        edges_kernel,
        grid=(1,),
        out_shape=(arr(HALO, COLS), arr(HALO, COLS)),
        in_specs=[pl.BlockSpec((512, 128), lambda i: (0, 0)), pl.BlockSpec((512, 128), lambda i: (0, 3))],
        out_specs=(pl.BlockSpec((HALO, COLS), lambda i: (0, 0)),) * 2,
        name="edges",
    )(members, members)
    ring = [(i, (i + 1) % 16) for i in range(16)]
    before = lax.ppermute(last, "hor", ring)
    after = lax.ppermute(first, "hor", [(b, a) for a, b in ring])
    state, sums, mixing = call(
        prepare_kernel,
        (arr(2 * rows, 128), arr(128, 128), arr(512, 256, dtype=BF16)),
        [smem()] * 2 + [vmem()] * 7,
        "prepare",
        [pltpu.VMEM((2048, 128), F32), pltpu.VMEM((2048, 128), F32)],
    )(info, partners, members, obs_column, obs_level, obs_value, obs_error, obs_live, coupling)
    wide = pltpu.VMEM((WIDE * LEVELS, WIDTH), F32)
    fields = pltpu.VMEM((2 * WIDE * LEVELS, WIDTH), F32)
    packed = call(
        first_kernel,
        arr(GROUP * 136, 128),
        [smem()] + [vmem()] * 5,
        "first",
        [fields, wide, pltpu.VMEM((4 * HALO * LEVELS, 128), F32), pltpu.VMEM((64, 128), F32)],
    )(info, state, before, after, sums, mixing)
    received = exchange(packed.reshape(GROUP, 136, 128), TILE).reshape(GROUP * 136, 128)
    folded = pltpu.VMEM((GROUP, FOLD, 128), F32)
    keep, send, hist, table = call(
        first_gram_kernel,
        (arr(8, FOLD, 128), arr(8, FOLD, 128), arr(GROUP, 128), arr(GROUP, 128, dtype=jnp.int32)),
        [smem(), vmem()],
        "gram",
        [folded, pltpu.SMEM((GROUP, 128), jnp.int32), pltpu.SemaphoreType.DMA(())],
    )(info, received)

    def roots(keep, send):
        parts = exchange(keep + swap(send), CHIPS)
        copies = call(root_kernel, arr(8, FOLD, 128), [vmem()], "root")(parts)
        same = exchange(copies, CHIPS)
        return same, swap(same)

    cost = pl.CostEstimate(flops=10**9, bytes_accessed=3 * 2**20, transcendentals=0)
    same, other = roots(keep, send)
    part = call(
        functools.partial(first_apply_kernel, False),
        arr(2 * rows, WIDTH),
        [smem()] + [vmem()] * 2,
        "apply",
        cost=cost,
    )(info, received, same)
    state, low, high = call(
        functools.partial(first_apply_kernel, True),
        (arr(2 * rows, WIDTH), arr(edges, WIDTH), arr(edges, WIDTH)),
        [smem()] + [vmem()] * 3,
        "apply",
        aliases={3: 0},
    )(info, received, other, part)
    from_low = across(high, True)
    from_high = across(low, False)
    both, keep, send = call(
        forecast_kernel,
        (arr(2 * WIDE * LEVELS, WIDTH), arr(8, FOLD, 128), arr(8, FOLD, 128)),
        [smem(), smem()] + [vmem()] * 5,
        "forecast",
        [wide, folded],
    )(table, info, state, from_low, from_high, hist, mixing)
    same, other = roots(keep, send)
    part = call(
        functools.partial(last_apply_kernel, False),
        arr(GROUP * 128, 128),
        [smem()] + [vmem()] * 2,
        "analyse",
        cost=cost,
    )(info, both, same)
    analysed = call(
        functools.partial(last_apply_kernel, True),
        arr(GROUP * 128, 128),
        [smem()] + [vmem()] * 3,
        "analyse",
        aliases={3: 0},
    )(info, both, other, part)
    got = exchange(analysed.reshape(GROUP, 128, 128), TILE).reshape(GROUP * 128, 128)
    placed = call(place_kernel, arr(512, 512), [smem(), vmem()], "place", [pltpu.VMEM((2048, 128), F32)])(info, got)
    return placed.reshape(ensemble.shape)


def solution(mesh):
    fine = Mesh(mesh.devices.reshape(4, 16, 2, 2), ALL)
    group = TILE
    in_specs = (
        P(group, None, None, "hor"),
        P(),
        P(None, group, "hor", None),
        P(None, group, "hor", None),
        P(None, group, "hor", None),
        P(None, group, "hor", None),
        P(None, group, "hor", None),
        P(group, "hor", None),
    )
    out_specs = P(group, None, None, "hor")
    return jax.shard_map(shards, mesh=fine, in_specs=in_specs, out_specs=out_specs, check_vma=False)
```

```python
import functools
import math

import jax
import jax.numpy as jnp
from jax import lax
from jax.experimental import pallas as pl
from jax.experimental.pallas import tpu as pltpu
from jax.sharding import Mesh, PartitionSpec as P

SUBSTEPS = 4
ROOT_STEPS = 8
RATE = 0.5 * 0.2
MIX = 128
GROUP = 16
WIDTH = 128
LEVELS = 32
COLS = 512
MINE = COLS // GROUP
HALO = 2 * SUBSTEPS
WIDE = MINE + 2 * HALO
FOLD = 72
F32 = jnp.float32
BF16 = jnp.bfloat16
VMEM_LIMIT = 48 * 1024 * 1024
ALL = ("mem", "hor", "zh", "core")
TILE = ("mem", "zh", "core")
CHIPS = ("mem", "zh")


def block_of(g):
    return ((g >> 1) & 1) * 8 + (g >> 2) * 2 + (g & 1)


MEMBER_AT = {block_of(g): g for g in range(GROUP)}


def split(a):
    high = a.astype(BF16)
    return high, (a - high.astype(F32)).astype(BF16)


def dot_split(a, b, turned=False):
    left = jnp.concatenate([a[0], a[0], a[1]], axis=1)
    right = jnp.concatenate([b[0], b[1], b[0]], axis=1 if turned else 0)
    dims = (((1,), (1 if turned else 0,)), ((), ()))
    return lax.dot_general(left, right, dims, preferred_element_type=F32)


def iota(shape, dim):
    return lax.broadcasted_iota(jnp.int32, shape, dim)


def chunk_transpose(rows):
    lane = iota(rows[0].shape, 1)
    out = []
    for p in range(4):
        total = None
        for q in range(4):
            piece = rows[q] if p == q else pltpu.roll(rows[q], (32 * (q - p)) % 128, 1)
            total = piece if total is None else jnp.where(lane >= 32 * q, piece, total)
        out.append(total)
    return out


def edges_kernel(ens, first, last):
    first[...] = ens[:, 0:128].T[0:HALO, :]
    last[...] = ens[:, COLS - 128 : COLS].T[128 - HALO :, :]


def prepare_kernel(
    info, partner, ens, column, level, value, error, live, coupling, state, out, mixing, tiles, blocks
):
    for t in range(4):
        tiles[pl.ds(512 * t, 512), :] = ens[:, pl.ds(128 * t, 128)]
    for f in range(2):
        for t in range(4):
            for m in range(8):
                at = t * 512 + (m * 2 + f) * LEVELS
                rows = [tiles[pl.ds(at + i, 8, stride=4), :] for i in range(4)]
                for p, block in enumerate(chunk_transpose(rows)):
                    blocks[pl.ds(f * 1024 + (4 * t + p) * 8 + m, 8, stride=128), :] = block
        for four in range(8):
            turned = blocks[pl.ds(f * 1024 + four * 128, 128), :].T
            for i in range(4):
                at = f * MINE * LEVELS + 4 * four + i
                state[pl.ds(at, MINE, stride=LEVELS), :] = turned[32 * i : 32 * i + 32, :]
    member = jnp.bitwise_xor(iota((GROUP, COLS), 0), info[1])
    place = ((member >> 1) & 1) * 8 + (member >> 2) * 2 + (member & 1)
    spot = iota((64, COLS), 0)
    zero = jnp.zeros((64, COLS), F32)
    for cycle in range(2):
        col = column[cycle, 0]
        weight = live[cycle, 0].astype(F32) / error[cycle, 0]
        weighted = weight * value[cycle, 0]
        here = (col >> 5) == place
        left = jnp.concatenate([jnp.where(here, weight, 0.0), jnp.where(here, weighted, 0.0)], axis=1)
        hit = jnp.where(level[cycle, 0] * 32 + (col & 31) == spot, 1.0, 0.0)
        right = jnp.concatenate(
            [jnp.concatenate([hit, zero], axis=1), jnp.concatenate([zero, hit], axis=1)], axis=0
        )
        sums = lax.dot_general(
            left, right, (((1,), (1,)), ((), ())), precision=lax.Precision.HIGHEST, preferred_element_type=F32
        )
        out[pl.ds(cycle, GROUP, stride=8), :] = sums
    lane = iota((GROUP, 128), 1)
    first = partner[0, 0, 0].astype(F32)
    second = partner[0, 0, 1].astype(F32)
    out[pl.ds(2, GROUP, stride=8), :] = jnp.where(lane == 0, first, second)
    wide = jnp.concatenate([coupling[...]] * (MIX // LEVELS), axis=1)
    wide = jnp.concatenate([wide] * (MIX // LEVELS), axis=0)
    wide = jnp.where((iota((MIX, MIX), 0) >> 5) == (iota((MIX, MIX), 1) >> 5), RATE * RATE * wide, 0.0)
    high, rest = split(wide)
    mixing[pl.ds(0, MIX), :] = high
    mixing[pl.ds(MIX, MIX), :] = rest


def substeps(sources, both, ps, mixing):
    mix = (mixing[pl.ds(0, MIX), :], mixing[pl.ds(MIX, MIX), :])
    wide = WIDE * LEVELS
    for c in (0, WIDE - 2):
        both[pl.ds(wide + c * LEVELS, 2 * LEVELS), :] = jnp.zeros((2 * LEVELS, WIDTH), F32)

    def rows(step, f, c, count):
        if step == 0:
            ref, at = sources(f, c)
            return ref[pl.ds(at, count * LEVELS), :]
        return both[pl.ds(f * wide + c * LEVELS, count * LEVELS), :]

    def speed(step, c):
        return RATE * rows(0, 0, c, 1) if step == 0 else rows(step, 0, c, 1)

    many = MIX // LEVELS
    for step in range(SUBSTEPS):
        lo, hi = 2 * step, WIDE - 2 * step
        for c in range(0, WIDE, 2 * many):
            block = jnp.concatenate([rows(step, 1, c, many), rows(step, 1, c + many, many)], axis=1)
            pressure = dot_split(mix, split(block))
            ps[pl.ds(c * LEVELS, MIX), :] = pressure[:, :128]
            ps[pl.ds(c * LEVELS + MIX, MIX), :] = pressure[:, 128:]
        before, here = speed(step, lo), speed(step, lo + 1)
        slope_one, slope_two = ps[pl.ds(lo * LEVELS, LEVELS), :], ps[pl.ds((lo + 1) * LEVELS, LEVELS), :]
        flux_two, flux_one, height_one = None, None, None
        for c in range(lo + 1, hi - 1):
            after = speed(step, c + 1)
            slope = ps[pl.ds((c + 1) * LEVELS, LEVELS), :]
            moved = (here - here * (after - before)) - (slope - slope_one)
            height = rows(step, 1, c, 1)
            flux = moved * height
            if c >= lo + 3:
                both[pl.ds(wide + (c - 1) * LEVELS, LEVELS), :] = height_one - (flux - flux_two)
            both[pl.ds(c * LEVELS, LEVELS), :] = moved if step < SUBSTEPS - 1 else moved * (1.0 / RATE)
            before, here = here, after
            slope_one, slope_two = slope_two, slope
            flux_two, flux_one, height_one = flux_one, flux, height


def four_levels(ref, at, four):
    rows = [ref[pl.ds(at + 4 * four + i, MINE, stride=LEVELS), :] for i in range(4)]
    return jnp.concatenate(rows, axis=0)


def slab_rows(ref, at, s):
    rows = [
        ref[pl.ds(f * WIDE * LEVELS + at + 2 * s + j, MINE, stride=LEVELS), :] for f in range(2) for j in range(2)
    ]
    return jnp.concatenate(rows, axis=0)


def first_kernel(info, state, before, after, sums, mixing, packed, both, ps, sides, spare):
    span = MINE * LEVELS
    edge = HALO * LEVELS
    pieces = []
    for ref in (before, after):
        for m in range(8):
            line = ref[:, pl.ds(128 * (m // 2), 128)]
            spare[pl.ds(8 * m, 8), :] = line if m % 2 == 0 else pltpu.roll(line, 64, 1)
        pieces += [spare[pl.ds(c, 8, stride=8), :] for c in range(8)]
    halo = jnp.concatenate(pieces, axis=0).T
    lane = iota((LEVELS, 128), 1)
    for f in range(2):
        line = halo[f * LEVELS : (f + 1) * LEVELS, :]
        for c in range(HALO):
            inner = pltpu.roll(state[pl.ds(f * span + (MINE - HALO + c) * LEVELS, LEVELS), :], 8, 1)
            outer = pltpu.roll(line, (128 - 8 * c) % 128, 1)
            sides[pl.ds((2 * f) * edge + c * LEVELS, LEVELS), :] = jnp.where(lane < 8, outer, inner)
            inner = pltpu.roll(state[pl.ds(f * span + c * LEVELS, LEVELS), :], 120, 1)
            outer = pltpu.roll(line, (56 - 8 * c) % 128, 1)
            sides[pl.ds((2 * f + 1) * edge + c * LEVELS, LEVELS), :] = jnp.where(lane >= 120, outer, inner)

    def sources(f, c):
        if c < HALO:
            return sides, 2 * f * edge + c * LEVELS
        if c < HALO + MINE:
            return state, f * span + (c - HALO) * LEVELS
        return sides, (2 * f + 1) * edge + (c - HALO - MINE) * LEVELS

    substeps(sources, both, ps, mixing)
    starts = [jnp.bitwise_xor(MEMBER_AT[k], info[1]) * 136 for k in range(GROUP)]
    for s in range(GROUP):
        square = slab_rows(both, edge, s).T
        for k in range(GROUP):
            packed[pl.ds(starts[k] + 8 * s, 8), :] = square[8 * k : 8 * k + 8, :]
    for g in range(GROUP):
        packed[pl.ds(g * 136 + 128, 8), :] = sums[pl.ds(g * 8, 8), :]


def square_of(ref, s):
    return jnp.concatenate([ref[pl.ds(g * 136 + s * 8, 8), :] for g in range(GROUP)], axis=0)


def fold(top, bottom, vector, extra=0.0):
    row, lane = iota((64, 128), 0), iota((64, 128), 1)
    body = jnp.where((lane >= 64) | (row <= lane), top, pltpu.roll(bottom, 64, 1))
    diagonal = jnp.sum(jnp.where(lane == row + 64, bottom, 0.0), axis=0, keepdims=True)
    at = iota((8, 128), 0)
    tail = jnp.where(at == 0, diagonal, jnp.where(at == 1, vector, extra))
    return body, tail


def half_of(body, tail):
    row, lane = iota((64, 128), 0), iota((64, 128), 1)
    top = jnp.where((lane >= 64) | (row < lane), body, jnp.where(row == lane, 0.5 * body, 0.0))
    moved = pltpu.roll(body, 64, 1)
    bottom = jnp.where(row > lane - 64, moved, jnp.where(row == lane - 64, 0.5 * tail[0:1, :], 0.0))
    bottom = jnp.where(lane >= 64, bottom, 0.0)
    return jnp.concatenate([top, bottom], axis=0)


def blend(fs, table, core, keep, send):
    for j in range(GROUP // 2):
        for which, ref in ((core, keep), (1 - core, send)):
            s = 2 * j + which
            ref[j] = fs[s] + fs[table[s, 0]] + fs[table[s, 1]]


def gram_of(fs, q, anomaly, halves, mean, line, upper):
    lane = iota((1, 128), 1)
    swapped = pltpu.roll(line, 64, 1)
    mine = (lane >= 64) if upper else (lane < 64)
    weight = jnp.where(mine, swapped if upper else line, 0.0)
    pull = jnp.where(mine, line if upper else swapped, 0.0) - weight * mean
    left = jnp.concatenate([anomaly * weight, jnp.broadcast_to(pull, (8, 128))], axis=0)
    gram = dot_split(split(left), halves, turned=True)
    body, tail = fold(gram[:64], gram[64:128], gram[128:129])
    fs[q, pl.ds(0, 64), :] = body
    fs[q, pl.ds(64, 8), :] = tail


def centred(square):
    mean = jnp.mean(square, axis=0, keepdims=True)
    anomaly = square - mean
    return anomaly, split(anomaly), mean


def first_gram_kernel(info, got, keep, send, later, table_out, fs, table, sem):
    table_out[...] = got[pl.ds(130, GROUP, stride=136), :].astype(jnp.int32)
    copy = pltpu.make_async_copy(table_out, table, sem)
    copy.start()
    later[...] = got[pl.ds(129, GROUP, stride=136), :]
    for q in range(GROUP):
        gram_of(fs, q, *centred(square_of(got, q)), got[pl.ds(q * 136 + 128, 1), :], True)
    copy.wait()
    blend(fs, table, info[0], keep, send)


def forecast_kernel(table, info, state, low, high, hist, mixing, both, keep, send, ps, fs):
    edge = HALO * LEVELS
    span = MINE * LEVELS

    def sources(f, c):
        if c < HALO:
            return low, f * edge + c * LEVELS
        if c < HALO + MINE:
            return state, f * span + (c - HALO) * LEVELS
        return high, f * edge + (c - HALO - MINE) * LEVELS

    substeps(sources, both, ps, mixing)
    for four in range(8):
        parts = centred(four_levels(both, WIDE * LEVELS + edge, four).T)
        for half in range(2):
            q = 2 * four + half
            gram_of(fs, q, *parts, hist[pl.ds(q, 1), :], half == 1)
    blend(fs, table, info[0], keep, send)


def root_kernel(got, out):
    total = got[0]
    for j in range(1, 8):
        total = total + got[j]
    half = half_of(total[:64], total[64:])
    gram, vector = half + half.T, total[65:66]
    eye = jnp.where(iota((WIDTH, WIDTH), 0) == iota((WIDTH, WIDTH), 1), 1.0, 0.0)
    third = 1.0 / 3.0
    blended = (WIDTH - 1.0) * eye + gram * third
    pull = vector * third
    squared = jnp.sum(jnp.sum(blended * blended, axis=0, keepdims=True), axis=1, keepdims=True)
    norm = jnp.sqrt(squared)
    a = blended / norm
    newton = 1.5 * eye - 0.5 * a
    a = dot_split(split(a), split(newton))
    z = newton
    for step in range(1, ROOT_STEPS):
        newton = 1.5 * eye - 0.5 * dot_split(split(z), split(a))
        if step < ROOT_STEPS - 1:
            both = dot_split(split(jnp.concatenate([a, z], axis=0)), split(newton))
            a, z = both[:WIDTH], both[WIDTH:]
        else:
            z = dot_split(split(z), split(newton))
    halves = split(z)
    wide = jnp.broadcast_to(pull, (8, WIDTH))
    inner = dot_split(split(wide), halves, turned=True)
    shift = dot_split(split(inner), halves, turned=True)[0:1, :] / norm
    spread = z * (math.sqrt(WIDTH - 1.0) / jnp.sqrt(norm))
    sums = jnp.sum(spread, axis=0, keepdims=True) + jnp.sum(shift, axis=1, keepdims=True)
    body, tail = fold(spread[:64], spread[64:], shift, (1.0 - sums) * (1.0 / WIDTH))
    for j in range(8):
        out[j, pl.ds(0, 64), :] = body
        out[j, pl.ds(64, 8), :] = tail


def weights_of(roots, j):
    body, tail = roots[j, pl.ds(0, 64), :], roots[j, pl.ds(64, 8), :]
    half = half_of(body, tail)
    return split((half + tail[1:2, :]) + (half + tail[2:3, :]).T)


def first_apply_kernel(second, info, got, roots, *refs):
    out = refs[1] if second else refs[0]
    span = MINE * LEVELS
    edge = HALO * LEVELS
    parity = 1 - info[0] if second else info[0]
    for j in range(8):
        s = 2 * j + parity
        square = jnp.concatenate(
            [got[pl.ds(pl.multiple_of(g * 136 + s * 8, 8), 8), :] for g in range(GROUP)], axis=0
        )
        result = dot_split(weights_of(roots, j), split(square)).T
        for fj in range(4):
            at = (fj // 2) * span + 2 * s + fj % 2
            out[pl.ds(at, MINE, stride=LEVELS), :] = result[fj * 32 : fj * 32 + 32, :]
    if second:
        low, high = refs[2:]
        for f in range(2):
            low[pl.ds(f * edge, edge), :] = out[pl.ds(f * span, edge), :]
            high[pl.ds(f * edge, edge), :] = out[pl.ds((f + 1) * span - edge, edge), :]


def last_apply_kernel(second, info, both, roots, *refs):
    out = refs[-1]
    parity = 1 - info[0] if second else info[0]
    starts = []
    for chunk in range(4):
        fj = (chunk + 4 - info[2]) & 3
        starts.append((fj >> 1) * (WIDE * LEVELS) + (fj & 1) + HALO * LEVELS)
    for j in range(8):
        s = 2 * j + parity
        field = jnp.concatenate(
            [both[pl.ds(at + 2 * s, MINE, stride=LEVELS), :] for at in starts], axis=0
        )
        result = dot_split(weights_of(roots, j), split(field), turned=True)
        for g in range(GROUP):
            out[pl.ds(pl.multiple_of((g * GROUP + s) * 8, 8), 8), :] = result[g * 8 : g * 8 + 8, :]


def place_kernel(info, got, out, tiles):
    starts = [jnp.bitwise_xor(MEMBER_AT[k], info[1]) * 128 for k in range(GROUP)]
    lane = iota((16, 128), 1)
    for t in range(4):
        for n in range(8):
            rows = [got[pl.ds(starts[4 * t + p] + n, 16, stride=8), :] for p in range(4)]
            for fj in range(4):
                block = rows[(0 - fj) % 4]
                for chunk in range(1, 4):
                    block = jnp.where(lane >= 32 * chunk, rows[(chunk - fj) % 4], block)
                if fj > 0:
                    block = pltpu.roll(block, 128 - 32 * fj, 1)
                tiles[pl.ds(512 * t + (n * 2 + fj // 2) * LEVELS + fj % 2, 16, stride=2), :] = block
    for t in range(4):
        out[:, pl.ds(128 * t, 128)] = tiles[pl.ds(512 * t, 512), :]


def vmem():
    return pl.BlockSpec(memory_space=pltpu.VMEM)


def smem():
    return pl.BlockSpec(memory_space=pltpu.SMEM)


def call(kernel, out, ins, name, scratch=(), aliases=None, cost=None):
    return pl.pallas_call(
        kernel,
        out_shape=out,
        in_specs=ins,
        out_specs=jax.tree.map(lambda _: vmem(), out),
        scratch_shapes=scratch,
        input_output_aliases=aliases or {},
        cost_estimate=cost,
        compiler_params=pltpu.CompilerParams(vmem_limit_bytes=VMEM_LIMIT),
        name=name,
    )


def arr(*shape, dtype=F32):
    return jax.ShapeDtypeStruct(shape, dtype)


def across(x, forward):
    pairs = []
    for hor in range(16):
        for block in range(GROUP):
            here = MEMBER_AT[block]
            nxt = MEMBER_AT[(block + 1) % GROUP]
            nhor = (hor + (block + 1) // GROUP) % 16

            def flat(g, h):
                return ((g >> 2) * 16 + h) * 4 + (g & 3)

            pair = (flat(here ^ (15 * (hor & 1)), hor), flat(nxt ^ (15 * (nhor & 1)), nhor))
            pairs.append(pair if forward else pair[::-1])
    return lax.ppermute(x, ALL, pairs)


def swap(x):
    return lax.ppermute(x, "core", [(0, 1), (1, 0)])


def exchange(x, axes):
    return lax.all_to_all(x, axes, split_axis=0, concat_axis=0, tiled=True)


def shards(ensemble, coupling, obs_column, obs_level, obs_value, obs_error, obs_live, partners):
    rows = MINE * LEVELS
    edges = 2 * HALO * LEVELS
    members = ensemble.reshape(512, COLS)
    flip = 15 * (lax.axis_index("hor") & 1)
    block = block_of(lax.axis_index(TILE) ^ flip)
    info = jnp.stack([lax.axis_index("core"), flip, block & 3]).astype(jnp.int32)
    first, last = call(edges_kernel, (arr(HALO, COLS), arr(HALO, COLS)), [vmem()], "edges")(members)
    ring = [(i, (i + 1) % 16) for i in range(16)]
    before = lax.ppermute(last, "hor", ring)
    after = lax.ppermute(first, "hor", [(b, a) for a, b in ring])
    state, sums, mixing = call(
        prepare_kernel,
        (arr(2 * rows, 128), arr(128, 128), arr(2 * MIX, MIX, dtype=BF16)),
        [smem()] * 2 + [vmem()] * 7,
        "prepare",
        [pltpu.VMEM((2048, 128), F32), pltpu.VMEM((2048, 128), F32)],
    )(info, partners, members, obs_column, obs_level, obs_value, obs_error, obs_live, coupling)
    wide = pltpu.VMEM((WIDE * LEVELS, WIDTH), F32)
    fields = pltpu.VMEM((2 * WIDE * LEVELS, WIDTH), F32)
    packed = call(
        first_kernel,
        arr(GROUP * 136, 128),
        [smem()] + [vmem()] * 5,
        "first",
        [fields, wide, pltpu.VMEM((4 * HALO * LEVELS, 128), F32), pltpu.VMEM((64, 128), F32)],
    )(info, state, before, after, sums, mixing)
    received = exchange(packed.reshape(GROUP, 136, 128), TILE).reshape(GROUP * 136, 128)
    folded = pltpu.VMEM((GROUP, FOLD, 128), F32)
    keep, send, hist, table = call(
        first_gram_kernel,
        (arr(8, FOLD, 128), arr(8, FOLD, 128), arr(GROUP, 128), arr(GROUP, 128, dtype=jnp.int32)),
        [smem(), vmem()],
        "gram",
        [folded, pltpu.SMEM((GROUP, 128), jnp.int32), pltpu.SemaphoreType.DMA(())],
    )(info, received)

    def roots(keep, send):
        parts = exchange(keep + swap(send), CHIPS)
        copies = call(root_kernel, arr(8, FOLD, 128), [vmem()], "root")(parts)
        same = exchange(copies, CHIPS)
        return same, swap(same)

    cost = pl.CostEstimate(flops=10**9, bytes_accessed=3 * 2**20, transcendentals=0)
    same, other = roots(keep, send)
    part = call(
        functools.partial(first_apply_kernel, False),
        arr(2 * rows, WIDTH),
        [smem()] + [vmem()] * 2,
        "apply",
        cost=cost,
    )(info, received, same)
    state, low, high = call(
        functools.partial(first_apply_kernel, True),
        (arr(2 * rows, WIDTH), arr(edges, WIDTH), arr(edges, WIDTH)),
        [smem()] + [vmem()] * 3,
        "apply",
        aliases={3: 0},
    )(info, received, other, part)
    from_low = across(high, True)
    from_high = across(low, False)
    both, keep, send = call(
        forecast_kernel,
        (arr(2 * WIDE * LEVELS, WIDTH), arr(8, FOLD, 128), arr(8, FOLD, 128)),
        [smem(), smem()] + [vmem()] * 5,
        "forecast",
        [wide, folded],
    )(table, info, state, from_low, from_high, hist, mixing)
    same, other = roots(keep, send)
    part = call(
        functools.partial(last_apply_kernel, False),
        arr(GROUP * 128, 128),
        [smem()] + [vmem()] * 2,
        "analyse",
        cost=cost,
    )(info, both, same)
    analysed = call(
        functools.partial(last_apply_kernel, True),
        arr(GROUP * 128, 128),
        [smem()] + [vmem()] * 3,
        "analyse",
        aliases={3: 0},
    )(info, both, other, part)
    got = exchange(analysed.reshape(GROUP, 128, 128), TILE).reshape(GROUP * 128, 128)
    placed = call(place_kernel, arr(512, 512), [smem(), vmem()], "place", [pltpu.VMEM((2048, 128), F32)])(info, got)
    return placed.reshape(ensemble.shape)


def solution(mesh):
    fine = Mesh(mesh.devices.reshape(4, 16, 2, 2), ALL)
    group = TILE
    in_specs = (
        P(group, None, None, "hor"),
        P(),
        P(None, group, "hor", None),
        P(None, group, "hor", None),
        P(None, group, "hor", None),
        P(None, group, "hor", None),
        P(None, group, "hor", None),
        P(group, "hor", None),
    )
    out_specs = P(group, None, None, "hor")
    return jax.shard_map(shards, mesh=fine, in_specs=in_specs, out_specs=out_specs, check_vma=False)
```

```python
import functools
import math

import jax
import jax.numpy as jnp
from jax import lax
from jax.experimental import pallas as pl
from jax.experimental.pallas import tpu as pltpu
from jax.sharding import Mesh, PartitionSpec as P

SUBSTEPS = 4
ROOT_STEPS = 8
RATE = 0.5 * 0.2
MIX = 128
GROUP = 16
WIDTH = 128
LEVELS = 32
COLS = 512
MINE = COLS // GROUP
HALO = 2 * SUBSTEPS
WIDE = MINE + 2 * HALO
FOLD = 72
F32 = jnp.float32
BF16 = jnp.bfloat16
VMEM_LIMIT = 48 * 1024 * 1024
ALL = ("mem", "hor", "zh", "core")
TILE = ("mem", "zh", "core")
CHIPS = ("mem", "zh")


def block_of(g):
    return ((g >> 1) & 1) * 8 + (g >> 2) * 2 + (g & 1)


MEMBER_AT = {block_of(g): g for g in range(GROUP)}


def split(a):
    high = a.astype(BF16)
    return high, (a - high.astype(F32)).astype(BF16)


def dot_split(a, b, turned=False):
    left = jnp.concatenate([a[0], a[0], a[1]], axis=1)
    right = jnp.concatenate([b[0], b[1], b[0]], axis=1 if turned else 0)
    dims = (((1,), (1 if turned else 0,)), ((), ()))
    return lax.dot_general(left, right, dims, preferred_element_type=F32)


def iota(shape, dim):
    return lax.broadcasted_iota(jnp.int32, shape, dim)


def chunk_transpose(rows):
    lane = iota(rows[0].shape, 1)
    out = []
    for p in range(4):
        total = None
        for q in range(4):
            piece = rows[q] if p == q else pltpu.roll(rows[q], (32 * (q - p)) % 128, 1)
            total = piece if total is None else jnp.where(lane >= 32 * q, piece, total)
        out.append(total)
    return out


def edges_kernel(ens, first, last):
    first[...] = ens[:, 0:128].T[0:HALO, :]
    last[...] = ens[:, COLS - 128 : COLS].T[128 - HALO :, :]


def prepare_kernel(
    info, partner, ens, column, level, value, error, live, coupling, state, out, mixing, tiles, blocks
):
    for t in range(4):
        tiles[pl.ds(512 * t, 512), :] = ens[:, pl.ds(128 * t, 128)]
    for f in range(2):
        for t in range(4):
            for m in range(8):
                at = t * 512 + (m * 2 + f) * LEVELS
                rows = [tiles[pl.ds(at + i, 8, stride=4), :] for i in range(4)]
                for p, block in enumerate(chunk_transpose(rows)):
                    blocks[pl.ds(f * 1024 + (4 * t + p) * 8 + m, 8, stride=128), :] = block
        for four in range(8):
            turned = blocks[pl.ds(f * 1024 + four * 128, 128), :].T
            for i in range(4):
                at = f * MINE * LEVELS + 4 * four + i
                state[pl.ds(at, MINE, stride=LEVELS), :] = turned[32 * i : 32 * i + 32, :]
    member = jnp.bitwise_xor(iota((GROUP, COLS), 0), info[1])
    place = ((member >> 1) & 1) * 8 + (member >> 2) * 2 + (member & 1)
    spot = iota((64, COLS), 0)
    zero = jnp.zeros((64, COLS), F32)
    for cycle in range(2):
        col = column[cycle, 0]
        weight = live[cycle, 0].astype(F32) / error[cycle, 0]
        weighted = weight * value[cycle, 0]
        here = (col >> 5) == place
        left = jnp.concatenate([jnp.where(here, weight, 0.0), jnp.where(here, weighted, 0.0)], axis=1)
        hit = jnp.where(level[cycle, 0] * 32 + (col & 31) == spot, 1.0, 0.0)
        right = jnp.concatenate(
            [jnp.concatenate([hit, zero], axis=1), jnp.concatenate([zero, hit], axis=1)], axis=0
        )
        sums = lax.dot_general(
            left, right, (((1,), (1,)), ((), ())), precision=lax.Precision.HIGHEST, preferred_element_type=F32
        )
        out[pl.ds(cycle, GROUP, stride=8), :] = sums
    lane = iota((GROUP, 128), 1)
    first = partner[0, 0, 0].astype(F32)
    second = partner[0, 0, 1].astype(F32)
    out[pl.ds(2, GROUP, stride=8), :] = jnp.where(lane == 0, first, second)
    wide = jnp.concatenate([coupling[...]] * (MIX // LEVELS), axis=1)
    wide = jnp.concatenate([wide] * (MIX // LEVELS), axis=0)
    wide = jnp.where((iota((MIX, MIX), 0) >> 5) == (iota((MIX, MIX), 1) >> 5), RATE * RATE * wide, 0.0)
    high, rest = split(wide)
    mixing[pl.ds(0, MIX), :] = high
    mixing[pl.ds(MIX, MIX), :] = rest


def substeps(sources, both, ps, mixing):
    mix = (mixing[pl.ds(0, MIX), :], mixing[pl.ds(MIX, MIX), :])
    wide = WIDE * LEVELS
    for c in (0, WIDE - 2):
        both[pl.ds(wide + c * LEVELS, 2 * LEVELS), :] = jnp.zeros((2 * LEVELS, WIDTH), F32)

    def rows(step, f, c, count):
        if step == 0:
            ref, at = sources(f, c)
            return ref[pl.ds(at, count * LEVELS), :]
        return both[pl.ds(f * wide + c * LEVELS, count * LEVELS), :]

    def speed(step, c):
        return RATE * rows(0, 0, c, 1) if step == 0 else rows(step, 0, c, 1)

    many = MIX // LEVELS
    for step in range(SUBSTEPS):
        lo, hi = 2 * step, WIDE - 2 * step
        for c in range(0, WIDE, 2 * many):
            block = jnp.concatenate([rows(step, 1, c, many), rows(step, 1, c + many, many)], axis=1)
            pressure = dot_split(mix, split(block))
            ps[pl.ds(c * LEVELS, MIX), :] = pressure[:, :128]
            ps[pl.ds(c * LEVELS + MIX, MIX), :] = pressure[:, 128:]
        before, here = speed(step, lo), speed(step, lo + 1)
        slope_one, slope_two = ps[pl.ds(lo * LEVELS, LEVELS), :], ps[pl.ds((lo + 1) * LEVELS, LEVELS), :]
        flux_two, flux_one, height_one = None, None, None
        for c in range(lo + 1, hi - 1):
            after = speed(step, c + 1)
            slope = ps[pl.ds((c + 1) * LEVELS, LEVELS), :]
            moved = (here - here * (after - before)) - (slope - slope_one)
            height = rows(step, 1, c, 1)
            flux = moved * height
            if c >= lo + 3:
                both[pl.ds(wide + (c - 1) * LEVELS, LEVELS), :] = height_one - (flux - flux_two)
            both[pl.ds(c * LEVELS, LEVELS), :] = moved if step < SUBSTEPS - 1 else moved * (1.0 / RATE)
            before, here = here, after
            slope_one, slope_two = slope_two, slope
            flux_two, flux_one, height_one = flux_one, flux, height


def four_levels(ref, at, four):
    rows = [ref[pl.ds(at + 4 * four + i, MINE, stride=LEVELS), :] for i in range(4)]
    return jnp.concatenate(rows, axis=0)


def slab_rows(ref, at, s):
    rows = [
        ref[pl.ds(f * WIDE * LEVELS + at + 2 * s + j, MINE, stride=LEVELS), :] for f in range(2) for j in range(2)
    ]
    return jnp.concatenate(rows, axis=0)


def first_kernel(info, state, before, after, sums, mixing, packed, both, ps, sides, spare):
    span = MINE * LEVELS
    edge = HALO * LEVELS
    pieces = []
    for ref in (before, after):
        for m in range(8):
            line = ref[:, pl.ds(128 * (m // 2), 128)]
            spare[pl.ds(8 * m, 8), :] = line if m % 2 == 0 else pltpu.roll(line, 64, 1)
        pieces += [spare[pl.ds(c, 8, stride=8), :] for c in range(8)]
    halo = jnp.concatenate(pieces, axis=0).T
    lane = iota((LEVELS, 128), 1)
    for f in range(2):
        line = halo[f * LEVELS : (f + 1) * LEVELS, :]
        for c in range(HALO):
            inner = pltpu.roll(state[pl.ds(f * span + (MINE - HALO + c) * LEVELS, LEVELS), :], 8, 1)
            outer = pltpu.roll(line, (128 - 8 * c) % 128, 1)
            sides[pl.ds((2 * f) * edge + c * LEVELS, LEVELS), :] = jnp.where(lane < 8, outer, inner)
            inner = pltpu.roll(state[pl.ds(f * span + c * LEVELS, LEVELS), :], 120, 1)
            outer = pltpu.roll(line, (56 - 8 * c) % 128, 1)
            sides[pl.ds((2 * f + 1) * edge + c * LEVELS, LEVELS), :] = jnp.where(lane >= 120, outer, inner)

    def sources(f, c):
        if c < HALO:
            return sides, 2 * f * edge + c * LEVELS
        if c < HALO + MINE:
            return state, f * span + (c - HALO) * LEVELS
        return sides, (2 * f + 1) * edge + (c - HALO - MINE) * LEVELS

    substeps(sources, both, ps, mixing)
    starts = [jnp.bitwise_xor(MEMBER_AT[k], info[1]) * 136 for k in range(GROUP)]
    for s in range(GROUP):
        square = slab_rows(both, edge, s).T
        for k in range(GROUP):
            packed[pl.ds(starts[k] + 8 * s, 8), :] = square[8 * k : 8 * k + 8, :]
    for g in range(GROUP):
        packed[pl.ds(g * 136 + 128, 8), :] = sums[pl.ds(g * 8, 8), :]


def square_of(ref, s):
    return jnp.concatenate([ref[pl.ds(g * 136 + s * 8, 8), :] for g in range(GROUP)], axis=0)


def fold(top, bottom, vector, extra=0.0):
    row, lane = iota((64, 128), 0), iota((64, 128), 1)
    body = jnp.where((lane >= 64) | (row <= lane), top, pltpu.roll(bottom, 64, 1))
    diagonal = jnp.sum(jnp.where(lane == row + 64, bottom, 0.0), axis=0, keepdims=True)
    at = iota((8, 128), 0)
    tail = jnp.where(at == 0, diagonal, jnp.where(at == 1, vector, extra))
    return body, tail


def half_of(body, tail):
    row, lane = iota((64, 128), 0), iota((64, 128), 1)
    top = jnp.where((lane >= 64) | (row < lane), body, jnp.where(row == lane, 0.5 * body, 0.0))
    moved = pltpu.roll(body, 64, 1)
    bottom = jnp.where(row > lane - 64, moved, jnp.where(row == lane - 64, 0.5 * tail[0:1, :], 0.0))
    bottom = jnp.where(lane >= 64, bottom, 0.0)
    return jnp.concatenate([top, bottom], axis=0)


def blend(fs, table, core, keep, send):
    for j in range(GROUP // 2):
        for which, ref in ((core, keep), (1 - core, send)):
            s = 2 * j + which
            ref[j] = fs[s] + fs[table[s, 0]] + fs[table[s, 1]]


def gram_of(fs, q, anomaly, halves, mean, line, upper):
    lane = iota((1, 128), 1)
    swapped = pltpu.roll(line, 64, 1)
    mine = (lane >= 64) if upper else (lane < 64)
    weight = jnp.where(mine, swapped if upper else line, 0.0)
    pull = jnp.where(mine, line if upper else swapped, 0.0) - weight * mean
    left = jnp.concatenate([anomaly * weight, jnp.broadcast_to(pull, (8, 128))], axis=0)
    gram = dot_split(split(left), halves, turned=True)
    body, tail = fold(gram[:64], gram[64:128], gram[128:129])
    fs[q, pl.ds(0, 64), :] = body
    fs[q, pl.ds(64, 8), :] = tail


def centred(square):
    mean = jnp.mean(square, axis=0, keepdims=True)
    anomaly = square - mean
    return anomaly, split(anomaly), mean


def first_gram_kernel(info, got, keep, send, later, table_out, fs, table, sem):
    table_out[...] = got[pl.ds(130, GROUP, stride=136), :].astype(jnp.int32)
    copy = pltpu.make_async_copy(table_out, table, sem)
    copy.start()
    later[...] = got[pl.ds(129, GROUP, stride=136), :]
    for q in range(GROUP):
        gram_of(fs, q, *centred(square_of(got, q)), got[pl.ds(q * 136 + 128, 1), :], True)
    copy.wait()
    blend(fs, table, info[0], keep, send)


def forecast_kernel(table, info, state, outer, low, high, hist, mixing, both, keep, send, ps, fs, sides):
    edge = HALO * LEVELS
    span = MINE * LEVELS
    for f in range(2):
        rows = pl.ds(f * edge, edge)
        sides[pl.ds(2 * f * edge, edge), :] = jnp.where(info[3] == 0, outer[rows, :], low[rows, :])
        sides[pl.ds((2 * f + 1) * edge, edge), :] = jnp.where(info[3] == GROUP - 1, outer[rows, :], high[rows, :])

    def sources(f, c):
        if c < HALO:
            return sides, 2 * f * edge + c * LEVELS
        if c < HALO + MINE:
            return state, f * span + (c - HALO) * LEVELS
        return sides, (2 * f + 1) * edge + (c - HALO - MINE) * LEVELS

    substeps(sources, both, ps, mixing)
    for four in range(8):
        parts = centred(four_levels(both, WIDE * LEVELS + edge, four).T)
        for half in range(2):
            q = 2 * four + half
            gram_of(fs, q, *parts, hist[pl.ds(q, 1), :], half == 1)
    blend(fs, table, info[0], keep, send)


def root_kernel(got, out):
    total = got[0]
    for j in range(1, 8):
        total = total + got[j]
    half = half_of(total[:64], total[64:])
    gram, vector = half + half.T, total[65:66]
    eye = jnp.where(iota((WIDTH, WIDTH), 0) == iota((WIDTH, WIDTH), 1), 1.0, 0.0)
    third = 1.0 / 3.0
    blended = (WIDTH - 1.0) * eye + gram * third
    pull = vector * third
    squared = jnp.sum(jnp.sum(blended * blended, axis=0, keepdims=True), axis=1, keepdims=True)
    norm = jnp.sqrt(squared)
    a = blended / norm
    newton = 1.5 * eye - 0.5 * a
    a = dot_split(split(a), split(newton))
    z = newton
    for step in range(1, ROOT_STEPS):
        newton = 1.5 * eye - 0.5 * dot_split(split(z), split(a))
        if step < ROOT_STEPS - 1:
            both = dot_split(split(jnp.concatenate([a, z], axis=0)), split(newton))
            a, z = both[:WIDTH], both[WIDTH:]
        else:
            z = dot_split(split(z), split(newton))
    halves = split(z)
    wide = jnp.broadcast_to(pull, (8, WIDTH))
    inner = dot_split(split(wide), halves, turned=True)
    shift = dot_split(split(inner), halves, turned=True)[0:1, :] / norm
    spread = z * (math.sqrt(WIDTH - 1.0) / jnp.sqrt(norm))
    sums = jnp.sum(spread, axis=0, keepdims=True) + jnp.sum(shift, axis=1, keepdims=True)
    body, tail = fold(spread[:64], spread[64:], shift, (1.0 - sums) * (1.0 / WIDTH))
    for j in range(8):
        out[j, pl.ds(0, 64), :] = body
        out[j, pl.ds(64, 8), :] = tail


def weights_of(roots, j):
    body, tail = roots[j, pl.ds(0, 64), :], roots[j, pl.ds(64, 8), :]
    half = half_of(body, tail)
    return split((half + tail[1:2, :]) + (half + tail[2:3, :]).T)


def first_apply_kernel(second, info, got, roots, *refs):
    out = refs[1] if second else refs[0]
    span = MINE * LEVELS
    edge = HALO * LEVELS
    parity = 1 - info[0] if second else info[0]
    for j in range(8):
        s = 2 * j + parity
        square = jnp.concatenate(
            [got[pl.ds(pl.multiple_of(g * 136 + s * 8, 8), 8), :] for g in range(GROUP)], axis=0
        )
        result = dot_split(weights_of(roots, j), split(square)).T
        for fj in range(4):
            at = (fj // 2) * span + 2 * s + fj % 2
            out[pl.ds(at, MINE, stride=LEVELS), :] = result[fj * 32 : fj * 32 + 32, :]
    if second:
        low, high, outer = refs[2:]
        for f in range(2):
            first = out[pl.ds(f * span, edge), :]
            final = out[pl.ds((f + 1) * span - edge, edge), :]
            low[pl.ds(f * edge, edge), :] = first
            high[pl.ds(f * edge, edge), :] = final
            outer[pl.ds(f * edge, edge), :] = jnp.where(info[3] == GROUP - 1, final, first)


def last_apply_kernel(second, info, both, roots, *refs):
    out = refs[-1]
    parity = 1 - info[0] if second else info[0]
    starts = []
    for chunk in range(4):
        fj = (chunk + 4 - info[2]) & 3
        starts.append((fj >> 1) * (WIDE * LEVELS) + (fj & 1) + HALO * LEVELS)
    for j in range(8):
        s = 2 * j + parity
        field = jnp.concatenate(
            [both[pl.ds(at + 2 * s, MINE, stride=LEVELS), :] for at in starts], axis=0
        )
        result = dot_split(weights_of(roots, j), split(field), turned=True)
        for g in range(GROUP):
            out[pl.ds(pl.multiple_of((g * GROUP + s) * 8, 8), 8), :] = result[g * 8 : g * 8 + 8, :]


def place_kernel(info, got, out, tiles):
    starts = [jnp.bitwise_xor(MEMBER_AT[k], info[1]) * 128 for k in range(GROUP)]
    lane = iota((16, 128), 1)
    for t in range(4):
        for n in range(8):
            rows = [got[pl.ds(starts[4 * t + p] + n, 16, stride=8), :] for p in range(4)]
            for fj in range(4):
                block = rows[(0 - fj) % 4]
                for chunk in range(1, 4):
                    block = jnp.where(lane >= 32 * chunk, rows[(chunk - fj) % 4], block)
                if fj > 0:
                    block = pltpu.roll(block, 128 - 32 * fj, 1)
                tiles[pl.ds(512 * t + (n * 2 + fj // 2) * LEVELS + fj % 2, 16, stride=2), :] = block
    for t in range(4):
        out[:, pl.ds(128 * t, 128)] = tiles[pl.ds(512 * t, 512), :]


def vmem():
    return pl.BlockSpec(memory_space=pltpu.VMEM)


def smem():
    return pl.BlockSpec(memory_space=pltpu.SMEM)


def call(kernel, out, ins, name, scratch=(), aliases=None, cost=None):
    return pl.pallas_call(
        kernel,
        out_shape=out,
        in_specs=ins,
        out_specs=jax.tree.map(lambda _: vmem(), out),
        scratch_shapes=scratch,
        input_output_aliases=aliases or {},
        cost_estimate=cost,
        compiler_params=pltpu.CompilerParams(vmem_limit_bytes=VMEM_LIMIT),
        name=name,
    )


def arr(*shape, dtype=F32):
    return jax.ShapeDtypeStruct(shape, dtype)


def holder(block, hor):
    g = MEMBER_AT[block] ^ (15 * (hor & 1))
    return ((g >> 2) * 16 + hor) * 4 + (g & 3)


def next_block(x, forward):
    pairs = [(holder(b, hor), holder(b + 1, hor)) for hor in range(16) for b in range(GROUP - 1)]
    return lax.ppermute(x, ALL, pairs if forward else [(b, a) for a, b in pairs])


def next_tile(x):
    pairs = [(holder(GROUP - 1, hor), holder(0, (hor + 1) % 16)) for hor in range(16)]
    return lax.ppermute(x, ALL, pairs + [(b, a) for a, b in pairs])


def swap(x):
    return lax.ppermute(x, "core", [(0, 1), (1, 0)])


def exchange(x, axes):
    return lax.all_to_all(x, axes, split_axis=0, concat_axis=0, tiled=True)


def shards(ensemble, coupling, obs_column, obs_level, obs_value, obs_error, obs_live, partners):
    rows = MINE * LEVELS
    edges = 2 * HALO * LEVELS
    members = ensemble.reshape(512, COLS)
    flip = 15 * (lax.axis_index("hor") & 1)
    block = block_of(lax.axis_index(TILE) ^ flip)
    info = jnp.stack([lax.axis_index("core"), flip, block & 3, block]).astype(jnp.int32)
    first, last = call(edges_kernel, (arr(HALO, COLS), arr(HALO, COLS)), [vmem()], "edges")(members)
    ring = [(i, (i + 1) % 16) for i in range(16)]
    before = lax.ppermute(last, "hor", ring)
    after = lax.ppermute(first, "hor", [(b, a) for a, b in ring])
    state, sums, mixing = call(
        prepare_kernel,
        (arr(2 * rows, 128), arr(128, 128), arr(2 * MIX, MIX, dtype=BF16)),
        [smem()] * 2 + [vmem()] * 7,
        "prepare",
        [pltpu.VMEM((2048, 128), F32), pltpu.VMEM((2048, 128), F32)],
    )(info, partners, members, obs_column, obs_level, obs_value, obs_error, obs_live, coupling)
    wide = pltpu.VMEM((WIDE * LEVELS, WIDTH), F32)
    fields = pltpu.VMEM((2 * WIDE * LEVELS, WIDTH), F32)
    packed = call(
        first_kernel,
        arr(GROUP * 136, 128),
        [smem()] + [vmem()] * 5,
        "first",
        [fields, wide, pltpu.VMEM((4 * HALO * LEVELS, 128), F32), pltpu.VMEM((64, 128), F32)],
    )(info, state, before, after, sums, mixing)
    received = exchange(packed.reshape(GROUP, 136, 128), TILE).reshape(GROUP * 136, 128)
    folded = pltpu.VMEM((GROUP, FOLD, 128), F32)
    keep, send, hist, table = call(
        first_gram_kernel,
        (arr(8, FOLD, 128), arr(8, FOLD, 128), arr(GROUP, 128), arr(GROUP, 128, dtype=jnp.int32)),
        [smem(), vmem()],
        "gram",
        [folded, pltpu.SMEM((GROUP, 128), jnp.int32), pltpu.SemaphoreType.DMA(())],
    )(info, received)

    def roots(keep, send):
        parts = exchange(keep + swap(send), CHIPS)
        copies = call(root_kernel, arr(8, FOLD, 128), [vmem()], "root")(parts)
        same = exchange(copies, CHIPS)
        return same, swap(same)

    cost = pl.CostEstimate(flops=10**9, bytes_accessed=3 * 2**20, transcendentals=0)
    same, other = roots(keep, send)
    part = call(
        functools.partial(first_apply_kernel, False),
        arr(2 * rows, WIDTH),
        [smem()] + [vmem()] * 2,
        "apply",
        cost=cost,
    )(info, received, same)
    state, low, high, outer = call(
        functools.partial(first_apply_kernel, True),
        (arr(2 * rows, WIDTH),) + (arr(edges, WIDTH),) * 3,
        [smem()] + [vmem()] * 3,
        "apply",
        aliases={3: 0},
    )(info, received, other, part)
    from_tile = next_tile(outer)
    from_low = next_block(high, True)
    from_high = next_block(low, False)
    both, keep, send = call(
        forecast_kernel,
        (arr(2 * WIDE * LEVELS, WIDTH), arr(8, FOLD, 128), arr(8, FOLD, 128)),
        [smem(), smem()] + [vmem()] * 6,
        "forecast",
        [wide, folded, pltpu.VMEM((4 * HALO * LEVELS, 128), F32)],
    )(table, info, state, from_tile, from_low, from_high, hist, mixing)
    same, other = roots(keep, send)
    part = call(
        functools.partial(last_apply_kernel, False),
        arr(GROUP * 128, 128),
        [smem()] + [vmem()] * 2,
        "analyse",
        cost=cost,
    )(info, both, same)
    analysed = call(
        functools.partial(last_apply_kernel, True),
        arr(GROUP * 128, 128),
        [smem()] + [vmem()] * 3,
        "analyse",
        aliases={3: 0},
    )(info, both, other, part)
    got = exchange(analysed.reshape(GROUP, 128, 128), TILE).reshape(GROUP * 128, 128)
    placed = call(place_kernel, arr(512, 512), [smem(), vmem()], "place", [pltpu.VMEM((2048, 128), F32)])(info, got)
    return placed.reshape(ensemble.shape)


def solution(mesh):
    fine = Mesh(mesh.devices.reshape(4, 16, 2, 2), ALL)
    group = TILE
    in_specs = (
        P(group, None, None, "hor"),
        P(),
        P(None, group, "hor", None),
        P(None, group, "hor", None),
        P(None, group, "hor", None),
        P(None, group, "hor", None),
        P(None, group, "hor", None),
        P(group, "hor", None),
    )
    out_specs = P(group, None, None, "hor")
    return jax.shard_map(shards, mesh=fine, in_specs=in_specs, out_specs=out_specs, check_vma=False)
```

```python
import functools
import math

import jax
import jax.numpy as jnp
from jax import lax
from jax.experimental import pallas as pl
from jax.experimental.pallas import tpu as pltpu
from jax.sharding import Mesh, PartitionSpec as P

SUBSTEPS = 4
ROOT_STEPS = 8
RATE = 0.5 * 0.2
MIX = 128
GROUP = 16
WIDTH = 128
LEVELS = 32
COLS = 512
MINE = COLS // GROUP
HALO = 2 * SUBSTEPS
WIDE = MINE + 2 * HALO
FOLD = 72
F32 = jnp.float32
BF16 = jnp.bfloat16
VMEM_LIMIT = 48 * 1024 * 1024
ALL = ("mem", "hor", "zh", "core")
TILE = ("mem", "zh", "core")
CHIPS = ("mem", "zh")


def block_of(g):
    return ((g >> 1) & 1) * 8 + (g >> 2) * 2 + (g & 1)


MEMBER_AT = {block_of(g): g for g in range(GROUP)}


def split(a):
    high = a.astype(BF16)
    return high, (a - high.astype(F32)).astype(BF16)


def dot_split(a, b, turned=False):
    left = jnp.concatenate([a[0], a[0], a[1]], axis=1)
    right = jnp.concatenate([b[0], b[1], b[0]], axis=1 if turned else 0)
    dims = (((1,), (1 if turned else 0,)), ((), ()))
    return lax.dot_general(left, right, dims, preferred_element_type=F32)


def iota(shape, dim):
    return lax.broadcasted_iota(jnp.int32, shape, dim)


def chunk_transpose(rows):
    lane = iota(rows[0].shape, 1)
    out = []
    for p in range(4):
        total = None
        for q in range(4):
            piece = rows[q] if p == q else pltpu.roll(rows[q], (32 * (q - p)) % 128, 1)
            total = piece if total is None else jnp.where(lane >= 32 * q, piece, total)
        out.append(total)
    return out


def edges_kernel(info, ens, near, far):
    first = ens[:, 0:128].T[0:HALO, :]
    last = ens[:, COLS - 128 : COLS].T[128 - HALO :, :]
    even = info[1] == 0
    near[...] = jnp.where(even, last, first)
    far[...] = jnp.where(even, first, last)


def prepare_kernel(
    info, partner, ens, column, level, value, error, live, coupling, state, out, mixing, tiles, blocks
):
    for t in range(4):
        tiles[pl.ds(512 * t, 512), :] = ens[:, pl.ds(128 * t, 128)]
    for f in range(2):
        for t in range(4):
            for m in range(8):
                at = t * 512 + (m * 2 + f) * LEVELS
                rows = [tiles[pl.ds(at + i, 8, stride=4), :] for i in range(4)]
                for p, block in enumerate(chunk_transpose(rows)):
                    blocks[pl.ds(f * 1024 + (4 * t + p) * 8 + m, 8, stride=128), :] = block
        for four in range(8):
            turned = blocks[pl.ds(f * 1024 + four * 128, 128), :].T
            for i in range(4):
                at = f * MINE * LEVELS + 4 * four + i
                state[pl.ds(at, MINE, stride=LEVELS), :] = turned[32 * i : 32 * i + 32, :]
    member = jnp.bitwise_xor(iota((GROUP, COLS), 0), info[1])
    place = ((member >> 1) & 1) * 8 + (member >> 2) * 2 + (member & 1)
    spot = iota((64, COLS), 0)
    zero = jnp.zeros((64, COLS), F32)
    for cycle in range(2):
        col = column[cycle, 0]
        weight = live[cycle, 0].astype(F32) / error[cycle, 0]
        weighted = weight * value[cycle, 0]
        here = (col >> 5) == place
        left = jnp.concatenate([jnp.where(here, weight, 0.0), jnp.where(here, weighted, 0.0)], axis=1)
        hit = jnp.where(level[cycle, 0] * 32 + (col & 31) == spot, 1.0, 0.0)
        right = jnp.concatenate(
            [jnp.concatenate([hit, zero], axis=1), jnp.concatenate([zero, hit], axis=1)], axis=0
        )
        sums = lax.dot_general(
            left, right, (((1,), (1,)), ((), ())), precision=lax.Precision.HIGHEST, preferred_element_type=F32
        )
        out[pl.ds(cycle, GROUP, stride=8), :] = sums
    lane = iota((GROUP, 128), 1)
    first = partner[0, 0, 0].astype(F32)
    second = partner[0, 0, 1].astype(F32)
    out[pl.ds(2, GROUP, stride=8), :] = jnp.where(lane == 0, first, second)
    wide = jnp.concatenate([coupling[...]] * (MIX // LEVELS), axis=1)
    wide = jnp.concatenate([wide] * (MIX // LEVELS), axis=0)
    wide = jnp.where((iota((MIX, MIX), 0) >> 5) == (iota((MIX, MIX), 1) >> 5), RATE * RATE * wide, 0.0)
    high, rest = split(wide)
    mixing[pl.ds(0, MIX), :] = high
    mixing[pl.ds(MIX, MIX), :] = rest


def substeps(sources, both, ps, mixing):
    mix = (mixing[pl.ds(0, MIX), :], mixing[pl.ds(MIX, MIX), :])
    wide = WIDE * LEVELS
    for c in (0, WIDE - 2):
        both[pl.ds(wide + c * LEVELS, 2 * LEVELS), :] = jnp.zeros((2 * LEVELS, WIDTH), F32)

    def rows(step, f, c, count):
        if step == 0:
            ref, at = sources(f, c)
            return ref[pl.ds(at, count * LEVELS), :]
        return both[pl.ds(f * wide + c * LEVELS, count * LEVELS), :]

    def speed(step, c):
        return RATE * rows(0, 0, c, 1) if step == 0 else rows(step, 0, c, 1)

    many = MIX // LEVELS
    for step in range(SUBSTEPS):
        lo, hi = 2 * step, WIDE - 2 * step
        for c in range(0, WIDE, 2 * many):
            block = jnp.concatenate([rows(step, 1, c, many), rows(step, 1, c + many, many)], axis=1)
            pressure = dot_split(mix, split(block))
            ps[pl.ds(c * LEVELS, MIX), :] = pressure[:, :128]
            ps[pl.ds(c * LEVELS + MIX, MIX), :] = pressure[:, 128:]
        before, here = speed(step, lo), speed(step, lo + 1)
        slope_one, slope_two = ps[pl.ds(lo * LEVELS, LEVELS), :], ps[pl.ds((lo + 1) * LEVELS, LEVELS), :]
        flux_two, flux_one, height_one = None, None, None
        for c in range(lo + 1, hi - 1):
            after = speed(step, c + 1)
            slope = ps[pl.ds((c + 1) * LEVELS, LEVELS), :]
            moved = (here - here * (after - before)) - (slope - slope_one)
            height = rows(step, 1, c, 1)
            flux = moved * height
            if c >= lo + 3:
                both[pl.ds(wide + (c - 1) * LEVELS, LEVELS), :] = height_one - (flux - flux_two)
            both[pl.ds(c * LEVELS, LEVELS), :] = moved if step < SUBSTEPS - 1 else moved * (1.0 / RATE)
            before, here = here, after
            slope_one, slope_two = slope_two, slope
            flux_two, flux_one, height_one = flux_one, flux, height


def four_levels(ref, at, four):
    rows = [ref[pl.ds(at + 4 * four + i, MINE, stride=LEVELS), :] for i in range(4)]
    return jnp.concatenate(rows, axis=0)


def slab_rows(ref, at, s):
    rows = [
        ref[pl.ds(f * WIDE * LEVELS + at + 2 * s + j, MINE, stride=LEVELS), :] for f in range(2) for j in range(2)
    ]
    return jnp.concatenate(rows, axis=0)


def first_kernel(info, state, near, far, sums, mixing, packed, both, ps, sides, spare):
    span = MINE * LEVELS
    edge = HALO * LEVELS
    pieces = []
    even = info[1] == 0
    for before, after in ((far, near), (near, far)):
        for m in range(8):
            lanes = pl.ds(128 * (m // 2), 128)
            line = jnp.where(even, before[:, lanes], after[:, lanes])
            spare[pl.ds(8 * m, 8), :] = line if m % 2 == 0 else pltpu.roll(line, 64, 1)
        pieces += [spare[pl.ds(c, 8, stride=8), :] for c in range(8)]
    halo = jnp.concatenate(pieces, axis=0).T
    lane = iota((LEVELS, 128), 1)
    for f in range(2):
        line = halo[f * LEVELS : (f + 1) * LEVELS, :]
        for c in range(HALO):
            inner = pltpu.roll(state[pl.ds(f * span + (MINE - HALO + c) * LEVELS, LEVELS), :], 8, 1)
            outer = pltpu.roll(line, (128 - 8 * c) % 128, 1)
            sides[pl.ds((2 * f) * edge + c * LEVELS, LEVELS), :] = jnp.where(lane < 8, outer, inner)
            inner = pltpu.roll(state[pl.ds(f * span + c * LEVELS, LEVELS), :], 120, 1)
            outer = pltpu.roll(line, (56 - 8 * c) % 128, 1)
            sides[pl.ds((2 * f + 1) * edge + c * LEVELS, LEVELS), :] = jnp.where(lane >= 120, outer, inner)

    def sources(f, c):
        if c < HALO:
            return sides, 2 * f * edge + c * LEVELS
        if c < HALO + MINE:
            return state, f * span + (c - HALO) * LEVELS
        return sides, (2 * f + 1) * edge + (c - HALO - MINE) * LEVELS

    substeps(sources, both, ps, mixing)
    starts = [jnp.bitwise_xor(MEMBER_AT[k], info[1]) * 136 for k in range(GROUP)]
    for s in range(GROUP):
        square = slab_rows(both, edge, s).T
        for k in range(GROUP):
            packed[pl.ds(starts[k] + 8 * s, 8), :] = square[8 * k : 8 * k + 8, :]
    for g in range(GROUP):
        packed[pl.ds(g * 136 + 128, 8), :] = sums[pl.ds(g * 8, 8), :]


def square_of(ref, s):
    return jnp.concatenate([ref[pl.ds(g * 136 + s * 8, 8), :] for g in range(GROUP)], axis=0)


def fold(top, bottom, vector, extra=0.0):
    row, lane = iota((64, 128), 0), iota((64, 128), 1)
    body = jnp.where((lane >= 64) | (row <= lane), top, pltpu.roll(bottom, 64, 1))
    diagonal = jnp.sum(jnp.where(lane == row + 64, bottom, 0.0), axis=0, keepdims=True)
    at = iota((8, 128), 0)
    tail = jnp.where(at == 0, diagonal, jnp.where(at == 1, vector, extra))
    return body, tail


def half_of(body, tail):
    row, lane = iota((64, 128), 0), iota((64, 128), 1)
    top = jnp.where((lane >= 64) | (row < lane), body, jnp.where(row == lane, 0.5 * body, 0.0))
    moved = pltpu.roll(body, 64, 1)
    bottom = jnp.where(row > lane - 64, moved, jnp.where(row == lane - 64, 0.5 * tail[0:1, :], 0.0))
    bottom = jnp.where(lane >= 64, bottom, 0.0)
    return jnp.concatenate([top, bottom], axis=0)


def blend(fs, table, core, keep, send):
    for j in range(GROUP // 2):
        for which, ref in ((core, keep), (1 - core, send)):
            s = 2 * j + which
            ref[j] = fs[s] + fs[table[s, 0]] + fs[table[s, 1]]


def gram_of(fs, q, anomaly, halves, mean, line, upper):
    lane = iota((1, 128), 1)
    swapped = pltpu.roll(line, 64, 1)
    mine = (lane >= 64) if upper else (lane < 64)
    weight = jnp.where(mine, swapped if upper else line, 0.0)
    pull = jnp.where(mine, line if upper else swapped, 0.0) - weight * mean
    left = jnp.concatenate([anomaly * weight, jnp.broadcast_to(pull, (8, 128))], axis=0)
    gram = dot_split(split(left), halves, turned=True)
    body, tail = fold(gram[:64], gram[64:128], gram[128:129])
    fs[q, pl.ds(0, 64), :] = body
    fs[q, pl.ds(64, 8), :] = tail


def centred(square):
    mean = jnp.mean(square, axis=0, keepdims=True)
    anomaly = square - mean
    return anomaly, split(anomaly), mean


def first_gram_kernel(info, got, keep, send, later, table_out, fs, table, sem):
    table_out[...] = got[pl.ds(130, GROUP, stride=136), :].astype(jnp.int32)
    copy = pltpu.make_async_copy(table_out, table, sem)
    copy.start()
    later[...] = got[pl.ds(129, GROUP, stride=136), :]
    for q in range(GROUP):
        gram_of(fs, q, *centred(square_of(got, q)), got[pl.ds(q * 136 + 128, 1), :], True)
    copy.wait()
    blend(fs, table, info[0], keep, send)


def forecast_kernel(table, info, state, outer, inner, hist, mixing, both, keep, send, ps, fs, sides):
    edge = HALO * LEVELS
    span = MINE * LEVELS
    odd = (info[3] & 1) == 1
    for f in range(2):
        rows = pl.ds(f * edge, edge)
        sides[pl.ds(2 * f * edge, edge), :] = jnp.where(odd, inner[rows, :], outer[rows, :])
        sides[pl.ds((2 * f + 1) * edge, edge), :] = jnp.where(odd, outer[rows, :], inner[rows, :])

    def sources(f, c):
        if c < HALO:
            return sides, 2 * f * edge + c * LEVELS
        if c < HALO + MINE:
            return state, f * span + (c - HALO) * LEVELS
        return sides, (2 * f + 1) * edge + (c - HALO - MINE) * LEVELS

    substeps(sources, both, ps, mixing)
    for four in range(8):
        parts = centred(four_levels(both, WIDE * LEVELS + edge, four).T)
        for half in range(2):
            q = 2 * four + half
            gram_of(fs, q, *parts, hist[pl.ds(q, 1), :], half == 1)
    blend(fs, table, info[0], keep, send)


def root_kernel(got, out):
    total = got[0]
    for j in range(1, 8):
        total = total + got[j]
    half = half_of(total[:64], total[64:])
    gram, vector = half + half.T, total[65:66]
    eye = jnp.where(iota((WIDTH, WIDTH), 0) == iota((WIDTH, WIDTH), 1), 1.0, 0.0)
    third = 1.0 / 3.0
    blended = (WIDTH - 1.0) * eye + gram * third
    pull = vector * third
    squared = jnp.sum(jnp.sum(blended * blended, axis=0, keepdims=True), axis=1, keepdims=True)
    norm = jnp.sqrt(squared)
    a = blended / norm
    newton = 1.5 * eye - 0.5 * a
    a = dot_split(split(a), split(newton))
    z = newton
    for step in range(1, ROOT_STEPS):
        newton = 1.5 * eye - 0.5 * dot_split(split(z), split(a))
        if step < ROOT_STEPS - 1:
            both = dot_split(split(jnp.concatenate([a, z], axis=0)), split(newton))
            a, z = both[:WIDTH], both[WIDTH:]
        else:
            z = dot_split(split(z), split(newton))
    halves = split(z)
    wide = jnp.broadcast_to(pull, (8, WIDTH))
    inner = dot_split(split(wide), halves, turned=True)
    shift = dot_split(split(inner), halves, turned=True)[0:1, :] / norm
    spread = z * (math.sqrt(WIDTH - 1.0) / jnp.sqrt(norm))
    sums = jnp.sum(spread, axis=0, keepdims=True) + jnp.sum(shift, axis=1, keepdims=True)
    body, tail = fold(spread[:64], spread[64:], shift, (1.0 - sums) * (1.0 / WIDTH))
    for j in range(8):
        out[j, pl.ds(0, 64), :] = body
        out[j, pl.ds(64, 8), :] = tail


def weights_of(roots, j):
    body, tail = roots[j, pl.ds(0, 64), :], roots[j, pl.ds(64, 8), :]
    half = half_of(body, tail)
    return split((half + tail[1:2, :]) + (half + tail[2:3, :]).T)


def first_apply_kernel(second, info, got, roots, *refs):
    out = refs[1] if second else refs[0]
    span = MINE * LEVELS
    edge = HALO * LEVELS
    parity = 1 - info[0] if second else info[0]
    for j in range(8):
        s = 2 * j + parity
        square = jnp.concatenate(
            [got[pl.ds(pl.multiple_of(g * 136 + s * 8, 8), 8), :] for g in range(GROUP)], axis=0
        )
        result = dot_split(weights_of(roots, j), split(square)).T
        for fj in range(4):
            at = (fj // 2) * span + 2 * s + fj % 2
            out[pl.ds(at, MINE, stride=LEVELS), :] = result[fj * 32 : fj * 32 + 32, :]
    if second:
        outer, inner = refs[2:]
        odd = (info[3] & 1) == 1
        for f in range(2):
            first = out[pl.ds(f * span, edge), :]
            final = out[pl.ds((f + 1) * span - edge, edge), :]
            outer[pl.ds(f * edge, edge), :] = jnp.where(odd, final, first)
            inner[pl.ds(f * edge, edge), :] = jnp.where(odd, first, final)


def last_apply_kernel(second, info, both, roots, *refs):
    out = refs[-1]
    parity = 1 - info[0] if second else info[0]
    starts = []
    for chunk in range(4):
        fj = (chunk + 4 - info[2]) & 3
        starts.append((fj >> 1) * (WIDE * LEVELS) + (fj & 1) + HALO * LEVELS)
    for j in range(8):
        s = 2 * j + parity
        field = jnp.concatenate(
            [both[pl.ds(at + 2 * s, MINE, stride=LEVELS), :] for at in starts], axis=0
        )
        result = dot_split(weights_of(roots, j), split(field), turned=True)
        for g in range(GROUP):
            out[pl.ds(pl.multiple_of((g * GROUP + s) * 8, 8), 8), :] = result[g * 8 : g * 8 + 8, :]


def place_kernel(info, got, out, tiles):
    starts = [jnp.bitwise_xor(MEMBER_AT[k], info[1]) * 128 for k in range(GROUP)]
    lane = iota((16, 128), 1)
    for t in range(4):
        for n in range(8):
            rows = [got[pl.ds(starts[4 * t + p] + n, 16, stride=8), :] for p in range(4)]
            for fj in range(4):
                block = rows[(0 - fj) % 4]
                for chunk in range(1, 4):
                    block = jnp.where(lane >= 32 * chunk, rows[(chunk - fj) % 4], block)
                if fj > 0:
                    block = pltpu.roll(block, 128 - 32 * fj, 1)
                tiles[pl.ds(512 * t + (n * 2 + fj // 2) * LEVELS + fj % 2, 16, stride=2), :] = block
    for t in range(4):
        out[:, pl.ds(128 * t, 128)] = tiles[pl.ds(512 * t, 512), :]


def vmem():
    return pl.BlockSpec(memory_space=pltpu.VMEM)


def smem():
    return pl.BlockSpec(memory_space=pltpu.SMEM)


def call(kernel, out, ins, name, scratch=(), aliases=None, cost=None):
    return pl.pallas_call(
        kernel,
        out_shape=out,
        in_specs=ins,
        out_specs=jax.tree.map(lambda _: vmem(), out),
        scratch_shapes=scratch,
        input_output_aliases=aliases or {},
        cost_estimate=cost,
        compiler_params=pltpu.CompilerParams(vmem_limit_bytes=VMEM_LIMIT),
        name=name,
    )


def arr(*shape, dtype=F32):
    return jax.ShapeDtypeStruct(shape, dtype)


def holder(block, hor):
    g = MEMBER_AT[block] ^ (15 * (hor & 1))
    return ((g >> 2) * 16 + hor) * 4 + (g & 3)


def block_pairs(start):
    pairs = []
    for hor in range(16):
        for block in range(start, GROUP, 2):
            after = block + 1
            pair = (holder(block, hor), holder(after % GROUP, (hor + after // GROUP) % 16))
            pairs += [pair, pair[::-1]]
    return pairs


def swap(x):
    return lax.ppermute(x, "core", [(0, 1), (1, 0)])


def exchange(x, axes):
    return lax.all_to_all(x, axes, split_axis=0, concat_axis=0, tiled=True)


def shards(ensemble, coupling, obs_column, obs_level, obs_value, obs_error, obs_live, partners):
    rows = MINE * LEVELS
    edges = 2 * HALO * LEVELS
    members = ensemble.reshape(512, COLS)
    flip = 15 * (lax.axis_index("hor") & 1)
    block = block_of(lax.axis_index(TILE) ^ flip)
    info = jnp.stack([lax.axis_index("core"), flip, block & 3, block]).astype(jnp.int32)
    near, far = call(edges_kernel, (arr(HALO, COLS), arr(HALO, COLS)), [smem(), vmem()], "edges")(info, members)
    near = lax.ppermute(near, "hor", [(i, i ^ 1) for i in range(16)])
    far = lax.ppermute(far, "hor", [(i, (i - 1 + 2 * (i & 1)) % 16) for i in range(16)])
    state, sums, mixing = call(
        prepare_kernel,
        (arr(2 * rows, 128), arr(128, 128), arr(2 * MIX, MIX, dtype=BF16)),
        [smem()] * 2 + [vmem()] * 7,
        "prepare",
        [pltpu.VMEM((2048, 128), F32), pltpu.VMEM((2048, 128), F32)],
    )(info, partners, members, obs_column, obs_level, obs_value, obs_error, obs_live, coupling)
    wide = pltpu.VMEM((WIDE * LEVELS, WIDTH), F32)
    fields = pltpu.VMEM((2 * WIDE * LEVELS, WIDTH), F32)
    packed = call(
        first_kernel,
        arr(GROUP * 136, 128),
        [smem()] + [vmem()] * 5,
        "first",
        [fields, wide, pltpu.VMEM((4 * HALO * LEVELS, 128), F32), pltpu.VMEM((64, 128), F32)],
    )(info, state, near, far, sums, mixing)
    received = exchange(packed.reshape(GROUP, 136, 128), TILE).reshape(GROUP * 136, 128)
    folded = pltpu.VMEM((GROUP, FOLD, 128), F32)
    keep, send, hist, table = call(
        first_gram_kernel,
        (arr(8, FOLD, 128), arr(8, FOLD, 128), arr(GROUP, 128), arr(GROUP, 128, dtype=jnp.int32)),
        [smem(), vmem()],
        "gram",
        [folded, pltpu.SMEM((GROUP, 128), jnp.int32), pltpu.SemaphoreType.DMA(())],
    )(info, received)

    def roots(keep, send):
        parts = exchange(keep + swap(send), CHIPS)
        copies = call(root_kernel, arr(8, FOLD, 128), [vmem()], "root")(parts)
        same = exchange(copies, CHIPS)
        return same, swap(same)

    cost = pl.CostEstimate(flops=10**9, bytes_accessed=3 * 2**20, transcendentals=0)
    same, other = roots(keep, send)
    part = call(
        functools.partial(first_apply_kernel, False),
        arr(2 * rows, WIDTH),
        [smem()] + [vmem()] * 2,
        "apply",
        cost=cost,
    )(info, received, same)
    state, outer, inner = call(
        functools.partial(first_apply_kernel, True),
        (arr(2 * rows, WIDTH),) + (arr(edges, WIDTH),) * 2,
        [smem()] + [vmem()] * 3,
        "apply",
        aliases={3: 0},
    )(info, received, other, part)
    outer = lax.ppermute(outer, ALL, block_pairs(1))
    inner = lax.ppermute(inner, ALL, block_pairs(0))
    both, keep, send = call(
        forecast_kernel,
        (arr(2 * WIDE * LEVELS, WIDTH), arr(8, FOLD, 128), arr(8, FOLD, 128)),
        [smem(), smem()] + [vmem()] * 5,
        "forecast",
        [wide, folded, pltpu.VMEM((4 * HALO * LEVELS, 128), F32)],
    )(table, info, state, outer, inner, hist, mixing)
    same, other = roots(keep, send)
    part = call(
        functools.partial(last_apply_kernel, False),
        arr(GROUP * 128, 128),
        [smem()] + [vmem()] * 2,
        "analyse",
        cost=cost,
    )(info, both, same)
    analysed = call(
        functools.partial(last_apply_kernel, True),
        arr(GROUP * 128, 128),
        [smem()] + [vmem()] * 3,
        "analyse",
        aliases={3: 0},
    )(info, both, other, part)
    got = exchange(analysed.reshape(GROUP, 128, 128), TILE).reshape(GROUP * 128, 128)
    placed = call(place_kernel, arr(512, 512), [smem(), vmem()], "place", [pltpu.VMEM((2048, 128), F32)])(info, got)
    return placed.reshape(ensemble.shape)


def solution(mesh):
    fine = Mesh(mesh.devices.reshape(4, 16, 2, 2), ALL)
    group = TILE
    in_specs = (
        P(group, None, None, "hor"),
        P(),
        P(None, group, "hor", None),
        P(None, group, "hor", None),
        P(None, group, "hor", None),
        P(None, group, "hor", None),
        P(None, group, "hor", None),
        P(group, "hor", None),
    )
    out_specs = P(group, None, None, "hor")
    return jax.shard_map(shards, mesh=fine, in_specs=in_specs, out_specs=out_specs, check_vma=False)
```

```python
import functools
import math

import jax
import jax.numpy as jnp
from jax import lax
from jax.experimental import pallas as pl
from jax.experimental.pallas import tpu as pltpu
from jax.sharding import Mesh, PartitionSpec as P

SUBSTEPS = 4
ROOT_STEPS = 8
RATE = 0.5 * 0.2
MIX = 128
GROUP = 16
WIDTH = 128
LEVELS = 32
COLS = 512
MINE = COLS // GROUP
HALO = 2 * SUBSTEPS
WIDE = MINE + 2 * HALO
FOLD = 72
F32 = jnp.float32
BF16 = jnp.bfloat16
VMEM_LIMIT = 48 * 1024 * 1024
ALL = ("mem", "hor", "zh", "core")
TILE = ("mem", "zh", "core")
CHIPS = ("mem", "zh")


def block_of(g):
    return ((g >> 1) & 1) * 8 + (g >> 2) * 2 + (g & 1)


MEMBER_AT = {block_of(g): g for g in range(GROUP)}


def my_place():
    core = lax.axis_index("core")
    flip = 15 * (lax.axis_index("hor") & 1)
    g = lax.axis_index("mem") * 4 + lax.axis_index("zh") * 2 + core
    return core, flip, block_of(jnp.bitwise_xor(g, flip))


def split(a):
    high = a.astype(BF16)
    return high, (a - high.astype(F32)).astype(BF16)


def dot_split(a, b, turned=False):
    left = jnp.concatenate([a[0], a[0], a[1]], axis=1)
    right = jnp.concatenate([b[0], b[1], b[0]], axis=1 if turned else 0)
    dims = (((1,), (1 if turned else 0,)), ((), ()))
    return lax.dot_general(left, right, dims, preferred_element_type=F32)


def iota(shape, dim):
    return lax.broadcasted_iota(jnp.int32, shape, dim)


def chunk_transpose(rows):
    lane = iota(rows[0].shape, 1)
    out = []
    for p in range(4):
        total = None
        for q in range(4):
            piece = rows[q] if p == q else pltpu.roll(rows[q], (32 * (q - p)) % 128, 1)
            total = piece if total is None else jnp.where(lane >= 32 * q, piece, total)
        out.append(total)
    return out


def edges_kernel(ens, near, far):
    first = ens[:, 0:128].T[0:HALO, :]
    last = ens[:, COLS - 128 : COLS].T[128 - HALO :, :]
    even = my_place()[1] == 0
    near[...] = jnp.where(even, last, first)
    far[...] = jnp.where(even, first, last)


def prepare_kernel(
    partner, ens, column, level, value, error, live, coupling, state, out, mixing, tiles, blocks
):
    for t in range(4):
        tiles[pl.ds(512 * t, 512), :] = ens[:, pl.ds(128 * t, 128)]
    for f in range(2):
        for t in range(4):
            for m in range(8):
                at = t * 512 + (m * 2 + f) * LEVELS
                rows = [tiles[pl.ds(at + i, 8, stride=4), :] for i in range(4)]
                for p, block in enumerate(chunk_transpose(rows)):
                    blocks[pl.ds(f * 1024 + (4 * t + p) * 8 + m, 8, stride=128), :] = block
        for four in range(8):
            turned = blocks[pl.ds(f * 1024 + four * 128, 128), :].T
            for i in range(4):
                at = f * MINE * LEVELS + 4 * four + i
                state[pl.ds(at, MINE, stride=LEVELS), :] = turned[32 * i : 32 * i + 32, :]
    member = jnp.bitwise_xor(iota((GROUP, COLS), 0), my_place()[1])
    place = ((member >> 1) & 1) * 8 + (member >> 2) * 2 + (member & 1)
    spot = iota((64, COLS), 0)
    zero = jnp.zeros((64, COLS), F32)
    for cycle in range(2):
        col = column[cycle, 0]
        weight = live[cycle, 0].astype(F32) / error[cycle, 0]
        weighted = weight * value[cycle, 0]
        here = (col >> 5) == place
        left = jnp.concatenate([jnp.where(here, weight, 0.0), jnp.where(here, weighted, 0.0)], axis=1)
        hit = jnp.where(level[cycle, 0] * 32 + (col & 31) == spot, 1.0, 0.0)
        right = jnp.concatenate(
            [jnp.concatenate([hit, zero], axis=1), jnp.concatenate([zero, hit], axis=1)], axis=0
        )
        sums = lax.dot_general(
            left, right, (((1,), (1,)), ((), ())), precision=lax.Precision.HIGHEST, preferred_element_type=F32
        )
        out[pl.ds(cycle, GROUP, stride=8), :] = sums
    lane = iota((GROUP, 128), 1)
    both = partner[0].astype(F32)
    out[pl.ds(2, GROUP, stride=8), :] = jnp.where(lane == 0, both[:, 0:1], both[:, 1:2])
    wide = jnp.concatenate([coupling[...]] * (MIX // LEVELS), axis=1)
    wide = jnp.concatenate([wide] * (MIX // LEVELS), axis=0)
    wide = jnp.where((iota((MIX, MIX), 0) >> 5) == (iota((MIX, MIX), 1) >> 5), RATE * RATE * wide, 0.0)
    high, rest = split(wide)
    mixing[pl.ds(0, MIX), :] = high
    mixing[pl.ds(MIX, MIX), :] = rest


def substeps(sources, both, ps, mixing):
    mix = (mixing[pl.ds(0, MIX), :], mixing[pl.ds(MIX, MIX), :])
    wide = WIDE * LEVELS
    for c in (0, WIDE - 2):
        both[pl.ds(wide + c * LEVELS, 2 * LEVELS), :] = jnp.zeros((2 * LEVELS, WIDTH), F32)

    def rows(step, f, c, count):
        if step == 0:
            ref, at = sources(f, c)
            return ref[pl.ds(at, count * LEVELS), :]
        return both[pl.ds(f * wide + c * LEVELS, count * LEVELS), :]

    def speed(step, c):
        return RATE * rows(0, 0, c, 1) if step == 0 else rows(step, 0, c, 1)

    many = MIX // LEVELS
    for step in range(SUBSTEPS):
        lo, hi = 2 * step, WIDE - 2 * step
        for c in range(0, WIDE, 2 * many):
            block = jnp.concatenate([rows(step, 1, c, many), rows(step, 1, c + many, many)], axis=1)
            pressure = dot_split(mix, split(block))
            ps[pl.ds(c * LEVELS, MIX), :] = pressure[:, :128]
            ps[pl.ds(c * LEVELS + MIX, MIX), :] = pressure[:, 128:]
        before, here = speed(step, lo), speed(step, lo + 1)
        slope_one, slope_two = ps[pl.ds(lo * LEVELS, LEVELS), :], ps[pl.ds((lo + 1) * LEVELS, LEVELS), :]
        flux_two, flux_one, height_one = None, None, None
        for c in range(lo + 1, hi - 1):
            after = speed(step, c + 1)
            slope = ps[pl.ds((c + 1) * LEVELS, LEVELS), :]
            moved = (here - here * (after - before)) - (slope - slope_one)
            height = rows(step, 1, c, 1)
            flux = moved * height
            if c >= lo + 3:
                both[pl.ds(wide + (c - 1) * LEVELS, LEVELS), :] = height_one - (flux - flux_two)
            both[pl.ds(c * LEVELS, LEVELS), :] = moved if step < SUBSTEPS - 1 else moved * (1.0 / RATE)
            before, here = here, after
            slope_one, slope_two = slope_two, slope
            flux_two, flux_one, height_one = flux_one, flux, height


def four_levels(ref, at, four):
    rows = [ref[pl.ds(at + 4 * four + i, MINE, stride=LEVELS), :] for i in range(4)]
    return jnp.concatenate(rows, axis=0)


def slab_rows(ref, at, s):
    rows = [
        ref[pl.ds(f * WIDE * LEVELS + at + 2 * s + j, MINE, stride=LEVELS), :] for f in range(2) for j in range(2)
    ]
    return jnp.concatenate(rows, axis=0)


def first_kernel(state, near, far, sums, mixing, packed, both, ps, sides, spare):
    span = MINE * LEVELS
    edge = HALO * LEVELS
    pieces = []
    flip = my_place()[1]
    even = flip == 0
    for before, after in ((far, near), (near, far)):
        for m in range(8):
            lanes = pl.ds(128 * (m // 2), 128)
            line = jnp.where(even, before[:, lanes], after[:, lanes])
            spare[pl.ds(8 * m, 8), :] = line if m % 2 == 0 else pltpu.roll(line, 64, 1)
        pieces += [spare[pl.ds(c, 8, stride=8), :] for c in range(8)]
    halo = jnp.concatenate(pieces, axis=0).T
    lane = iota((LEVELS, 128), 1)
    for f in range(2):
        line = halo[f * LEVELS : (f + 1) * LEVELS, :]
        for c in range(HALO):
            inner = pltpu.roll(state[pl.ds(f * span + (MINE - HALO + c) * LEVELS, LEVELS), :], 8, 1)
            outer = pltpu.roll(line, (128 - 8 * c) % 128, 1)
            sides[pl.ds((2 * f) * edge + c * LEVELS, LEVELS), :] = jnp.where(lane < 8, outer, inner)
            inner = pltpu.roll(state[pl.ds(f * span + c * LEVELS, LEVELS), :], 120, 1)
            outer = pltpu.roll(line, (56 - 8 * c) % 128, 1)
            sides[pl.ds((2 * f + 1) * edge + c * LEVELS, LEVELS), :] = jnp.where(lane >= 120, outer, inner)

    def sources(f, c):
        if c < HALO:
            return sides, 2 * f * edge + c * LEVELS
        if c < HALO + MINE:
            return state, f * span + (c - HALO) * LEVELS
        return sides, (2 * f + 1) * edge + (c - HALO - MINE) * LEVELS

    substeps(sources, both, ps, mixing)
    starts = [jnp.bitwise_xor(MEMBER_AT[k], flip) * 136 for k in range(GROUP)]
    for s in range(GROUP):
        square = slab_rows(both, edge, s).T
        for k in range(GROUP):
            packed[pl.ds(starts[k] + 8 * s, 8), :] = square[8 * k : 8 * k + 8, :]
    for g in range(GROUP):
        packed[pl.ds(g * 136 + 128, 8), :] = sums[pl.ds(g * 8, 8), :]


def square_of(ref, s):
    return jnp.concatenate([ref[pl.ds(g * 136 + s * 8, 8), :] for g in range(GROUP)], axis=0)


def fold(top, bottom, vector, extra=0.0):
    row, lane = iota((64, 128), 0), iota((64, 128), 1)
    body = jnp.where((lane >= 64) | (row <= lane), top, pltpu.roll(bottom, 64, 1))
    diagonal = jnp.sum(jnp.where(lane == row + 64, bottom, 0.0), axis=0, keepdims=True)
    at = iota((8, 128), 0)
    tail = jnp.where(at == 0, diagonal, jnp.where(at == 1, vector, extra))
    return body, tail


def half_of(body, tail):
    row, lane = iota((64, 128), 0), iota((64, 128), 1)
    top = jnp.where((lane >= 64) | (row < lane), body, jnp.where(row == lane, 0.5 * body, 0.0))
    moved = pltpu.roll(body, 64, 1)
    bottom = jnp.where(row > lane - 64, moved, jnp.where(row == lane - 64, 0.5 * tail[0:1, :], 0.0))
    bottom = jnp.where(lane >= 64, bottom, 0.0)
    return jnp.concatenate([top, bottom], axis=0)


def blend(fs, table, core, keep, send):
    for j in range(GROUP // 2):
        for which, ref in ((core, keep), (1 - core, send)):
            s = 2 * j + which
            ref[j] = fs[s] + fs[table[s, 0]] + fs[table[s, 1]]


def gram_of(fs, q, anomaly, halves, mean, line, upper):
    lane = iota((1, 128), 1)
    swapped = pltpu.roll(line, 64, 1)
    mine = (lane >= 64) if upper else (lane < 64)
    weight = jnp.where(mine, swapped if upper else line, 0.0)
    pull = jnp.where(mine, line if upper else swapped, 0.0) - weight * mean
    left = jnp.concatenate([anomaly * weight, jnp.broadcast_to(pull, (8, 128))], axis=0)
    gram = dot_split(split(left), halves, turned=True)
    body, tail = fold(gram[:64], gram[64:128], gram[128:129])
    fs[q, pl.ds(0, 64), :] = body
    fs[q, pl.ds(64, 8), :] = tail


def centred(square):
    mean = jnp.mean(square, axis=0, keepdims=True)
    anomaly = square - mean
    return anomaly, split(anomaly), mean


def first_gram_kernel(got, keep, send, later, table_out, fs, table, sem):
    table_out[...] = got[pl.ds(130, GROUP, stride=136), :].astype(jnp.int32)
    copy = pltpu.make_async_copy(table_out, table, sem)
    copy.start()
    later[...] = got[pl.ds(129, GROUP, stride=136), :]
    for q in range(GROUP):
        gram_of(fs, q, *centred(square_of(got, q)), got[pl.ds(q * 136 + 128, 1), :], True)
    copy.wait()
    blend(fs, table, my_place()[0], keep, send)


def forecast_kernel(table_in, state, outer, inner, hist, mixing, both, keep, send, ps, fs, sides, table, sem):
    edge = HALO * LEVELS
    span = MINE * LEVELS
    copy = pltpu.make_async_copy(table_in, table, sem)
    copy.start()
    odd = (my_place()[2] & 1) == 1
    for f in range(2):
        rows = pl.ds(f * edge, edge)
        sides[pl.ds(2 * f * edge, edge), :] = jnp.where(odd, inner[rows, :], outer[rows, :])
        sides[pl.ds((2 * f + 1) * edge, edge), :] = jnp.where(odd, outer[rows, :], inner[rows, :])

    def sources(f, c):
        if c < HALO:
            return sides, 2 * f * edge + c * LEVELS
        if c < HALO + MINE:
            return state, f * span + (c - HALO) * LEVELS
        return sides, (2 * f + 1) * edge + (c - HALO - MINE) * LEVELS

    substeps(sources, both, ps, mixing)
    for four in range(8):
        parts = centred(four_levels(both, WIDE * LEVELS + edge, four).T)
        for half in range(2):
            q = 2 * four + half
            gram_of(fs, q, *parts, hist[pl.ds(q, 1), :], half == 1)
    copy.wait()
    blend(fs, table, my_place()[0], keep, send)


def root_kernel(got, out):
    total = got[0]
    for j in range(1, 8):
        total = total + got[j]
    half = half_of(total[:64], total[64:])
    gram, vector = half + half.T, total[65:66]
    eye = jnp.where(iota((WIDTH, WIDTH), 0) == iota((WIDTH, WIDTH), 1), 1.0, 0.0)
    third = 1.0 / 3.0
    blended = (WIDTH - 1.0) * eye + gram * third
    pull = vector * third
    squared = jnp.sum(jnp.sum(blended * blended, axis=0, keepdims=True), axis=1, keepdims=True)
    norm = jnp.sqrt(squared)
    a = blended / norm
    newton = 1.5 * eye - 0.5 * a
    a = dot_split(split(a), split(newton))
    z = newton
    for step in range(1, ROOT_STEPS):
        newton = 1.5 * eye - 0.5 * dot_split(split(z), split(a))
        if step < ROOT_STEPS - 1:
            both = dot_split(split(jnp.concatenate([a, z], axis=0)), split(newton))
            a, z = both[:WIDTH], both[WIDTH:]
        else:
            z = dot_split(split(z), split(newton))
    halves = split(z)
    wide = jnp.broadcast_to(pull, (8, WIDTH))
    inner = dot_split(split(wide), halves, turned=True)
    shift = dot_split(split(inner), halves, turned=True)[0:1, :] / norm
    spread = z * (math.sqrt(WIDTH - 1.0) / jnp.sqrt(norm))
    sums = jnp.sum(spread, axis=0, keepdims=True) + jnp.sum(shift, axis=1, keepdims=True)
    body, tail = fold(spread[:64], spread[64:], shift, (1.0 - sums) * (1.0 / WIDTH))
    for j in range(8):
        out[j, pl.ds(0, 64), :] = body
        out[j, pl.ds(64, 8), :] = tail


def weights_of(roots, j):
    body, tail = roots[j, pl.ds(0, 64), :], roots[j, pl.ds(64, 8), :]
    half = half_of(body, tail)
    return split((half + tail[1:2, :]) + (half + tail[2:3, :]).T)


def first_apply_kernel(second, got, roots, *refs):
    out = refs[1] if second else refs[0]
    span = MINE * LEVELS
    edge = HALO * LEVELS
    core, _, block = my_place()
    parity = 1 - core if second else core
    for j in range(8):
        s = 2 * j + parity
        square = jnp.concatenate(
            [got[pl.ds(pl.multiple_of(g * 136 + s * 8, 8), 8), :] for g in range(GROUP)], axis=0
        )
        result = dot_split(weights_of(roots, j), split(square)).T
        for fj in range(4):
            at = (fj // 2) * span + 2 * s + fj % 2
            out[pl.ds(at, MINE, stride=LEVELS), :] = result[fj * 32 : fj * 32 + 32, :]
    if second:
        outer, inner = refs[2:]
        odd = (block & 1) == 1
        for f in range(2):
            first = out[pl.ds(f * span, edge), :]
            final = out[pl.ds((f + 1) * span - edge, edge), :]
            outer[pl.ds(f * edge, edge), :] = jnp.where(odd, final, first)
            inner[pl.ds(f * edge, edge), :] = jnp.where(odd, first, final)


def last_apply_kernel(second, both, roots, *refs):
    out = refs[-1]
    core, _, block = my_place()
    parity = 1 - core if second else core
    starts = []
    for chunk in range(4):
        fj = (chunk + 16 - block) & 3
        starts.append((fj >> 1) * (WIDE * LEVELS) + (fj & 1) + HALO * LEVELS)
    for j in range(8):
        s = 2 * j + parity
        field = jnp.concatenate(
            [both[pl.ds(at + 2 * s, MINE, stride=LEVELS), :] for at in starts], axis=0
        )
        result = dot_split(weights_of(roots, j), split(field), turned=True)
        for g in range(GROUP):
            out[pl.ds(pl.multiple_of((g * GROUP + s) * 8, 8), 8), :] = result[g * 8 : g * 8 + 8, :]


def place_kernel(got, out, tiles):
    flip = my_place()[1]
    starts = [jnp.bitwise_xor(MEMBER_AT[k], flip) * 128 for k in range(GROUP)]
    lane = iota((16, 128), 1)
    for t in range(4):
        for n in range(8):
            rows = [got[pl.ds(starts[4 * t + p] + n, 16, stride=8), :] for p in range(4)]
            for fj in range(4):
                block = rows[(0 - fj) % 4]
                for chunk in range(1, 4):
                    block = jnp.where(lane >= 32 * chunk, rows[(chunk - fj) % 4], block)
                if fj > 0:
                    block = pltpu.roll(block, 128 - 32 * fj, 1)
                tiles[pl.ds(512 * t + (n * 2 + fj // 2) * LEVELS + fj % 2, 16, stride=2), :] = block
    for t in range(4):
        out[:, pl.ds(128 * t, 128)] = tiles[pl.ds(512 * t, 512), :]


def vmem():
    return pl.BlockSpec(memory_space=pltpu.VMEM)


def call(kernel, out, ins, name, scratch=(), aliases=None, cost=None):
    return pl.pallas_call(
        kernel,
        out_shape=out,
        in_specs=ins,
        out_specs=jax.tree.map(lambda _: vmem(), out),
        scratch_shapes=scratch,
        input_output_aliases=aliases or {},
        cost_estimate=cost,
        compiler_params=pltpu.CompilerParams(vmem_limit_bytes=VMEM_LIMIT),
        name=name,
    )


def arr(*shape, dtype=F32):
    return jax.ShapeDtypeStruct(shape, dtype)


def holder(block, hor):
    g = MEMBER_AT[block] ^ (15 * (hor & 1))
    return ((g >> 2) * 16 + hor) * 4 + (g & 3)


def block_pairs(start):
    pairs = []
    for hor in range(16):
        for block in range(start, GROUP, 2):
            after = block + 1
            pair = (holder(block, hor), holder(after % GROUP, (hor + after // GROUP) % 16))
            pairs += [pair, pair[::-1]]
    return pairs


def swap(x):
    return lax.ppermute(x, "core", [(0, 1), (1, 0)])


def exchange(x, axes):
    return lax.all_to_all(x, axes, split_axis=0, concat_axis=0, tiled=True)


def shards(ensemble, coupling, obs_column, obs_level, obs_value, obs_error, obs_live, partners):
    rows = MINE * LEVELS
    edges = 2 * HALO * LEVELS
    members = ensemble.reshape(512, COLS)
    near, far = call(edges_kernel, (arr(HALO, COLS), arr(HALO, COLS)), [vmem()], "edges")(members)
    far = lax.ppermute(far, "hor", [(i, (i - 1 + 2 * (i & 1)) % 16) for i in range(16)])
    near = lax.ppermute(near, "hor", [(i, i ^ 1) for i in range(16)])
    state, sums, mixing = call(
        prepare_kernel,
        (arr(2 * rows, 128), arr(128, 128), arr(2 * MIX, MIX, dtype=BF16)),
        [vmem()] * 8,
        "prepare",
        [pltpu.VMEM((2048, 128), F32), pltpu.VMEM((2048, 128), F32)],
    )(partners, members, obs_column, obs_level, obs_value, obs_error, obs_live, coupling)
    wide = pltpu.VMEM((WIDE * LEVELS, WIDTH), F32)
    fields = pltpu.VMEM((2 * WIDE * LEVELS, WIDTH), F32)
    packed = call(
        first_kernel,
        arr(GROUP * 136, 128),
        [vmem()] * 5,
        "first",
        [fields, wide, pltpu.VMEM((4 * HALO * LEVELS, 128), F32), pltpu.VMEM((64, 128), F32)],
    )(state, near, far, sums, mixing)
    received = exchange(packed.reshape(GROUP, 136, 128), TILE).reshape(GROUP * 136, 128)
    folded = pltpu.VMEM((GROUP, FOLD, 128), F32)
    scalars = pltpu.SMEM((GROUP, 128), jnp.int32)
    keep, send, hist, table = call(
        first_gram_kernel,
        (arr(8, FOLD, 128), arr(8, FOLD, 128), arr(GROUP, 128), arr(GROUP, 128, dtype=jnp.int32)),
        [vmem()],
        "gram",
        [folded, scalars, pltpu.SemaphoreType.DMA(())],
    )(received)

    def roots(keep, send):
        parts = exchange(keep + swap(send), CHIPS)
        copies = call(root_kernel, arr(8, FOLD, 128), [vmem()], "root")(parts)
        same = exchange(copies, CHIPS)
        return same, swap(same)

    cost = pl.CostEstimate(flops=10**9, bytes_accessed=3 * 2**20, transcendentals=0)
    same, other = roots(keep, send)
    part = call(
        functools.partial(first_apply_kernel, False),
        arr(2 * rows, WIDTH),
        [vmem()] * 2,
        "apply",
        cost=cost,
    )(received, same)
    state, outer, inner = call(
        functools.partial(first_apply_kernel, True),
        (arr(2 * rows, WIDTH),) + (arr(edges, WIDTH),) * 2,
        [vmem()] * 3,
        "apply",
        aliases={2: 0},
    )(received, other, part)
    outer = lax.ppermute(outer, ALL, block_pairs(1))
    inner = lax.ppermute(inner, ALL, block_pairs(0))
    both, keep, send = call(
        forecast_kernel,
        (arr(2 * WIDE * LEVELS, WIDTH), arr(8, FOLD, 128), arr(8, FOLD, 128)),
        [vmem()] * 6,
        "forecast",
        [wide, folded, pltpu.VMEM((4 * HALO * LEVELS, 128), F32), scalars, pltpu.SemaphoreType.DMA(())],
    )(table, state, outer, inner, hist, mixing)
    same, other = roots(keep, send)
    part = call(
        functools.partial(last_apply_kernel, False),
        arr(GROUP * 128, 128),
        [vmem()] * 2,
        "analyse",
        cost=cost,
    )(both, same)
    analysed = call(
        functools.partial(last_apply_kernel, True),
        arr(GROUP * 128, 128),
        [vmem()] * 3,
        "analyse",
        aliases={2: 0},
    )(both, other, part)
    got = exchange(analysed.reshape(GROUP, 128, 128), TILE).reshape(GROUP * 128, 128)
    placed = call(place_kernel, arr(512, 512), [vmem()], "place", [pltpu.VMEM((2048, 128), F32)])(got)
    return placed.reshape(ensemble.shape)


def solution(mesh):
    fine = Mesh(mesh.devices.reshape(4, 16, 2, 2), ALL)
    group = TILE
    in_specs = (
        P(group, None, None, "hor"),
        P(),
        P(None, group, "hor", None),
        P(None, group, "hor", None),
        P(None, group, "hor", None),
        P(None, group, "hor", None),
        P(None, group, "hor", None),
        P(group, "hor", None),
    )
    out_specs = P(group, None, None, "hor")
    return jax.shard_map(shards, mesh=fine, in_specs=in_specs, out_specs=out_specs, check_vma=False)
```

```python
import functools
import math

import jax
import jax.numpy as jnp
from jax import lax
from jax.experimental import pallas as pl
from jax.experimental.pallas import tpu as pltpu
from jax.sharding import Mesh, PartitionSpec as P

SUBSTEPS = 4
ROOT_STEPS = 8
RATE = 0.5 * 0.2
MIX = 128
GROUP = 16
WIDTH = 128
LEVELS = 32
COLS = 512
MINE = COLS // GROUP
HALO = 2 * SUBSTEPS
WIDE = MINE + 2 * HALO
FOLD = 72
F32 = jnp.float32
BF16 = jnp.bfloat16
VMEM_LIMIT = 48 * 1024 * 1024
ALL = ("mem", "hor", "zh", "core")
TILE = ("mem", "zh", "core")
CHIPS = ("mem", "zh")


def block_of(g):
    return ((g >> 1) & 1) * 8 + (g >> 2) * 2 + (g & 1)


MEMBER_AT = {block_of(g): g for g in range(GROUP)}


def my_place():
    core = lax.axis_index("core")
    flip = 15 * (lax.axis_index("hor") & 1)
    g = lax.axis_index("mem") * 4 + lax.axis_index("zh") * 2 + core
    return core, flip, block_of(jnp.bitwise_xor(g, flip))


def split(a):
    high = a.astype(BF16)
    return high, (a - high.astype(F32)).astype(BF16)


def dot_split(a, b, turned=False):
    left = jnp.concatenate([a[0], a[0], a[1]], axis=1)
    right = jnp.concatenate([b[0], b[1], b[0]], axis=1 if turned else 0)
    dims = (((1,), (1 if turned else 0,)), ((), ()))
    return lax.dot_general(left, right, dims, preferred_element_type=F32)


def iota(shape, dim):
    return lax.broadcasted_iota(jnp.int32, shape, dim)


def chunk_transpose(rows):
    lane = iota(rows[0].shape, 1)
    out = []
    for p in range(4):
        total = None
        for q in range(4):
            piece = rows[q] if p == q else pltpu.roll(rows[q], (32 * (q - p)) % 128, 1)
            total = piece if total is None else jnp.where(lane >= 32 * q, piece, total)
        out.append(total)
    return out


def edges_kernel(ens, near, far):
    first = ens[:, 0:128].T[0:HALO, :]
    last = ens[:, COLS - 128 : COLS].T[128 - HALO :, :]
    even = my_place()[1] == 0
    near[...] = jnp.where(even, last, first)
    far[...] = jnp.where(even, first, last)


def prepare_kernel(
    partner, ens, column, level, value, error, live, coupling, state, out, mixing, tiles, blocks
):
    for t in range(4):
        tiles[pl.ds(512 * t, 512), :] = ens[:, pl.ds(128 * t, 128)]
    for f in range(2):
        for t in range(4):
            for m in range(8):
                at = t * 512 + (m * 2 + f) * LEVELS
                rows = [tiles[pl.ds(at + i, 8, stride=4), :] for i in range(4)]
                for p, block in enumerate(chunk_transpose(rows)):
                    blocks[pl.ds(f * 1024 + (4 * t + p) * 8 + m, 8, stride=128), :] = block
        for four in range(8):
            turned = blocks[pl.ds(f * 1024 + four * 128, 128), :].T
            for i in range(4):
                at = f * MINE * LEVELS + 4 * four + i
                state[pl.ds(at, MINE, stride=LEVELS), :] = turned[32 * i : 32 * i + 32, :]
    member = jnp.bitwise_xor(iota((GROUP, COLS), 0), my_place()[1])
    place = ((member >> 1) & 1) * 8 + (member >> 2) * 2 + (member & 1)
    spot = iota((64, COLS), 0)
    zero = jnp.zeros((64, COLS), F32)
    for cycle in range(2):
        col = column[cycle, 0]
        weight = live[cycle, 0].astype(F32) / error[cycle, 0]
        weighted = weight * value[cycle, 0]
        here = (col >> 5) == place
        left = jnp.concatenate([jnp.where(here, weight, 0.0), jnp.where(here, weighted, 0.0)], axis=1)
        hit = jnp.where(level[cycle, 0] * 32 + (col & 31) == spot, 1.0, 0.0)
        right = jnp.concatenate(
            [jnp.concatenate([hit, zero], axis=1), jnp.concatenate([zero, hit], axis=1)], axis=0
        )
        sums = lax.dot_general(
            left, right, (((1,), (1,)), ((), ())), precision=lax.Precision.HIGHEST, preferred_element_type=F32
        )
        out[pl.ds(cycle, GROUP, stride=8), :] = sums
    lane = iota((GROUP, 128), 1)
    both = partner[0].astype(F32)
    out[pl.ds(2, GROUP, stride=8), :] = jnp.where(lane == 0, both[:, 0:1], both[:, 1:2])
    wide = jnp.concatenate([coupling[...]] * (MIX // LEVELS), axis=1)
    wide = jnp.concatenate([wide] * (MIX // LEVELS), axis=0)
    wide = jnp.where((iota((MIX, MIX), 0) >> 5) == (iota((MIX, MIX), 1) >> 5), RATE * RATE * wide, 0.0)
    high, rest = split(wide)
    mixing[pl.ds(0, MIX), :] = high
    mixing[pl.ds(MIX, MIX), :] = rest


def substeps(sources, both, ps, mixing):
    mix = (mixing[pl.ds(0, MIX), :], mixing[pl.ds(MIX, MIX), :])
    wide = WIDE * LEVELS
    for c in (0, WIDE - 2):
        both[pl.ds(wide + c * LEVELS, 2 * LEVELS), :] = jnp.zeros((2 * LEVELS, WIDTH), F32)

    def rows(step, f, c, count):
        if step == 0:
            ref, at = sources(f, c)
            return ref[pl.ds(at, count * LEVELS), :]
        return both[pl.ds(f * wide + c * LEVELS, count * LEVELS), :]

    def speed(step, c):
        return RATE * rows(0, 0, c, 1) if step == 0 else rows(step, 0, c, 1)

    many = MIX // LEVELS
    for step in range(SUBSTEPS):
        lo, hi = 2 * step, WIDE - 2 * step
        for c in range(0, WIDE, 2 * many):
            block = jnp.concatenate([rows(step, 1, c, many), rows(step, 1, c + many, many)], axis=1)
            pressure = dot_split(mix, split(block))
            ps[pl.ds(c * LEVELS, MIX), :] = pressure[:, :128]
            ps[pl.ds(c * LEVELS + MIX, MIX), :] = pressure[:, 128:]
        before, here = speed(step, lo), speed(step, lo + 1)
        slope_one, slope_two = ps[pl.ds(lo * LEVELS, LEVELS), :], ps[pl.ds((lo + 1) * LEVELS, LEVELS), :]
        flux_two, flux_one, height_one = None, None, None
        for c in range(lo + 1, hi - 1):
            after = speed(step, c + 1)
            slope = ps[pl.ds((c + 1) * LEVELS, LEVELS), :]
            moved = (here - here * (after - before)) - (slope - slope_one)
            height = rows(step, 1, c, 1)
            flux = moved * height
            if c >= lo + 3:
                both[pl.ds(wide + (c - 1) * LEVELS, LEVELS), :] = height_one - (flux - flux_two)
            both[pl.ds(c * LEVELS, LEVELS), :] = moved if step < SUBSTEPS - 1 else moved * (1.0 / RATE)
            before, here = here, after
            slope_one, slope_two = slope_two, slope
            flux_two, flux_one, height_one = flux_one, flux, height


def four_levels(ref, at, four):
    rows = [ref[pl.ds(at + 4 * four + i, MINE, stride=LEVELS), :] for i in range(4)]
    return jnp.concatenate(rows, axis=0)


def slab_rows(ref, at, s):
    rows = [
        ref[pl.ds(f * WIDE * LEVELS + at + 2 * s + j, MINE, stride=LEVELS), :] for f in range(2) for j in range(2)
    ]
    return jnp.concatenate(rows, axis=0)


def first_kernel(state, near, far, sums, mixing, packed, both, ps, sides, spare):
    span = MINE * LEVELS
    edge = HALO * LEVELS
    pieces = []
    flip = my_place()[1]
    even = flip == 0
    for before, after in ((far, near), (near, far)):
        for m in range(8):
            lanes = pl.ds(128 * (m // 2), 128)
            line = jnp.where(even, before[:, lanes], after[:, lanes])
            spare[pl.ds(8 * m, 8), :] = line if m % 2 == 0 else pltpu.roll(line, 64, 1)
        pieces += [spare[pl.ds(c, 8, stride=8), :] for c in range(8)]
    halo = jnp.concatenate(pieces, axis=0).T
    lane = iota((LEVELS, 128), 1)
    for f in range(2):
        line = halo[f * LEVELS : (f + 1) * LEVELS, :]
        for c in range(HALO):
            inner = pltpu.roll(state[pl.ds(f * span + (MINE - HALO + c) * LEVELS, LEVELS), :], 8, 1)
            outer = pltpu.roll(line, (128 - 8 * c) % 128, 1)
            sides[pl.ds((2 * f) * edge + c * LEVELS, LEVELS), :] = jnp.where(lane < 8, outer, inner)
            inner = pltpu.roll(state[pl.ds(f * span + c * LEVELS, LEVELS), :], 120, 1)
            outer = pltpu.roll(line, (56 - 8 * c) % 128, 1)
            sides[pl.ds((2 * f + 1) * edge + c * LEVELS, LEVELS), :] = jnp.where(lane >= 120, outer, inner)

    def sources(f, c):
        if c < HALO:
            return sides, 2 * f * edge + c * LEVELS
        if c < HALO + MINE:
            return state, f * span + (c - HALO) * LEVELS
        return sides, (2 * f + 1) * edge + (c - HALO - MINE) * LEVELS

    substeps(sources, both, ps, mixing)
    starts = [jnp.bitwise_xor(MEMBER_AT[k], flip) * 136 for k in range(GROUP)]
    for s in range(GROUP):
        square = slab_rows(both, edge, s).T
        for k in range(GROUP):
            packed[pl.ds(starts[k] + 8 * s, 8), :] = square[8 * k : 8 * k + 8, :]
    for g in range(GROUP):
        packed[pl.ds(g * 136 + 128, 8), :] = sums[pl.ds(g * 8, 8), :]


def square_of(ref, s):
    return jnp.concatenate([ref[pl.ds(g * 136 + s * 8, 8), :] for g in range(GROUP)], axis=0)


def fold(top, bottom, vector, extra=0.0):
    row, lane = iota((64, 128), 0), iota((64, 128), 1)
    body = jnp.where((lane >= 64) | (row <= lane), top, pltpu.roll(bottom, 64, 1))
    diagonal = jnp.sum(jnp.where(lane == row + 64, bottom, 0.0), axis=0, keepdims=True)
    at = iota((8, 128), 0)
    tail = jnp.where(at == 0, diagonal, jnp.where(at == 1, vector, extra))
    return body, tail


def half_of(body, tail):
    row, lane = iota((64, 128), 0), iota((64, 128), 1)
    top = jnp.where((lane >= 64) | (row < lane), body, jnp.where(row == lane, 0.5 * body, 0.0))
    moved = pltpu.roll(body, 64, 1)
    bottom = jnp.where(row > lane - 64, moved, jnp.where(row == lane - 64, 0.5 * tail[0:1, :], 0.0))
    bottom = jnp.where(lane >= 64, bottom, 0.0)
    return jnp.concatenate([top, bottom], axis=0)


def blend(fs, table, core, keep, send):
    for j in range(GROUP // 2):
        for which, ref in ((core, keep), (1 - core, send)):
            s = 2 * j + which
            ref[j] = fs[s] + fs[table[s, 0]] + fs[table[s, 1]]


def gram_of(fs, q, anomaly, halves, mean, line, upper):
    lane = iota((1, 128), 1)
    swapped = pltpu.roll(line, 64, 1)
    mine = (lane >= 64) if upper else (lane < 64)
    weight = jnp.where(mine, swapped if upper else line, 0.0)
    pull = jnp.where(mine, line if upper else swapped, 0.0) - weight * mean
    left = jnp.concatenate([anomaly * weight, jnp.broadcast_to(pull, (8, 128))], axis=0)
    gram = dot_split(split(left), halves, turned=True)
    body, tail = fold(gram[:64], gram[64:128], gram[128:129])
    fs[q, pl.ds(0, 64), :] = body
    fs[q, pl.ds(64, 8), :] = tail


def centred(square):
    mean = jnp.mean(square, axis=0, keepdims=True)
    anomaly = square - mean
    return anomaly, split(anomaly), mean


def first_gram_kernel(got, keep, send, later, table_out, fs, table, sem):
    table_out[...] = got[pl.ds(130, GROUP, stride=136), :].astype(jnp.int32)
    copy = pltpu.make_async_copy(table_out, table, sem)
    copy.start()
    later[...] = got[pl.ds(129, GROUP, stride=136), :]
    for q in range(GROUP):
        gram_of(fs, q, *centred(square_of(got, q)), got[pl.ds(q * 136 + 128, 1), :], True)
    copy.wait()
    blend(fs, table, my_place()[0], keep, send)


def forecast_kernel(table_in, state, outer, inner, hist, mixing, both, keep, send, ps, fs, sides, table, sem):
    edge = HALO * LEVELS
    span = MINE * LEVELS
    copy = pltpu.make_async_copy(table_in, table, sem)
    copy.start()
    odd = (my_place()[2] & 1) == 1
    for f in range(2):
        rows = pl.ds(f * edge, edge)
        sides[pl.ds(2 * f * edge, edge), :] = jnp.where(odd, inner[rows, :], outer[rows, :])
        sides[pl.ds((2 * f + 1) * edge, edge), :] = jnp.where(odd, outer[rows, :], inner[rows, :])

    def sources(f, c):
        if c < HALO:
            return sides, 2 * f * edge + c * LEVELS
        if c < HALO + MINE:
            return state, f * span + (c - HALO) * LEVELS
        return sides, (2 * f + 1) * edge + (c - HALO - MINE) * LEVELS

    substeps(sources, both, ps, mixing)
    for four in range(8):
        parts = centred(four_levels(both, WIDE * LEVELS + edge, four).T)
        for half in range(2):
            q = 2 * four + half
            gram_of(fs, q, *parts, hist[pl.ds(q, 1), :], half == 1)
    copy.wait()
    blend(fs, table, my_place()[0], keep, send)


def root_kernel(got, out):
    total = got[0]
    for j in range(1, 8):
        total = total + got[j]
    half = half_of(total[:64], total[64:])
    gram, vector = half + half.T, total[65:66]
    eye = jnp.where(iota((WIDTH, WIDTH), 0) == iota((WIDTH, WIDTH), 1), 1.0, 0.0)
    third = 1.0 / 3.0
    blended = (WIDTH - 1.0) * eye + gram * third
    pull = vector * third
    squared = jnp.sum(jnp.sum(blended * blended, axis=0, keepdims=True), axis=1, keepdims=True)
    norm = jnp.sqrt(squared)
    a = blended / norm
    newton = 1.5 * eye - 0.5 * a
    a = dot_split(split(a), split(newton))
    z = newton
    for step in range(1, ROOT_STEPS):
        newton = 1.5 * eye - 0.5 * dot_split(split(z), split(a))
        if step < ROOT_STEPS - 1:
            both = dot_split(split(jnp.concatenate([a, z], axis=0)), split(newton))
            a, z = both[:WIDTH], both[WIDTH:]
        else:
            z = dot_split(split(z), split(newton))
    halves = split(z)
    wide = jnp.broadcast_to(pull, (8, WIDTH))
    inner = dot_split(split(wide), halves, turned=True)
    shift = dot_split(split(inner), halves, turned=True)[0:1, :] / norm
    spread = z * (math.sqrt(WIDTH - 1.0) / jnp.sqrt(norm))
    sums = jnp.sum(spread, axis=0, keepdims=True) + jnp.sum(shift, axis=1, keepdims=True)
    body, tail = fold(spread[:64], spread[64:], shift, (1.0 - sums) * (1.0 / WIDTH))
    for j in range(8):
        out[j, pl.ds(0, 64), :] = body
        out[j, pl.ds(64, 8), :] = tail


def weights_of(roots, j):
    body, tail = roots[j, pl.ds(0, 64), :], roots[j, pl.ds(64, 8), :]
    half = half_of(body, tail)
    return split((half + tail[1:2, :]) + (half + tail[2:3, :]).T)


def first_apply_kernel(second, got, roots, *refs):
    out = refs[1] if second else refs[0]
    span = MINE * LEVELS
    edge = HALO * LEVELS
    core, _, block = my_place()
    parity = 1 - core if second else core
    for j in range(8):
        s = 2 * j + parity
        square = jnp.concatenate(
            [got[pl.ds(pl.multiple_of(g * 136 + s * 8, 8), 8), :] for g in range(GROUP)], axis=0
        )
        result = dot_split(weights_of(roots, j), split(square)).T
        for fj in range(4):
            at = (fj // 2) * span + 2 * s + fj % 2
            out[pl.ds(at, MINE, stride=LEVELS), :] = result[fj * 32 : fj * 32 + 32, :]
    if second:
        outer, inner = refs[2:]
        odd = (block & 1) == 1
        for f in range(2):
            first = out[pl.ds(f * span, edge), :]
            final = out[pl.ds((f + 1) * span - edge, edge), :]
            outer[pl.ds(f * edge, edge), :] = jnp.where(odd, final, first)
            inner[pl.ds(f * edge, edge), :] = jnp.where(odd, first, final)


def last_apply_kernel(second, both, roots, *refs):
    out = refs[-1]
    core, _, block = my_place()
    parity = 1 - core if second else core
    starts = []
    for chunk in range(4):
        fj = (chunk + 16 - block) & 3
        starts.append((fj >> 1) * (WIDE * LEVELS) + (fj & 1) + HALO * LEVELS)
    for j in range(8):
        s = 2 * j + parity
        field = jnp.concatenate(
            [both[pl.ds(at + 2 * s, MINE, stride=LEVELS), :] for at in starts], axis=0
        )
        result = dot_split(weights_of(roots, j), split(field), turned=True)
        for g in range(GROUP):
            out[pl.ds(pl.multiple_of((g * GROUP + s) * 8, 8), 8), :] = result[g * 8 : g * 8 + 8, :]


def place_kernel(got, out, tiles):
    flip = my_place()[1]
    starts = [jnp.bitwise_xor(MEMBER_AT[k], flip) * 128 for k in range(GROUP)]
    lane = iota((16, 128), 1)
    for t in range(4):
        for n in range(8):
            rows = [got[pl.ds(starts[4 * t + p] + n, 16, stride=8), :] for p in range(4)]
            for fj in range(4):
                block = rows[(0 - fj) % 4]
                for chunk in range(1, 4):
                    block = jnp.where(lane >= 32 * chunk, rows[(chunk - fj) % 4], block)
                if fj > 0:
                    block = pltpu.roll(block, 128 - 32 * fj, 1)
                tiles[pl.ds(512 * t + (n * 2 + fj // 2) * LEVELS + fj % 2, 16, stride=2), :] = block
    for t in range(4):
        out[:, pl.ds(128 * t, 128)] = tiles[pl.ds(512 * t, 512), :]


def vmem():
    return pl.BlockSpec(memory_space=pltpu.VMEM)


def call(kernel, out, ins, name, scratch=(), aliases=None, cost=None):
    return pl.pallas_call(
        kernel,
        out_shape=out,
        in_specs=ins,
        out_specs=jax.tree.map(lambda _: vmem(), out),
        scratch_shapes=scratch,
        input_output_aliases=aliases or {},
        cost_estimate=cost,
        compiler_params=pltpu.CompilerParams(vmem_limit_bytes=VMEM_LIMIT),
        name=name,
    )


def arr(*shape, dtype=F32):
    return jax.ShapeDtypeStruct(shape, dtype)


def holder(block, hor):
    g = MEMBER_AT[block] ^ (15 * (hor & 1))
    return ((g >> 2) * 16 + hor) * 4 + (g & 3)


def block_pairs(start):
    pairs = []
    for hor in range(16):
        for block in range(start, GROUP, 2):
            after = block + 1
            pair = (holder(block, hor), holder(after % GROUP, (hor + after // GROUP) % 16))
            pairs += [pair, pair[::-1]]
    return pairs


def swap(x):
    return lax.ppermute(x, "core", [(0, 1), (1, 0)])


def exchange(x, axes):
    return lax.all_to_all(x, axes, split_axis=0, concat_axis=0, tiled=True)


def shards(ensemble, coupling, obs_column, obs_level, obs_value, obs_error, obs_live, partners):
    rows = MINE * LEVELS
    edges = 2 * HALO * LEVELS
    members = ensemble.reshape(512, COLS)
    cost = pl.CostEstimate(flops=10**9, bytes_accessed=3 * 2**20, transcendentals=0)
    near, far = call(edges_kernel, (arr(HALO, COLS), arr(HALO, COLS)), [vmem()], "edges", cost=cost)(members)
    far = lax.ppermute(far, "hor", [(i, (i - 1 + 2 * (i & 1)) % 16) for i in range(16)])
    near = lax.ppermute(near, "hor", [(i, i ^ 1) for i in range(16)])
    state, sums, mixing = call(
        prepare_kernel,
        (arr(2 * rows, 128), arr(128, 128), arr(2 * MIX, MIX, dtype=BF16)),
        [vmem()] * 8,
        "prepare",
        [pltpu.VMEM((2048, 128), F32), pltpu.VMEM((2048, 128), F32)],
    )(partners, members, obs_column, obs_level, obs_value, obs_error, obs_live, coupling)
    wide = pltpu.VMEM((WIDE * LEVELS, WIDTH), F32)
    fields = pltpu.VMEM((2 * WIDE * LEVELS, WIDTH), F32)
    packed = call(
        first_kernel,
        arr(GROUP * 136, 128),
        [vmem()] * 5,
        "first",
        [fields, wide, pltpu.VMEM((4 * HALO * LEVELS, 128), F32), pltpu.VMEM((64, 128), F32)],
    )(state, near, far, sums, mixing)
    received = exchange(packed.reshape(GROUP, 136, 128), TILE).reshape(GROUP * 136, 128)
    folded = pltpu.VMEM((GROUP, FOLD, 128), F32)
    scalars = pltpu.SMEM((GROUP, 128), jnp.int32)
    keep, send, hist, table = call(
        first_gram_kernel,
        (arr(8, FOLD, 128), arr(8, FOLD, 128), arr(GROUP, 128), arr(GROUP, 128, dtype=jnp.int32)),
        [vmem()],
        "gram",
        [folded, scalars, pltpu.SemaphoreType.DMA(())],
    )(received)

    def roots(keep, send):
        parts = exchange(keep + swap(send), CHIPS)
        copies = call(root_kernel, arr(8, FOLD, 128), [vmem()], "root")(parts)
        same = exchange(copies, CHIPS)
        return same, swap(same)

    cost = pl.CostEstimate(flops=10**9, bytes_accessed=3 * 2**20, transcendentals=0)
    same, other = roots(keep, send)
    part = call(
        functools.partial(first_apply_kernel, False),
        arr(2 * rows, WIDTH),
        [vmem()] * 2,
        "apply",
        cost=cost,
    )(received, same)
    state, outer, inner = call(
        functools.partial(first_apply_kernel, True),
        (arr(2 * rows, WIDTH),) + (arr(edges, WIDTH),) * 2,
        [vmem()] * 3,
        "apply",
        aliases={2: 0},
    )(received, other, part)
    outer = lax.ppermute(outer, ALL, block_pairs(1))
    inner = lax.ppermute(inner, ALL, block_pairs(0))
    both, keep, send = call(
        forecast_kernel,
        (arr(2 * WIDE * LEVELS, WIDTH), arr(8, FOLD, 128), arr(8, FOLD, 128)),
        [vmem()] * 6,
        "forecast",
        [wide, folded, pltpu.VMEM((4 * HALO * LEVELS, 128), F32), scalars, pltpu.SemaphoreType.DMA(())],
    )(table, state, outer, inner, hist, mixing)
    same, other = roots(keep, send)
    part = call(
        functools.partial(last_apply_kernel, False),
        arr(GROUP * 128, 128),
        [vmem()] * 2,
        "analyse",
        cost=cost,
    )(both, same)
    analysed = call(
        functools.partial(last_apply_kernel, True),
        arr(GROUP * 128, 128),
        [vmem()] * 3,
        "analyse",
        aliases={2: 0},
    )(both, other, part)
    got = exchange(analysed.reshape(GROUP, 128, 128), TILE).reshape(GROUP * 128, 128)
    placed = call(place_kernel, arr(512, 512), [vmem()], "place", [pltpu.VMEM((2048, 128), F32)])(got)
    return placed.reshape(ensemble.shape)


def solution(mesh):
    fine = Mesh(mesh.devices.reshape(4, 16, 2, 2), ALL)
    group = TILE
    in_specs = (
        P(group, None, None, "hor"),
        P(),
        P(None, group, "hor", None),
        P(None, group, "hor", None),
        P(None, group, "hor", None),
        P(None, group, "hor", None),
        P(None, group, "hor", None),
        P(group, "hor", None),
    )
    out_specs = P(group, None, None, "hor")
    return jax.shard_map(shards, mesh=fine, in_specs=in_specs, out_specs=out_specs, check_vma=False)
```

```python
import functools
import math

import jax
import jax.numpy as jnp
from jax import lax
from jax.experimental import pallas as pl
from jax.experimental.pallas import tpu as pltpu
from jax.sharding import Mesh, PartitionSpec as P

SUBSTEPS = 4
ROOT_STEPS = 8
RATE = 0.5 * 0.2
MIX = 128
GROUP = 16
WIDTH = 128
LEVELS = 32
COLS = 512
MINE = COLS // GROUP
HALO = 2 * SUBSTEPS
WIDE = MINE + 2 * HALO
FINAL = (4 - 1) * 2 * WIDE * 32
FOLD = 72
F32 = jnp.float32
BF16 = jnp.bfloat16
VMEM_LIMIT = 16 * 1024 * 1024
ALL = ("mem", "hor", "zh", "core")
TILE = ("mem", "zh", "core")
CHIPS = ("mem", "zh")


def block_of(g):
    return ((g >> 1) & 1) * 8 + (g >> 2) * 2 + (g & 1)


MEMBER_AT = {block_of(g): g for g in range(GROUP)}


def my_place():
    core = lax.axis_index("core")
    flip = 15 * (lax.axis_index("hor") & 1)
    g = lax.axis_index("mem") * 4 + lax.axis_index("zh") * 2 + core
    return core, flip, block_of(jnp.bitwise_xor(g, flip))


def split(a):
    high = a.astype(BF16)
    return high, (a - high.astype(F32)).astype(BF16)


def dot_split(a, b, turned=False):
    left = jnp.concatenate([a[0], a[0], a[1]], axis=1)
    right = jnp.concatenate([b[0], b[1], b[0]], axis=1 if turned else 0)
    dims = (((1,), (1 if turned else 0,)), ((), ()))
    return lax.dot_general(left, right, dims, preferred_element_type=F32)


def iota(shape, dim):
    return lax.broadcasted_iota(jnp.int32, shape, dim)


def chunk_transpose(rows):
    lane = iota(rows[0].shape, 1)
    out = []
    for p in range(4):
        total = None
        for q in range(4):
            piece = rows[q] if p == q else pltpu.roll(rows[q], (32 * (q - p)) % 128, 1)
            total = piece if total is None else jnp.where(lane >= 32 * q, piece, total)
        out.append(total)
    return out


def edges_kernel(ens, near, far):
    first = ens[:, 0:128].T[0:HALO, :]
    last = ens[:, COLS - 128 : COLS].T[128 - HALO :, :]
    even = my_place()[1] == 0
    near[...] = jnp.where(even, last, first)
    far[...] = jnp.where(even, first, last)


def prepare_kernel(
    partner, ens, column, level, value, error, live, coupling, state, out, mixing, tiles, blocks
):
    for t in range(4):
        tiles[pl.ds(512 * t, 512), :] = ens[:, pl.ds(128 * t, 128)]
    for f in range(2):
        for t in range(4):
            for m in range(8):
                at = t * 512 + (m * 2 + f) * LEVELS
                rows = [tiles[pl.ds(at + i, 8, stride=4), :] for i in range(4)]
                for p, block in enumerate(chunk_transpose(rows)):
                    blocks[pl.ds(f * 1024 + (4 * t + p) * 8 + m, 8, stride=128), :] = block
        for four in range(8):
            turned = blocks[pl.ds(f * 1024 + four * 128, 128), :].T
            for i in range(4):
                at = f * MINE * LEVELS + 4 * four + i
                state[pl.ds(at, MINE, stride=LEVELS), :] = turned[32 * i : 32 * i + 32, :]
    member = jnp.bitwise_xor(iota((GROUP, COLS), 0), my_place()[1])
    place = ((member >> 1) & 1) * 8 + (member >> 2) * 2 + (member & 1)
    spot = iota((64, COLS), 0)
    zero = jnp.zeros((64, COLS), F32)
    for cycle in range(2):
        col = column[cycle, 0]
        weight = live[cycle, 0].astype(F32) / error[cycle, 0]
        weighted = weight * value[cycle, 0]
        here = (col >> 5) == place
        left = jnp.concatenate([jnp.where(here, weight, 0.0), jnp.where(here, weighted, 0.0)], axis=1)
        hit = jnp.where(level[cycle, 0] * 32 + (col & 31) == spot, 1.0, 0.0)
        right = jnp.concatenate(
            [jnp.concatenate([hit, zero], axis=1), jnp.concatenate([zero, hit], axis=1)], axis=0
        )
        sums = lax.dot_general(
            left, right, (((1,), (1,)), ((), ())), precision=lax.Precision.HIGHEST, preferred_element_type=F32
        )
        out[pl.ds(cycle, GROUP, stride=8), :] = sums
    lane = iota((GROUP, 128), 1)
    both = partner[0].astype(F32)
    out[pl.ds(2, GROUP, stride=8), :] = jnp.where(lane == 0, both[:, 0:1], both[:, 1:2])
    wide = jnp.concatenate([coupling[...]] * (MIX // LEVELS), axis=1)
    wide = jnp.concatenate([wide] * (MIX // LEVELS), axis=0)
    wide = jnp.where((iota((MIX, MIX), 0) >> 5) == (iota((MIX, MIX), 1) >> 5), RATE * RATE * wide, 0.0)
    high, rest = split(wide)
    mixing[pl.ds(0, MIX), :] = high
    mixing[pl.ds(MIX, MIX), :] = rest


def rows_after(sources, levels, step, f, c, count=1):
    if step == 0:
        ref, at = sources(f, c)
        return ref[pl.ds(at, count * LEVELS), :]
    return levels[pl.ds(((step - 1) * 2 + f) * WIDE * LEVELS + c * LEVELS, count * LEVELS), :]


def pressures(step, groups, sources, levels, ps, mixing):
    mix = (mixing[pl.ds(0, MIX), :], mixing[pl.ds(MIX, MIX), :])
    many = MIX // LEVELS
    for c in groups:
        block = jnp.concatenate(
            [rows_after(sources, levels, step - 1, 1, c, many), rows_after(sources, levels, step - 1, 1, c + many, many)],
            axis=1,
        )
        pressure = dot_split(mix, split(block))
        ps[pl.ds(c * LEVELS, MIX), :] = pressure[:, :128]
        ps[pl.ds(c * LEVELS + MIX, MIX), :] = pressure[:, 128:]


def sweep(step, start, stop, new, sources, levels, ps):
    last = step == SUBSTEPS

    def speed(at, c):
        value = rows_after(sources, levels, at, 0, c)
        return RATE * value if at in (0, SUBSTEPS) else value

    def slope(c):
        return ps[pl.ds(c * LEVELS, LEVELS), :]

    def put(f, c, value):
        levels[pl.ds(((step - 1) * 2 + f) * WIDE * LEVELS + c * LEVELS, LEVELS), :] = value

    flux_two, flux_one, height_one = None, None, None
    for c in range(start, stop):
        if new[0] <= c < new[1]:
            here = speed(step - 1, c)
            change = here * (speed(step - 1, c + 1) - speed(step - 1, c - 1))
            moved = (here - change) - (slope(c + 1) - slope(c - 1))
            put(0, c, moved * (1.0 / RATE) if last else moved)
        else:
            moved = speed(step, c)
        height = rows_after(sources, levels, step - 1, 1, c)
        flux = moved * height
        if c >= start + 2:
            put(1, c - 1, height_one - (flux - flux_two))
        flux_two, flux_one, height_one = flux_one, flux, height


def inner_kernel(state, mixing, levels, ps):
    span = MINE * LEVELS

    def sources(f, c):
        return state, f * span + (c - HALO) * LEVELS

    blank = jnp.zeros((LEVELS, 128), F32)
    for step in range(1, SUBSTEPS + 1):
        lo, hi = HALO + 2 * step, HALO + MINE - 2 * step
        if step < SUBSTEPS:
            for c in [*range(HALO, lo), *range(hi, HALO + MINE)]:
                levels[pl.ds(((step - 1) * 2 + 1) * WIDE * LEVELS + c * LEVELS, LEVELS), :] = blank
        pressures(step, range(HALO, HALO + MINE, 8), sources, levels, ps, mixing)
        sweep(step, lo - 1, hi + 1, (lo - 1, hi + 1), sources, levels, ps)


def outer_steps(sources, levels, ps, mixing):
    blank = jnp.zeros((LEVELS, 128), F32)
    for step in range(1, SUBSTEPS + 1):
        lo, hi = 2 * step, WIDE - 2 * step
        if step < SUBSTEPS:
            for c in [*range(lo), *range(hi, WIDE)]:
                levels[pl.ds(((step - 1) * 2 + 1) * WIDE * LEVELS + c * LEVELS, LEVELS), :] = blank
        pressures(step, (0, HALO, WIDE - 2 * HALO, WIDE - HALO), sources, levels, ps, mixing)
        sweep(step, lo - 1, lo + HALO + 1, (lo - 1, lo + HALO - 1), sources, levels, ps)
        sweep(step, hi - HALO - 1, hi + 1, (hi - HALO + 1, hi + 1), sources, levels, ps)


def four_levels(ref, at, four):
    rows = [ref[pl.ds(at + 4 * four + i, MINE, stride=LEVELS), :] for i in range(4)]
    return jnp.concatenate(rows, axis=0)


def slab_rows(ref, at, s):
    rows = [
        ref[pl.ds(f * WIDE * LEVELS + at + 2 * s + j, MINE, stride=LEVELS), :] for f in range(2) for j in range(2)
    ]
    return jnp.concatenate(rows, axis=0)


def first_kernel(levels_in, state, near, far, sums, mixing, packed, levels, ps, sides, spare):
    del levels_in
    span = MINE * LEVELS
    edge = HALO * LEVELS
    pieces = []
    flip = my_place()[1]
    even = flip == 0
    for before, after in ((far, near), (near, far)):
        for m in range(8):
            lanes = pl.ds(128 * (m // 2), 128)
            line = jnp.where(even, before[:, lanes], after[:, lanes])
            spare[pl.ds(8 * m, 8), :] = line if m % 2 == 0 else pltpu.roll(line, 64, 1)
        pieces += [spare[pl.ds(c, 8, stride=8), :] for c in range(8)]
    halo = jnp.concatenate(pieces, axis=0).T
    lane = iota((LEVELS, 128), 1)
    for f in range(2):
        line = halo[f * LEVELS : (f + 1) * LEVELS, :]
        for c in range(HALO):
            inner = pltpu.roll(state[pl.ds(f * span + (MINE - HALO + c) * LEVELS, LEVELS), :], 8, 1)
            outer = pltpu.roll(line, (128 - 8 * c) % 128, 1)
            sides[pl.ds((2 * f) * edge + c * LEVELS, LEVELS), :] = jnp.where(lane < 8, outer, inner)
            inner = pltpu.roll(state[pl.ds(f * span + c * LEVELS, LEVELS), :], 120, 1)
            outer = pltpu.roll(line, (56 - 8 * c) % 128, 1)
            sides[pl.ds((2 * f + 1) * edge + c * LEVELS, LEVELS), :] = jnp.where(lane >= 120, outer, inner)

    def sources(f, c):
        if c < HALO:
            return sides, 2 * f * edge + c * LEVELS
        if c < HALO + MINE:
            return state, f * span + (c - HALO) * LEVELS
        return sides, (2 * f + 1) * edge + (c - HALO - MINE) * LEVELS

    outer_steps(sources, levels, ps, mixing)
    starts = [jnp.bitwise_xor(MEMBER_AT[k], flip) * 136 for k in range(GROUP)]
    for s in range(GROUP):
        square = slab_rows(levels, FINAL + edge, s).T
        for k in range(GROUP):
            packed[pl.ds(starts[k] + 8 * s, 8), :] = square[8 * k : 8 * k + 8, :]
    for g in range(GROUP):
        packed[pl.ds(g * 136 + 128, 8), :] = sums[pl.ds(g * 8, 8), :]


def square_of(ref, s):
    return jnp.concatenate([ref[pl.ds(g * 136 + s * 8, 8), :] for g in range(GROUP)], axis=0)


def fold(top, bottom, vector, extra=0.0):
    row, lane = iota((64, 128), 0), iota((64, 128), 1)
    body = jnp.where((lane >= 64) | (row <= lane), top, pltpu.roll(bottom, 64, 1))
    diagonal = jnp.sum(jnp.where(lane == row + 64, bottom, 0.0), axis=0, keepdims=True)
    at = iota((8, 128), 0)
    tail = jnp.where(at == 0, diagonal, jnp.where(at == 1, vector, extra))
    return body, tail


def half_of(body, tail):
    row, lane = iota((64, 128), 0), iota((64, 128), 1)
    top = jnp.where((lane >= 64) | (row < lane), body, jnp.where(row == lane, 0.5 * body, 0.0))
    moved = pltpu.roll(body, 64, 1)
    bottom = jnp.where(row > lane - 64, moved, jnp.where(row == lane - 64, 0.5 * tail[0:1, :], 0.0))
    bottom = jnp.where(lane >= 64, bottom, 0.0)
    return jnp.concatenate([top, bottom], axis=0)


def blend(fs, table, core, keep, send):
    for j in range(GROUP // 2):
        for which, ref in ((core, keep), (1 - core, send)):
            s = 2 * j + which
            ref[j] = fs[s] + fs[table[s, 0]] + fs[table[s, 1]]


def gram_of(fs, q, anomaly, halves, mean, line, upper):
    lane = iota((1, 128), 1)
    swapped = pltpu.roll(line, 64, 1)
    mine = (lane >= 64) if upper else (lane < 64)
    weight = jnp.where(mine, swapped if upper else line, 0.0)
    pull = jnp.where(mine, line if upper else swapped, 0.0) - weight * mean
    left = jnp.concatenate([anomaly * weight, jnp.broadcast_to(pull, (8, 128))], axis=0)
    gram = dot_split(split(left), halves, turned=True)
    body, tail = fold(gram[:64], gram[64:128], gram[128:129])
    fs[q, pl.ds(0, 64), :] = body
    fs[q, pl.ds(64, 8), :] = tail


def centred(square):
    mean = jnp.mean(square, axis=0, keepdims=True)
    anomaly = square - mean
    return anomaly, split(anomaly), mean


def first_gram_kernel(got, keep, send, later, table_out, fs, table, sem):
    table_out[...] = got[pl.ds(130, GROUP, stride=136), :].astype(jnp.int32)
    copy = pltpu.make_async_copy(table_out, table, sem)
    copy.start()
    later[...] = got[pl.ds(129, GROUP, stride=136), :]
    for q in range(GROUP):
        gram_of(fs, q, *centred(square_of(got, q)), got[pl.ds(q * 136 + 128, 1), :], True)
    copy.wait()
    blend(fs, table, my_place()[0], keep, send)


def forecast_kernel(levels_in, table_in, state, outer, inner, hist, mixing, levels, keep, send, ps, fs, sides, table, sem):
    del levels_in
    edge = HALO * LEVELS
    span = MINE * LEVELS
    copy = pltpu.make_async_copy(table_in, table, sem)
    copy.start()
    odd = (my_place()[2] & 1) == 1
    for f in range(2):
        rows = pl.ds(f * edge, edge)
        sides[pl.ds(2 * f * edge, edge), :] = jnp.where(odd, inner[rows, :], outer[rows, :])
        sides[pl.ds((2 * f + 1) * edge, edge), :] = jnp.where(odd, outer[rows, :], inner[rows, :])

    def sources(f, c):
        if c < HALO:
            return sides, 2 * f * edge + c * LEVELS
        if c < HALO + MINE:
            return state, f * span + (c - HALO) * LEVELS
        return sides, (2 * f + 1) * edge + (c - HALO - MINE) * LEVELS

    outer_steps(sources, levels, ps, mixing)
    for four in range(8):
        parts = centred(four_levels(levels, FINAL + WIDE * LEVELS + edge, four).T)
        for half in range(2):
            q = 2 * four + half
            gram_of(fs, q, *parts, hist[pl.ds(q, 1), :], half == 1)
    copy.wait()
    blend(fs, table, my_place()[0], keep, send)


def root_kernel(got, out):
    total = got[0]
    for j in range(1, 8):
        total = total + got[j]
    half = half_of(total[:64], total[64:])
    gram, vector = half + half.T, total[65:66]
    eye = jnp.where(iota((WIDTH, WIDTH), 0) == iota((WIDTH, WIDTH), 1), 1.0, 0.0)
    third = 1.0 / 3.0
    blended = (WIDTH - 1.0) * eye + gram * third
    pull = vector * third
    squared = jnp.sum(jnp.sum(blended * blended, axis=0, keepdims=True), axis=1, keepdims=True)
    norm = jnp.sqrt(squared)
    a = blended / norm
    newton = 1.5 * eye - 0.5 * a
    a = dot_split(split(a), split(newton))
    z = newton
    for step in range(1, ROOT_STEPS):
        newton = 1.5 * eye - 0.5 * dot_split(split(z), split(a))
        if step < ROOT_STEPS - 1:
            both = dot_split(split(jnp.concatenate([a, z], axis=0)), split(newton))
            a, z = both[:WIDTH], both[WIDTH:]
        else:
            z = dot_split(split(z), split(newton))
    halves = split(z)
    wide = jnp.broadcast_to(pull, (8, WIDTH))
    inner = dot_split(split(wide), halves, turned=True)
    shift = dot_split(split(inner), halves, turned=True)[0:1, :] / norm
    spread = z * (math.sqrt(WIDTH - 1.0) / jnp.sqrt(norm))
    sums = jnp.sum(spread, axis=0, keepdims=True) + jnp.sum(shift, axis=1, keepdims=True)
    body, tail = fold(spread[:64], spread[64:], shift, (1.0 - sums) * (1.0 / WIDTH))
    for j in range(8):
        out[j, pl.ds(0, 64), :] = body
        out[j, pl.ds(64, 8), :] = tail


def weights_of(roots, j):
    body, tail = roots[j, pl.ds(0, 64), :], roots[j, pl.ds(64, 8), :]
    half = half_of(body, tail)
    return split((half + tail[1:2, :]) + (half + tail[2:3, :]).T)


def first_apply_kernel(second, got, roots, *refs):
    out = refs[1] if second else refs[0]
    span = MINE * LEVELS
    edge = HALO * LEVELS
    core, _, block = my_place()
    parity = 1 - core if second else core
    for j in range(8):
        s = 2 * j + parity
        square = jnp.concatenate(
            [got[pl.ds(pl.multiple_of(g * 136 + s * 8, 8), 8), :] for g in range(GROUP)], axis=0
        )
        result = dot_split(weights_of(roots, j), split(square)).T
        for fj in range(4):
            at = (fj // 2) * span + 2 * s + fj % 2
            out[pl.ds(at, MINE, stride=LEVELS), :] = result[fj * 32 : fj * 32 + 32, :]
    if second:
        outer, inner = refs[2:]
        odd = (block & 1) == 1
        for f in range(2):
            first = out[pl.ds(f * span, edge), :]
            final = out[pl.ds((f + 1) * span - edge, edge), :]
            outer[pl.ds(f * edge, edge), :] = jnp.where(odd, final, first)
            inner[pl.ds(f * edge, edge), :] = jnp.where(odd, first, final)


def last_apply_kernel(second, both, roots, *refs):
    out = refs[-1]
    core, _, block = my_place()
    parity = 1 - core if second else core
    starts = []
    for chunk in range(4):
        fj = (chunk + 16 - block) & 3
        starts.append((fj >> 1) * (WIDE * LEVELS) + (fj & 1) + (FINAL + HALO * LEVELS))
    for j in range(8):
        s = 2 * j + parity
        field = jnp.concatenate(
            [both[pl.ds(at + 2 * s, MINE, stride=LEVELS), :] for at in starts], axis=0
        )
        result = dot_split(weights_of(roots, j), split(field), turned=True)
        for g in range(GROUP):
            out[pl.ds(pl.multiple_of((g * GROUP + s) * 8, 8), 8), :] = result[g * 8 : g * 8 + 8, :]


def place_kernel(got, out, tiles):
    flip = my_place()[1]
    starts = [jnp.bitwise_xor(MEMBER_AT[k], flip) * 128 for k in range(GROUP)]
    lane = iota((16, 128), 1)
    for t in range(4):
        for n in range(8):
            rows = [got[pl.ds(starts[4 * t + p] + n, 16, stride=8), :] for p in range(4)]
            for fj in range(4):
                block = rows[(0 - fj) % 4]
                for chunk in range(1, 4):
                    block = jnp.where(lane >= 32 * chunk, rows[(chunk - fj) % 4], block)
                if fj > 0:
                    block = pltpu.roll(block, 128 - 32 * fj, 1)
                tiles[pl.ds(512 * t + (n * 2 + fj // 2) * LEVELS + fj % 2, 16, stride=2), :] = block
    for t in range(4):
        out[:, pl.ds(128 * t, 128)] = tiles[pl.ds(512 * t, 512), :]


def vmem():
    return pl.BlockSpec(memory_space=pltpu.VMEM)


def call(kernel, out, ins, name, scratch=(), aliases=None, cost=None):
    return pl.pallas_call(
        kernel,
        out_shape=out,
        in_specs=ins,
        out_specs=jax.tree.map(lambda _: vmem(), out),
        scratch_shapes=scratch,
        input_output_aliases=aliases or {},
        cost_estimate=cost,
        compiler_params=pltpu.CompilerParams(vmem_limit_bytes=VMEM_LIMIT),
        name=name,
    )


def arr(*shape, dtype=F32):
    return jax.ShapeDtypeStruct(shape, dtype)


def holder(block, hor):
    g = MEMBER_AT[block] ^ (15 * (hor & 1))
    return ((g >> 2) * 16 + hor) * 4 + (g & 3)


def block_pairs(start):
    pairs = []
    for hor in range(16):
        for block in range(start, GROUP, 2):
            after = block + 1
            pair = (holder(block, hor), holder(after % GROUP, (hor + after // GROUP) % 16))
            pairs += [pair, pair[::-1]]
    return pairs


def swap(x):
    return lax.ppermute(x, "core", [(0, 1), (1, 0)])


def exchange(x, axes):
    return lax.all_to_all(x, axes, split_axis=0, concat_axis=0, tiled=True)


def shards(ensemble, coupling, obs_column, obs_level, obs_value, obs_error, obs_live, partners):
    rows = MINE * LEVELS
    edges = 2 * HALO * LEVELS
    members = ensemble.reshape(512, COLS)
    early = pl.CostEstimate(flops=10**10, bytes_accessed=3 * 2**20, transcendentals=0)
    cost = pl.CostEstimate(flops=10**9, bytes_accessed=3 * 2**20, transcendentals=0)
    near, far = call(edges_kernel, (arr(HALO, COLS), arr(HALO, COLS)), [vmem()], "edges", cost=early)(members)
    far = lax.ppermute(far, "hor", [(i, (i - 1 + 2 * (i & 1)) % 16) for i in range(16)])
    near = lax.ppermute(near, "hor", [(i, i ^ 1) for i in range(16)])
    state, sums, mixing = call(
        prepare_kernel,
        (arr(2 * rows, 128), arr(128, 128), arr(2 * MIX, MIX, dtype=BF16)),
        [vmem()] * 8,
        "prepare",
        [pltpu.VMEM((2048, 128), F32), pltpu.VMEM((2048, 128), F32)],
    )(partners, members, obs_column, obs_level, obs_value, obs_error, obs_live, coupling)
    wide = pltpu.VMEM((WIDE * LEVELS, WIDTH), F32)
    all_levels = arr(SUBSTEPS * 2 * WIDE * LEVELS, WIDTH)
    inside = call(inner_kernel, all_levels, [vmem()] * 2, "inside", [wide], cost=cost)
    packed, _ = call(
        first_kernel,
        (arr(GROUP * 136, 128), all_levels),
        [vmem()] * 6,
        "first",
        [wide, pltpu.VMEM((4 * HALO * LEVELS, 128), F32), pltpu.VMEM((64, 128), F32)],
        aliases={0: 1},
    )(inside(state, mixing), state, near, far, sums, mixing)
    received = exchange(packed.reshape(GROUP, 136, 128), TILE).reshape(GROUP * 136, 128)
    folded = pltpu.VMEM((GROUP, FOLD, 128), F32)
    scalars = pltpu.SMEM((GROUP, 128), jnp.int32)
    keep, send, hist, table = call(
        first_gram_kernel,
        (arr(8, FOLD, 128), arr(8, FOLD, 128), arr(GROUP, 128), arr(GROUP, 128, dtype=jnp.int32)),
        [vmem()],
        "gram",
        [folded, scalars, pltpu.SemaphoreType.DMA(())],
    )(received)

    def roots(keep, send):
        parts = exchange(keep + swap(send), CHIPS)
        copies = call(root_kernel, arr(8, FOLD, 128), [vmem()], "root")(parts)
        same = exchange(copies, CHIPS)
        return same, swap(same)

    same, other = roots(keep, send)
    part = call(
        functools.partial(first_apply_kernel, False),
        arr(2 * rows, WIDTH),
        [vmem()] * 2,
        "apply",
        cost=cost,
    )(received, same)
    state, outer, inner = call(
        functools.partial(first_apply_kernel, True),
        (arr(2 * rows, WIDTH),) + (arr(edges, WIDTH),) * 2,
        [vmem()] * 3,
        "apply",
        aliases={2: 0},
    )(received, other, part)
    outer = lax.ppermute(outer, ALL, block_pairs(1))
    inner = lax.ppermute(inner, ALL, block_pairs(0))
    both, keep, send = call(
        forecast_kernel,
        (all_levels, arr(8, FOLD, 128), arr(8, FOLD, 128)),
        [vmem()] * 7,
        "forecast",
        [wide, folded, pltpu.VMEM((4 * HALO * LEVELS, 128), F32), scalars, pltpu.SemaphoreType.DMA(())],
        aliases={0: 0},
    )(inside(state, mixing), table, state, outer, inner, hist, mixing)
    same, other = roots(keep, send)
    part = call(
        functools.partial(last_apply_kernel, False),
        arr(GROUP * 128, 128),
        [vmem()] * 2,
        "analyse",
        cost=cost,
    )(both, same)
    analysed = call(
        functools.partial(last_apply_kernel, True),
        arr(GROUP * 128, 128),
        [vmem()] * 3,
        "analyse",
        aliases={2: 0},
    )(both, other, part)
    got = exchange(analysed.reshape(GROUP, 128, 128), TILE).reshape(GROUP * 128, 128)
    placed = call(place_kernel, arr(512, 512), [vmem()], "place", [pltpu.VMEM((2048, 128), F32)])(got)
    return placed.reshape(ensemble.shape)


def solution(mesh):
    fine = Mesh(mesh.devices.reshape(4, 16, 2, 2), ALL)
    group = TILE
    in_specs = (
        P(group, None, None, "hor"),
        P(),
        P(None, group, "hor", None),
        P(None, group, "hor", None),
        P(None, group, "hor", None),
        P(None, group, "hor", None),
        P(None, group, "hor", None),
        P(group, "hor", None),
    )
    out_specs = P(group, None, None, "hor")
    return jax.shard_map(shards, mesh=fine, in_specs=in_specs, out_specs=out_specs, check_vma=False)
```

```python
import functools
import math

import jax
import jax.numpy as jnp
from jax import lax
from jax.experimental import pallas as pl
from jax.experimental.pallas import tpu as pltpu
from jax.sharding import Mesh, PartitionSpec as P

SUBSTEPS = 4
ROOT_STEPS = 8
RATE = 0.5 * 0.2
MIX = 128
GROUP = 16
WIDTH = 128
LEVELS = 32
COLS = 512
MINE = COLS // GROUP
HALO = 2 * SUBSTEPS
WIDE = MINE + 2 * HALO
FINAL = (4 - 1) * 2 * WIDE * 32
FOLD = 72
F32 = jnp.float32
BF16 = jnp.bfloat16
VMEM_LIMIT = 16 * 1024 * 1024
ALL = ("mem", "hor", "zh", "core")
TILE = ("mem", "zh", "core")
CHIPS = ("mem", "zh")


def block_of(g):
    return ((g >> 1) & 1) * 8 + (g >> 2) * 2 + (g & 1)


MEMBER_AT = {block_of(g): g for g in range(GROUP)}


def my_place():
    core = lax.axis_index("core")
    flip = 15 * (lax.axis_index("hor") & 1)
    g = lax.axis_index("mem") * 4 + lax.axis_index("zh") * 2 + core
    return core, flip, block_of(jnp.bitwise_xor(g, flip))


def split(a):
    high = a.astype(BF16)
    return high, (a - high.astype(F32)).astype(BF16)


def dot_split(a, b, turned=False):
    left = jnp.concatenate([a[0], a[0], a[1]], axis=1)
    right = jnp.concatenate([b[0], b[1], b[0]], axis=1 if turned else 0)
    dims = (((1,), (1 if turned else 0,)), ((), ()))
    return lax.dot_general(left, right, dims, preferred_element_type=F32)


def iota(shape, dim):
    return lax.broadcasted_iota(jnp.int32, shape, dim)


def chunk_transpose(rows):
    lane = iota(rows[0].shape, 1)
    out = []
    for p in range(4):
        total = None
        for q in range(4):
            piece = rows[q] if p == q else pltpu.roll(rows[q], (32 * (q - p)) % 128, 1)
            total = piece if total is None else jnp.where(lane >= 32 * q, piece, total)
        out.append(total)
    return out


def edges_kernel(ens, near, far):
    first = ens[:, 0:128].T[0:HALO, :]
    last = ens[:, COLS - 128 : COLS].T[128 - HALO :, :]
    even = my_place()[1] == 0
    near[...] = jnp.where(even, last, first)
    far[...] = jnp.where(even, first, last)


def prepare_kernel(
    partner, ens, column, level, value, error, live, coupling, state, out, mixing, tiles, blocks
):
    for t in range(4):
        tiles[pl.ds(512 * t, 512), :] = ens[:, pl.ds(128 * t, 128)]
    for f in range(2):
        for t in range(4):
            for m in range(8):
                at = t * 512 + (m * 2 + f) * LEVELS
                rows = [tiles[pl.ds(at + i, 8, stride=4), :] for i in range(4)]
                for p, block in enumerate(chunk_transpose(rows)):
                    blocks[pl.ds(f * 1024 + (4 * t + p) * 8 + m, 8, stride=128), :] = block
        for four in range(8):
            turned = blocks[pl.ds(f * 1024 + four * 128, 128), :].T
            for i in range(4):
                at = f * MINE * LEVELS + 4 * four + i
                state[pl.ds(at, MINE, stride=LEVELS), :] = turned[32 * i : 32 * i + 32, :]
    member = jnp.bitwise_xor(iota((GROUP, COLS), 0), my_place()[1])
    place = ((member >> 1) & 1) * 8 + (member >> 2) * 2 + (member & 1)
    spot = iota((64, COLS), 0)
    zero = jnp.zeros((64, COLS), F32)
    for cycle in range(2):
        col = column[cycle, 0]
        weight = live[cycle, 0].astype(F32) / error[cycle, 0]
        weighted = weight * value[cycle, 0]
        here = (col >> 5) == place
        left = jnp.concatenate([jnp.where(here, weight, 0.0), jnp.where(here, weighted, 0.0)], axis=1)
        hit = jnp.where(level[cycle, 0] * 32 + (col & 31) == spot, 1.0, 0.0)
        right = jnp.concatenate(
            [jnp.concatenate([hit, zero], axis=1), jnp.concatenate([zero, hit], axis=1)], axis=0
        )
        sums = lax.dot_general(
            left, right, (((1,), (1,)), ((), ())), precision=lax.Precision.HIGHEST, preferred_element_type=F32
        )
        out[pl.ds(cycle, GROUP, stride=8), :] = sums
    lane = iota((GROUP, 128), 1)
    both = partner[0].astype(F32)
    out[pl.ds(2, GROUP, stride=8), :] = jnp.where(lane == 0, both[:, 0:1], both[:, 1:2])
    wide = jnp.concatenate([coupling[...]] * (MIX // LEVELS), axis=1)
    wide = jnp.concatenate([wide] * (MIX // LEVELS), axis=0)
    wide = jnp.where((iota((MIX, MIX), 0) >> 5) == (iota((MIX, MIX), 1) >> 5), RATE * RATE * wide, 0.0)
    high, rest = split(wide)
    mixing[pl.ds(0, MIX), :] = high
    mixing[pl.ds(MIX, MIX), :] = rest


def rows_after(sources, levels, step, f, c, count=1):
    if step == 0:
        ref, at = sources(f, c)
        return ref[pl.ds(at, count * LEVELS), :]
    return levels[pl.ds(((step - 1) * 2 + f) * WIDE * LEVELS + c * LEVELS, count * LEVELS), :]


def pressures(step, groups, sources, levels, ps, mixing):
    mix = (mixing[pl.ds(0, MIX), :], mixing[pl.ds(MIX, MIX), :])
    many = MIX // LEVELS
    for c in groups:
        block = jnp.concatenate(
            [rows_after(sources, levels, step - 1, 1, c, many), rows_after(sources, levels, step - 1, 1, c + many, many)],
            axis=1,
        )
        pressure = dot_split(mix, split(block))
        ps[pl.ds(c * LEVELS, MIX), :] = pressure[:, :128]
        ps[pl.ds(c * LEVELS + MIX, MIX), :] = pressure[:, 128:]


def sweep(step, start, stop, new, sources, levels, ps):
    last = step == SUBSTEPS

    def speed(at, c):
        value = rows_after(sources, levels, at, 0, c)
        return RATE * value if at in (0, SUBSTEPS) else value

    def slope(c):
        return ps[pl.ds(c * LEVELS, LEVELS), :]

    def put(f, c, value):
        levels[pl.ds(((step - 1) * 2 + f) * WIDE * LEVELS + c * LEVELS, LEVELS), :] = value

    flux_two, flux_one, height_one = None, None, None
    for c in range(start, stop):
        if new[0] <= c < new[1]:
            here = speed(step - 1, c)
            change = here * (speed(step - 1, c + 1) - speed(step - 1, c - 1))
            moved = (here - change) - (slope(c + 1) - slope(c - 1))
            put(0, c, moved * (1.0 / RATE) if last else moved)
        else:
            moved = speed(step, c)
        height = rows_after(sources, levels, step - 1, 1, c)
        flux = moved * height
        if c >= start + 2:
            put(1, c - 1, height_one - (flux - flux_two))
        flux_two, flux_one, height_one = flux_one, flux, height


def inner_kernel(state, mixing, levels, ps):
    span = MINE * LEVELS

    def sources(f, c):
        return state, f * span + (c - HALO) * LEVELS

    blank = jnp.zeros((LEVELS, 128), F32)
    for step in range(1, SUBSTEPS + 1):
        lo, hi = HALO + 2 * step, HALO + MINE - 2 * step
        if step < SUBSTEPS:
            for c in [*range(HALO, lo), *range(hi, HALO + MINE)]:
                levels[pl.ds(((step - 1) * 2 + 1) * WIDE * LEVELS + c * LEVELS, LEVELS), :] = blank
        pressures(step, range(HALO, HALO + MINE, 8), sources, levels, ps, mixing)
        sweep(step, lo - 1, hi + 1, (lo - 1, hi + 1), sources, levels, ps)


def outer_steps(sources, levels, ps, mixing):
    blank = jnp.zeros((LEVELS, 128), F32)
    for step in range(1, SUBSTEPS + 1):
        lo, hi = 2 * step, WIDE - 2 * step
        if step < SUBSTEPS:
            for c in [*range(lo), *range(hi, WIDE)]:
                levels[pl.ds(((step - 1) * 2 + 1) * WIDE * LEVELS + c * LEVELS, LEVELS), :] = blank
        pressures(step, (0, HALO, WIDE - 2 * HALO, WIDE - HALO), sources, levels, ps, mixing)
        sweep(step, lo - 1, lo + HALO + 1, (lo - 1, lo + HALO - 1), sources, levels, ps)
        sweep(step, hi - HALO - 1, hi + 1, (hi - HALO + 1, hi + 1), sources, levels, ps)


def four_levels(ref, at, four):
    rows = [ref[pl.ds(at + 4 * four + i, MINE, stride=LEVELS), :] for i in range(4)]
    return jnp.concatenate(rows, axis=0)


def slab_rows(ref, at, s):
    rows = [
        ref[pl.ds(f * WIDE * LEVELS + at + 2 * s + j, MINE, stride=LEVELS), :] for f in range(2) for j in range(2)
    ]
    return jnp.concatenate(rows, axis=0)


def first_kernel(levels_in, far, near, state, sums, mixing, packed, levels, ps, sides, spare):
    del levels_in
    span = MINE * LEVELS
    edge = HALO * LEVELS
    pieces = []
    flip = my_place()[1]
    even = flip == 0
    for before, after in ((far, near), (near, far)):
        for m in range(8):
            lanes = pl.ds(128 * (m // 2), 128)
            line = jnp.where(even, before[:, lanes], after[:, lanes])
            spare[pl.ds(8 * m, 8), :] = line if m % 2 == 0 else pltpu.roll(line, 64, 1)
        pieces += [spare[pl.ds(c, 8, stride=8), :] for c in range(8)]
    halo = jnp.concatenate(pieces, axis=0).T
    lane = iota((LEVELS, 128), 1)
    for f in range(2):
        line = halo[f * LEVELS : (f + 1) * LEVELS, :]
        for c in range(HALO):
            inner = pltpu.roll(state[pl.ds(f * span + (MINE - HALO + c) * LEVELS, LEVELS), :], 8, 1)
            outer = pltpu.roll(line, (128 - 8 * c) % 128, 1)
            sides[pl.ds((2 * f) * edge + c * LEVELS, LEVELS), :] = jnp.where(lane < 8, outer, inner)
            inner = pltpu.roll(state[pl.ds(f * span + c * LEVELS, LEVELS), :], 120, 1)
            outer = pltpu.roll(line, (56 - 8 * c) % 128, 1)
            sides[pl.ds((2 * f + 1) * edge + c * LEVELS, LEVELS), :] = jnp.where(lane >= 120, outer, inner)

    def sources(f, c):
        if c < HALO:
            return sides, 2 * f * edge + c * LEVELS
        if c < HALO + MINE:
            return state, f * span + (c - HALO) * LEVELS
        return sides, (2 * f + 1) * edge + (c - HALO - MINE) * LEVELS

    outer_steps(sources, levels, ps, mixing)
    starts = [jnp.bitwise_xor(MEMBER_AT[k], flip) * 136 for k in range(GROUP)]
    for s in range(GROUP):
        square = slab_rows(levels, FINAL + edge, s).T
        for k in range(GROUP):
            packed[pl.ds(starts[k] + 8 * s, 8), :] = square[8 * k : 8 * k + 8, :]
    for g in range(GROUP):
        packed[pl.ds(g * 136 + 128, 8), :] = sums[pl.ds(g * 8, 8), :]


def square_of(ref, s):
    return jnp.concatenate([ref[pl.ds(g * 136 + s * 8, 8), :] for g in range(GROUP)], axis=0)


def fold(top, bottom, vector, extra=0.0):
    row, lane = iota((64, 128), 0), iota((64, 128), 1)
    body = jnp.where((lane >= 64) | (row <= lane), top, pltpu.roll(bottom, 64, 1))
    diagonal = jnp.sum(jnp.where(lane == row + 64, bottom, 0.0), axis=0, keepdims=True)
    at = iota((8, 128), 0)
    tail = jnp.where(at == 0, diagonal, jnp.where(at == 1, vector, extra))
    return body, tail


def half_of(body, tail):
    row, lane = iota((64, 128), 0), iota((64, 128), 1)
    top = jnp.where((lane >= 64) | (row < lane), body, jnp.where(row == lane, 0.5 * body, 0.0))
    moved = pltpu.roll(body, 64, 1)
    bottom = jnp.where(row > lane - 64, moved, jnp.where(row == lane - 64, 0.5 * tail[0:1, :], 0.0))
    bottom = jnp.where(lane >= 64, bottom, 0.0)
    return jnp.concatenate([top, bottom], axis=0)


def blend(fs, table, core, keep, send):
    for j in range(GROUP // 2):
        for which, ref in ((core, keep), (1 - core, send)):
            s = 2 * j + which
            ref[j] = fs[s] + fs[table[s, 0]] + fs[table[s, 1]]


def gram_of(fs, q, anomaly, halves, mean, line, upper):
    lane = iota((1, 128), 1)
    swapped = pltpu.roll(line, 64, 1)
    mine = (lane >= 64) if upper else (lane < 64)
    weight = jnp.where(mine, swapped if upper else line, 0.0)
    pull = jnp.where(mine, line if upper else swapped, 0.0) - weight * mean
    left = jnp.concatenate([anomaly * weight, jnp.broadcast_to(pull, (8, 128))], axis=0)
    gram = dot_split(split(left), halves, turned=True)
    body, tail = fold(gram[:64], gram[64:128], gram[128:129])
    fs[q, pl.ds(0, 64), :] = body
    fs[q, pl.ds(64, 8), :] = tail


def centred(square):
    mean = jnp.mean(square, axis=0, keepdims=True)
    anomaly = square - mean
    return anomaly, split(anomaly), mean


def first_gram_kernel(got, keep, send, later, table_out, fs, table, sem):
    table_out[...] = got[pl.ds(130, GROUP, stride=136), :].astype(jnp.int32)
    copy = pltpu.make_async_copy(table_out, table, sem)
    copy.start()
    later[...] = got[pl.ds(129, GROUP, stride=136), :]
    for q in range(GROUP):
        gram_of(fs, q, *centred(square_of(got, q)), got[pl.ds(q * 136 + 128, 1), :], True)
    copy.wait()
    blend(fs, table, my_place()[0], keep, send)


def forecast_kernel(levels_in, table_in, state, outer, inner, hist, mixing, levels, keep, send, ps, fs, sides, table, sem):
    del levels_in
    edge = HALO * LEVELS
    span = MINE * LEVELS
    copy = pltpu.make_async_copy(table_in, table, sem)
    copy.start()
    odd = (my_place()[2] & 1) == 1
    for f in range(2):
        rows = pl.ds(f * edge, edge)
        sides[pl.ds(2 * f * edge, edge), :] = jnp.where(odd, inner[rows, :], outer[rows, :])
        sides[pl.ds((2 * f + 1) * edge, edge), :] = jnp.where(odd, outer[rows, :], inner[rows, :])

    def sources(f, c):
        if c < HALO:
            return sides, 2 * f * edge + c * LEVELS
        if c < HALO + MINE:
            return state, f * span + (c - HALO) * LEVELS
        return sides, (2 * f + 1) * edge + (c - HALO - MINE) * LEVELS

    outer_steps(sources, levels, ps, mixing)
    for four in range(8):
        parts = centred(four_levels(levels, FINAL + WIDE * LEVELS + edge, four).T)
        for half in range(2):
            q = 2 * four + half
            gram_of(fs, q, *parts, hist[pl.ds(q, 1), :], half == 1)
    copy.wait()
    blend(fs, table, my_place()[0], keep, send)


def root_kernel(got, out):
    total = got[0]
    for j in range(1, 8):
        total = total + got[j]
    half = half_of(total[:64], total[64:])
    gram, vector = half + half.T, total[65:66]
    eye = jnp.where(iota((WIDTH, WIDTH), 0) == iota((WIDTH, WIDTH), 1), 1.0, 0.0)
    third = 1.0 / 3.0
    blended = (WIDTH - 1.0) * eye + gram * third
    pull = vector * third
    squared = jnp.sum(jnp.sum(blended * blended, axis=0, keepdims=True), axis=1, keepdims=True)
    norm = jnp.sqrt(squared)
    a = blended / norm
    newton = 1.5 * eye - 0.5 * a
    a = dot_split(split(a), split(newton))
    z = newton
    for step in range(1, ROOT_STEPS):
        newton = 1.5 * eye - 0.5 * dot_split(split(z), split(a))
        if step < ROOT_STEPS - 1:
            both = dot_split(split(jnp.concatenate([a, z], axis=0)), split(newton))
            a, z = both[:WIDTH], both[WIDTH:]
        else:
            z = dot_split(split(z), split(newton))
    halves = split(z)
    wide = jnp.broadcast_to(pull, (8, WIDTH))
    inner = dot_split(split(wide), halves, turned=True)
    shift = dot_split(split(inner), halves, turned=True)[0:1, :] / norm
    spread = z * (math.sqrt(WIDTH - 1.0) / jnp.sqrt(norm))
    sums = jnp.sum(spread, axis=0, keepdims=True) + jnp.sum(shift, axis=1, keepdims=True)
    body, tail = fold(spread[:64], spread[64:], shift, (1.0 - sums) * (1.0 / WIDTH))
    for j in range(8):
        out[j, pl.ds(0, 64), :] = body
        out[j, pl.ds(64, 8), :] = tail


def weights_of(roots, j):
    body, tail = roots[j, pl.ds(0, 64), :], roots[j, pl.ds(64, 8), :]
    half = half_of(body, tail)
    return split((half + tail[1:2, :]) + (half + tail[2:3, :]).T)


def first_apply_kernel(second, got, roots, *refs):
    out = refs[1] if second else refs[0]
    span = MINE * LEVELS
    edge = HALO * LEVELS
    core, _, block = my_place()
    parity = 1 - core if second else core
    for j in range(8):
        s = 2 * j + parity
        square = jnp.concatenate(
            [got[pl.ds(pl.multiple_of(g * 136 + s * 8, 8), 8), :] for g in range(GROUP)], axis=0
        )
        result = dot_split(weights_of(roots, j), split(square)).T
        for fj in range(4):
            at = (fj // 2) * span + 2 * s + fj % 2
            out[pl.ds(at, MINE, stride=LEVELS), :] = result[fj * 32 : fj * 32 + 32, :]
    if second:
        outer, inner = refs[2:]
        odd = (block & 1) == 1
        for f in range(2):
            first = out[pl.ds(f * span, edge), :]
            final = out[pl.ds((f + 1) * span - edge, edge), :]
            outer[pl.ds(f * edge, edge), :] = jnp.where(odd, final, first)
            inner[pl.ds(f * edge, edge), :] = jnp.where(odd, first, final)


def last_apply_kernel(second, both, roots, *refs):
    out = refs[-1]
    core, _, block = my_place()
    parity = 1 - core if second else core
    starts = []
    for chunk in range(4):
        fj = (chunk + 16 - block) & 3
        starts.append((fj >> 1) * (WIDE * LEVELS) + (fj & 1) + (FINAL + HALO * LEVELS))
    for j in range(8):
        s = 2 * j + parity
        field = jnp.concatenate(
            [both[pl.ds(at + 2 * s, MINE, stride=LEVELS), :] for at in starts], axis=0
        )
        result = dot_split(weights_of(roots, j), split(field), turned=True)
        for g in range(GROUP):
            out[pl.ds(pl.multiple_of((g * GROUP + s) * 8, 8), 8), :] = result[g * 8 : g * 8 + 8, :]


def place_kernel(got, out, tiles):
    flip = my_place()[1]
    starts = [jnp.bitwise_xor(MEMBER_AT[k], flip) * 128 for k in range(GROUP)]
    lane = iota((16, 128), 1)
    for t in range(4):
        for n in range(8):
            rows = [got[pl.ds(starts[4 * t + p] + n, 16, stride=8), :] for p in range(4)]
            for fj in range(4):
                block = rows[(0 - fj) % 4]
                for chunk in range(1, 4):
                    block = jnp.where(lane >= 32 * chunk, rows[(chunk - fj) % 4], block)
                if fj > 0:
                    block = pltpu.roll(block, 128 - 32 * fj, 1)
                tiles[pl.ds(512 * t + (n * 2 + fj // 2) * LEVELS + fj % 2, 16, stride=2), :] = block
    for t in range(4):
        out[:, pl.ds(128 * t, 128)] = tiles[pl.ds(512 * t, 512), :]


def vmem():
    return pl.BlockSpec(memory_space=pltpu.VMEM)


def call(kernel, out, ins, name, scratch=(), aliases=None, cost=None):
    return pl.pallas_call(
        kernel,
        out_shape=out,
        in_specs=ins,
        out_specs=jax.tree.map(lambda _: vmem(), out),
        scratch_shapes=scratch,
        input_output_aliases=aliases or {},
        cost_estimate=cost,
        compiler_params=pltpu.CompilerParams(vmem_limit_bytes=VMEM_LIMIT),
        name=name,
    )


def arr(*shape, dtype=F32):
    return jax.ShapeDtypeStruct(shape, dtype)


def holder(block, hor):
    g = MEMBER_AT[block] ^ (15 * (hor & 1))
    return ((g >> 2) * 16 + hor) * 4 + (g & 3)


def block_pairs(start):
    pairs = []
    for hor in range(16):
        for block in range(start, GROUP, 2):
            after = block + 1
            pair = (holder(block, hor), holder(after % GROUP, (hor + after // GROUP) % 16))
            pairs += [pair, pair[::-1]]
    return pairs


def swap(x):
    return lax.ppermute(x, "core", [(0, 1), (1, 0)])


def exchange(x, axes):
    return lax.all_to_all(x, axes, split_axis=0, concat_axis=0, tiled=True)


def shards(ensemble, coupling, obs_column, obs_level, obs_value, obs_error, obs_live, partners):
    rows = MINE * LEVELS
    edges = 2 * HALO * LEVELS
    members = ensemble.reshape(512, COLS)
    early = pl.CostEstimate(flops=10**10, bytes_accessed=3 * 2**20, transcendentals=0)
    cost = pl.CostEstimate(flops=10**9, bytes_accessed=3 * 2**20, transcendentals=0)
    near, far = call(edges_kernel, (arr(HALO, COLS), arr(HALO, COLS)), [vmem()], "edges", cost=early)(members)
    far = lax.ppermute(far, "hor", [(i, (i - 1 + 2 * (i & 1)) % 16) for i in range(16)])
    near = lax.ppermute(near, "hor", [(i, i ^ 1) for i in range(16)])
    state, sums, mixing = call(
        prepare_kernel,
        (arr(2 * rows, 128), arr(128, 128), arr(2 * MIX, MIX, dtype=BF16)),
        [vmem()] * 8,
        "prepare",
        [pltpu.VMEM((2048, 128), F32), pltpu.VMEM((2048, 128), F32)],
    )(partners, members, obs_column, obs_level, obs_value, obs_error, obs_live, coupling)
    wide = pltpu.VMEM((WIDE * LEVELS, WIDTH), F32)
    all_levels = arr(SUBSTEPS * 2 * WIDE * LEVELS, WIDTH)
    inside = call(inner_kernel, all_levels, [vmem()] * 2, "inside", [wide], cost=cost)
    packed, _ = call(
        first_kernel,
        (arr(GROUP * 136, 128), all_levels),
        [vmem()] * 6,
        "first",
        [wide, pltpu.VMEM((4 * HALO * LEVELS, 128), F32), pltpu.VMEM((64, 128), F32)],
        aliases={0: 1},
    )(inside(state, mixing), far, near, state, sums, mixing)
    received = exchange(packed.reshape(GROUP, 136, 128), TILE).reshape(GROUP * 136, 128)
    folded = pltpu.VMEM((GROUP, FOLD, 128), F32)
    scalars = pltpu.SMEM((GROUP, 128), jnp.int32)
    keep, send, hist, table = call(
        first_gram_kernel,
        (arr(8, FOLD, 128), arr(8, FOLD, 128), arr(GROUP, 128), arr(GROUP, 128, dtype=jnp.int32)),
        [vmem()],
        "gram",
        [folded, scalars, pltpu.SemaphoreType.DMA(())],
    )(received)

    def roots(keep, send):
        parts = exchange(keep + swap(send), CHIPS)
        copies = call(root_kernel, arr(8, FOLD, 128), [vmem()], "root")(parts)
        same = exchange(copies, CHIPS)
        return same, swap(same)

    same, other = roots(keep, send)
    part = call(
        functools.partial(first_apply_kernel, False),
        arr(2 * rows, WIDTH),
        [vmem()] * 2,
        "apply",
        cost=cost,
    )(received, same)
    state, outer, inner = call(
        functools.partial(first_apply_kernel, True),
        (arr(2 * rows, WIDTH),) + (arr(edges, WIDTH),) * 2,
        [vmem()] * 3,
        "apply",
        aliases={2: 0},
    )(received, other, part)
    outer = lax.ppermute(outer, ALL, block_pairs(1))
    inner = lax.ppermute(inner, ALL, block_pairs(0))
    both, keep, send = call(
        forecast_kernel,
        (all_levels, arr(8, FOLD, 128), arr(8, FOLD, 128)),
        [vmem()] * 7,
        "forecast",
        [wide, folded, pltpu.VMEM((4 * HALO * LEVELS, 128), F32), scalars, pltpu.SemaphoreType.DMA(())],
        aliases={0: 0},
    )(inside(state, mixing), table, state, outer, inner, hist, mixing)
    same, other = roots(keep, send)
    part = call(
        functools.partial(last_apply_kernel, False),
        arr(GROUP * 128, 128),
        [vmem()] * 2,
        "analyse",
        cost=cost,
    )(both, same)
    analysed = call(
        functools.partial(last_apply_kernel, True),
        arr(GROUP * 128, 128),
        [vmem()] * 3,
        "analyse",
        aliases={2: 0},
    )(both, other, part)
    got = exchange(analysed.reshape(GROUP, 128, 128), TILE).reshape(GROUP * 128, 128)
    placed = call(place_kernel, arr(512, 512), [vmem()], "place", [pltpu.VMEM((2048, 128), F32)])(got)
    return placed.reshape(ensemble.shape)


def solution(mesh):
    fine = Mesh(mesh.devices.reshape(4, 16, 2, 2), ALL)
    group = TILE
    in_specs = (
        P(group, None, None, "hor"),
        P(),
        P(None, group, "hor", None),
        P(None, group, "hor", None),
        P(None, group, "hor", None),
        P(None, group, "hor", None),
        P(None, group, "hor", None),
        P(group, "hor", None),
    )
    out_specs = P(group, None, None, "hor")
    return jax.shard_map(shards, mesh=fine, in_specs=in_specs, out_specs=out_specs, check_vma=False)
```

```python
import functools
import math

import jax
import jax.numpy as jnp
from jax import lax
from jax.experimental import pallas as pl
from jax.experimental.pallas import tpu as pltpu
from jax.sharding import Mesh, PartitionSpec as P

SUBSTEPS = 4
ROOT_STEPS = 8
RATE = 0.5 * 0.2
MIX = 128
GROUP = 16
WIDTH = 128
LEVELS = 32
COLS = 512
MINE = COLS // GROUP
HALO = 2 * SUBSTEPS
WIDE = MINE + 2 * HALO
FINAL = (4 - 1) * 2 * WIDE * 32
FOLD = 72
F32 = jnp.float32
BF16 = jnp.bfloat16
VMEM_LIMIT = 16 * 1024 * 1024
ALL = ("mem", "hor", "zh", "core")
TILE = ("mem", "zh", "core")
CHIPS = ("mem", "zh")


def block_of(g):
    return ((g >> 1) & 1) * 8 + (g >> 2) * 2 + (g & 1)


MEMBER_AT = {block_of(g): g for g in range(GROUP)}


def my_place():
    core = lax.axis_index("core")
    flip = 15 * (lax.axis_index("hor") & 1)
    g = lax.axis_index("mem") * 4 + lax.axis_index("zh") * 2 + core
    return core, flip, block_of(jnp.bitwise_xor(g, flip))


def split(a):
    high = a.astype(BF16)
    return high, (a - high.astype(F32)).astype(BF16)


def dot_split(a, b, turned=False):
    left = jnp.concatenate([a[0], a[0], a[1]], axis=1)
    right = jnp.concatenate([b[0], b[1], b[0]], axis=1 if turned else 0)
    dims = (((1,), (1 if turned else 0,)), ((), ()))
    return lax.dot_general(left, right, dims, preferred_element_type=F32)


def iota(shape, dim):
    return lax.broadcasted_iota(jnp.int32, shape, dim)


def chunk_transpose(rows):
    lane = iota(rows[0].shape, 1)
    out = []
    for p in range(4):
        total = None
        for q in range(4):
            piece = rows[q] if p == q else pltpu.roll(rows[q], (32 * (q - p)) % 128, 1)
            total = piece if total is None else jnp.where(lane >= 32 * q, piece, total)
        out.append(total)
    return out


def edges_kernel(ens, near, far):
    first = ens[:, 0:128].T[0:HALO, :]
    last = ens[:, COLS - 128 : COLS].T[128 - HALO :, :]
    even = my_place()[1] == 0
    near[...] = jnp.where(even, last, first)
    far[...] = jnp.where(even, first, last)


def prepare_kernel(
    partner, ens, column, level, value, error, live, coupling, state, out, mixing, tiles, blocks
):
    for t in range(4):
        tiles[pl.ds(512 * t, 512), :] = ens[:, pl.ds(128 * t, 128)]
    for f in range(2):
        for t in range(4):
            for m in range(8):
                at = t * 512 + (m * 2 + f) * LEVELS
                rows = [tiles[pl.ds(at + i, 8, stride=4), :] for i in range(4)]
                for p, block in enumerate(chunk_transpose(rows)):
                    blocks[pl.ds(f * 1024 + (4 * t + p) * 8 + m, 8, stride=128), :] = block
        for four in range(8):
            turned = blocks[pl.ds(f * 1024 + four * 128, 128), :].T
            for i in range(4):
                at = f * MINE * LEVELS + 4 * four + i
                state[pl.ds(at, MINE, stride=LEVELS), :] = turned[32 * i : 32 * i + 32, :]
    member = jnp.bitwise_xor(iota((GROUP, COLS), 0), my_place()[1])
    place = ((member >> 1) & 1) * 8 + (member >> 2) * 2 + (member & 1)
    spot = iota((64, COLS), 0)
    zero = jnp.zeros((64, COLS), F32)
    for cycle in range(2):
        col = column[cycle, 0]
        weight = live[cycle, 0].astype(F32) / error[cycle, 0]
        weighted = weight * value[cycle, 0]
        here = (col >> 5) == place
        left = jnp.concatenate([jnp.where(here, weight, 0.0), jnp.where(here, weighted, 0.0)], axis=1)
        hit = jnp.where(level[cycle, 0] * 32 + (col & 31) == spot, 1.0, 0.0)
        right = jnp.concatenate(
            [jnp.concatenate([hit, zero], axis=1), jnp.concatenate([zero, hit], axis=1)], axis=0
        )
        sums = lax.dot_general(
            left, right, (((1,), (1,)), ((), ())), precision=lax.Precision.HIGHEST, preferred_element_type=F32
        )
        out[pl.ds(cycle, GROUP, stride=8), :] = sums
    lane = iota((GROUP, 128), 1)
    both = partner[0].astype(F32)
    out[pl.ds(2, GROUP, stride=8), :] = jnp.where(lane == 0, both[:, 0:1], both[:, 1:2])
    wide = jnp.concatenate([coupling[...]] * (MIX // LEVELS), axis=1)
    wide = jnp.concatenate([wide] * (MIX // LEVELS), axis=0)
    wide = jnp.where((iota((MIX, MIX), 0) >> 5) == (iota((MIX, MIX), 1) >> 5), RATE * RATE * wide, 0.0)
    high, rest = split(wide)
    mixing[pl.ds(0, MIX), :] = high
    mixing[pl.ds(MIX, MIX), :] = rest


def rows_after(sources, levels, step, f, c, count=1):
    if step == 0:
        ref, at = sources(f, c)
        return ref[pl.ds(at, count * LEVELS), :]
    return levels[pl.ds(((step - 1) * 2 + f) * WIDE * LEVELS + c * LEVELS, count * LEVELS), :]


def pressures(step, groups, sources, levels, ps, mixing):
    mix = (mixing[pl.ds(0, MIX), :], mixing[pl.ds(MIX, MIX), :])
    many = MIX // LEVELS
    for one, two in groups:
        block = jnp.concatenate(
            [rows_after(sources, levels, step - 1, 1, one, many), rows_after(sources, levels, step - 1, 1, two, many)],
            axis=1,
        )
        pressure = dot_split(mix, split(block))
        ps[pl.ds(one * LEVELS, MIX), :] = pressure[:, :128]
        ps[pl.ds(two * LEVELS, MIX), :] = pressure[:, 128:]


def sweep(step, start, stop, new, sources, levels, ps):
    last = step == SUBSTEPS

    def speed(at, c):
        value = rows_after(sources, levels, at, 0, c)
        return RATE * value if at in (0, SUBSTEPS) else value

    def slope(c):
        return ps[pl.ds(c * LEVELS, LEVELS), :]

    def put(f, c, value):
        levels[pl.ds(((step - 1) * 2 + f) * WIDE * LEVELS + c * LEVELS, LEVELS), :] = value

    flux_two, flux_one, height_one = None, None, None
    for c in range(start, stop):
        if new[0] <= c < new[1]:
            here = speed(step - 1, c)
            change = here * (speed(step - 1, c + 1) - speed(step - 1, c - 1))
            moved = (here - change) - (slope(c + 1) - slope(c - 1))
            put(0, c, moved * (1.0 / RATE) if last else moved)
        else:
            moved = speed(step, c)
        height = rows_after(sources, levels, step - 1, 1, c)
        flux = moved * height
        if c >= start + 2:
            put(1, c - 1, height_one - (flux - flux_two))
        flux_two, flux_one, height_one = flux_one, flux, height


def inner_kernel(state, mixing, levels, ps):
    span = MINE * LEVELS

    def sources(f, c):
        return state, f * span + (c - HALO) * LEVELS

    blank = jnp.zeros((LEVELS, 128), F32)
    for step in range(1, SUBSTEPS + 1):
        lo, hi = HALO + 2 * step, HALO + MINE - 2 * step
        if step < SUBSTEPS:
            for c in [*range(HALO, lo), *range(hi, HALO + MINE)]:
                levels[pl.ds(((step - 1) * 2 + 1) * WIDE * LEVELS + c * LEVELS, LEVELS), :] = blank
        begin = (lo - 2) // 4 * 4
        groups = [(c, c + 4) for c in range(begin, WIDE - begin, 8)]
        pressures(step, groups, sources, levels, ps, mixing)
        sweep(step, lo - 1, hi + 1, (lo - 1, hi + 1), sources, levels, ps)


def outer_steps(sources, levels, ps, mixing):
    blank = jnp.zeros((LEVELS, 128), F32)
    for step in range(1, SUBSTEPS + 1):
        lo, hi = 2 * step, WIDE - 2 * step
        if step < SUBSTEPS:
            for c in [*range(lo), *range(hi, WIDE)]:
                levels[pl.ds(((step - 1) * 2 + 1) * WIDE * LEVELS + c * LEVELS, LEVELS), :] = blank
        begin = (lo - 2) // 4 * 4
        groups = [(c, WIDE - 4 - c) for c in range(begin, begin + 12, 4)]
        pressures(step, groups, sources, levels, ps, mixing)
        sweep(step, lo - 1, lo + HALO + 1, (lo - 1, lo + HALO - 1), sources, levels, ps)
        sweep(step, hi - HALO - 1, hi + 1, (hi - HALO + 1, hi + 1), sources, levels, ps)


def four_levels(ref, at, four):
    rows = [ref[pl.ds(at + 4 * four + i, MINE, stride=LEVELS), :] for i in range(4)]
    return jnp.concatenate(rows, axis=0)


def slab_rows(ref, at, s):
    rows = [
        ref[pl.ds(f * WIDE * LEVELS + at + 2 * s + j, MINE, stride=LEVELS), :] for f in range(2) for j in range(2)
    ]
    return jnp.concatenate(rows, axis=0)


def first_kernel(levels_in, state, near, far, sums, mixing, packed, levels, ps, sides, spare):
    del levels_in
    span = MINE * LEVELS
    edge = HALO * LEVELS
    pieces = []
    flip = my_place()[1]
    even = flip == 0
    for before, after in ((far, near), (near, far)):
        for m in range(8):
            lanes = pl.ds(128 * (m // 2), 128)
            line = jnp.where(even, before[:, lanes], after[:, lanes])
            spare[pl.ds(8 * m, 8), :] = line if m % 2 == 0 else pltpu.roll(line, 64, 1)
        pieces += [spare[pl.ds(c, 8, stride=8), :] for c in range(8)]
    halo = jnp.concatenate(pieces, axis=0).T
    lane = iota((LEVELS, 128), 1)
    for f in range(2):
        line = halo[f * LEVELS : (f + 1) * LEVELS, :]
        for c in range(HALO):
            inner = pltpu.roll(state[pl.ds(f * span + (MINE - HALO + c) * LEVELS, LEVELS), :], 8, 1)
            outer = pltpu.roll(line, (128 - 8 * c) % 128, 1)
            sides[pl.ds((2 * f) * edge + c * LEVELS, LEVELS), :] = jnp.where(lane < 8, outer, inner)
            inner = pltpu.roll(state[pl.ds(f * span + c * LEVELS, LEVELS), :], 120, 1)
            outer = pltpu.roll(line, (56 - 8 * c) % 128, 1)
            sides[pl.ds((2 * f + 1) * edge + c * LEVELS, LEVELS), :] = jnp.where(lane >= 120, outer, inner)

    def sources(f, c):
        if c < HALO:
            return sides, 2 * f * edge + c * LEVELS
        if c < HALO + MINE:
            return state, f * span + (c - HALO) * LEVELS
        return sides, (2 * f + 1) * edge + (c - HALO - MINE) * LEVELS

    outer_steps(sources, levels, ps, mixing)
    starts = [jnp.bitwise_xor(MEMBER_AT[k], flip) * 136 for k in range(GROUP)]
    for s in range(GROUP):
        square = slab_rows(levels, FINAL + edge, s).T
        for k in range(GROUP):
            packed[pl.ds(starts[k] + 8 * s, 8), :] = square[8 * k : 8 * k + 8, :]
    for g in range(GROUP):
        packed[pl.ds(g * 136 + 128, 8), :] = sums[pl.ds(g * 8, 8), :]


def square_of(ref, s):
    return jnp.concatenate([ref[pl.ds(g * 136 + s * 8, 8), :] for g in range(GROUP)], axis=0)


def fold(top, bottom, vector, extra=0.0):
    row, lane = iota((64, 128), 0), iota((64, 128), 1)
    body = jnp.where((lane >= 64) | (row <= lane), top, pltpu.roll(bottom, 64, 1))
    diagonal = jnp.sum(jnp.where(lane == row + 64, bottom, 0.0), axis=0, keepdims=True)
    at = iota((8, 128), 0)
    tail = jnp.where(at == 0, diagonal, jnp.where(at == 1, vector, extra))
    return body, tail


def half_of(body, tail):
    row, lane = iota((64, 128), 0), iota((64, 128), 1)
    top = jnp.where((lane >= 64) | (row < lane), body, jnp.where(row == lane, 0.5 * body, 0.0))
    moved = pltpu.roll(body, 64, 1)
    bottom = jnp.where(row > lane - 64, moved, jnp.where(row == lane - 64, 0.5 * tail[0:1, :], 0.0))
    bottom = jnp.where(lane >= 64, bottom, 0.0)
    return jnp.concatenate([top, bottom], axis=0)


def blend(fs, table, core, keep, send):
    for j in range(GROUP // 2):
        for which, ref in ((core, keep), (1 - core, send)):
            s = 2 * j + which
            ref[j] = fs[s] + fs[table[s, 0]] + fs[table[s, 1]]


def gram_of(fs, q, anomaly, halves, mean, line, upper):
    lane = iota((1, 128), 1)
    swapped = pltpu.roll(line, 64, 1)
    mine = (lane >= 64) if upper else (lane < 64)
    weight = jnp.where(mine, swapped if upper else line, 0.0)
    pull = jnp.where(mine, line if upper else swapped, 0.0) - weight * mean
    left = jnp.concatenate([anomaly * weight, jnp.broadcast_to(pull, (8, 128))], axis=0)
    gram = dot_split(split(left), halves, turned=True)
    body, tail = fold(gram[:64], gram[64:128], gram[128:129])
    fs[q, pl.ds(0, 64), :] = body
    fs[q, pl.ds(64, 8), :] = tail


def centred(square):
    mean = jnp.mean(square, axis=0, keepdims=True)
    anomaly = square - mean
    return anomaly, split(anomaly), mean


def first_gram_kernel(got, keep, send, later, table_out, fs, table, sem):
    table_out[...] = got[pl.ds(130, GROUP, stride=136), :].astype(jnp.int32)
    copy = pltpu.make_async_copy(table_out, table, sem)
    copy.start()
    later[...] = got[pl.ds(129, GROUP, stride=136), :]
    for q in range(GROUP):
        gram_of(fs, q, *centred(square_of(got, q)), got[pl.ds(q * 136 + 128, 1), :], True)
    copy.wait()
    blend(fs, table, my_place()[0], keep, send)


def forecast_kernel(levels_in, table_in, state, outer, inner, hist, mixing, levels, keep, send, ps, fs, sides, table, sem):
    del levels_in
    edge = HALO * LEVELS
    span = MINE * LEVELS
    copy = pltpu.make_async_copy(table_in, table, sem)
    copy.start()
    odd = (my_place()[2] & 1) == 1
    for f in range(2):
        rows = pl.ds(f * edge, edge)
        sides[pl.ds(2 * f * edge, edge), :] = jnp.where(odd, inner[rows, :], outer[rows, :])
        sides[pl.ds((2 * f + 1) * edge, edge), :] = jnp.where(odd, outer[rows, :], inner[rows, :])

    def sources(f, c):
        if c < HALO:
            return sides, 2 * f * edge + c * LEVELS
        if c < HALO + MINE:
            return state, f * span + (c - HALO) * LEVELS
        return sides, (2 * f + 1) * edge + (c - HALO - MINE) * LEVELS

    outer_steps(sources, levels, ps, mixing)
    for four in range(8):
        parts = centred(four_levels(levels, FINAL + WIDE * LEVELS + edge, four).T)
        for half in range(2):
            q = 2 * four + half
            gram_of(fs, q, *parts, hist[pl.ds(q, 1), :], half == 1)
    copy.wait()
    blend(fs, table, my_place()[0], keep, send)


def root_kernel(got, out):
    total = got[0]
    for j in range(1, 8):
        total = total + got[j]
    half = half_of(total[:64], total[64:])
    gram, vector = half + half.T, total[65:66]
    eye = jnp.where(iota((WIDTH, WIDTH), 0) == iota((WIDTH, WIDTH), 1), 1.0, 0.0)
    third = 1.0 / 3.0
    blended = (WIDTH - 1.0) * eye + gram * third
    pull = vector * third
    squared = jnp.sum(jnp.sum(blended * blended, axis=0, keepdims=True), axis=1, keepdims=True)
    norm = jnp.sqrt(squared)
    a = blended / norm
    newton = 1.5 * eye - 0.5 * a
    inner = jnp.broadcast_to(pull, (8, WIDTH))
    both = dot_split(split(jnp.concatenate([a, inner], axis=0)), split(newton))
    a, z, inner = both[:WIDTH], newton, both[WIDTH:]
    for step in range(1, ROOT_STEPS):
        newton = 1.5 * eye - 0.5 * dot_split(split(z), split(a))
        if step < ROOT_STEPS - 1:
            both = dot_split(split(jnp.concatenate([a, z, inner], axis=0)), split(newton))
            a, z, inner = both[:WIDTH], both[WIDTH : 2 * WIDTH], both[2 * WIDTH :]
        else:
            both = dot_split(split(jnp.concatenate([z, inner], axis=0)), split(newton))
            z, inner = both[:WIDTH], both[WIDTH:]
    shift = dot_split(split(inner), split(z), turned=True)[0:1, :] / norm
    spread = z * (math.sqrt(WIDTH - 1.0) / jnp.sqrt(norm))
    sums = jnp.sum(spread, axis=0, keepdims=True) + jnp.sum(shift, axis=1, keepdims=True)
    body, tail = fold(spread[:64], spread[64:], shift, (1.0 - sums) * (1.0 / WIDTH))
    for j in range(8):
        out[j, pl.ds(0, 64), :] = body
        out[j, pl.ds(64, 8), :] = tail


def weights_of(roots, j):
    body, tail = roots[j, pl.ds(0, 64), :], roots[j, pl.ds(64, 8), :]
    half = half_of(body, tail)
    return split((half + tail[1:2, :]) + (half + tail[2:3, :]).T)


def first_apply_kernel(second, got, roots, *refs):
    out = refs[1] if second else refs[0]
    span = MINE * LEVELS
    edge = HALO * LEVELS
    core, _, block = my_place()
    parity = 1 - core if second else core
    for j in range(8):
        s = 2 * j + parity
        square = jnp.concatenate(
            [got[pl.ds(pl.multiple_of(g * 136 + s * 8, 8), 8), :] for g in range(GROUP)], axis=0
        )
        result = dot_split(weights_of(roots, j), split(square)).T
        for fj in range(4):
            at = (fj // 2) * span + 2 * s + fj % 2
            out[pl.ds(at, MINE, stride=LEVELS), :] = result[fj * 32 : fj * 32 + 32, :]
    if second:
        outer, inner = refs[2:]
        odd = (block & 1) == 1
        for f in range(2):
            first = out[pl.ds(f * span, edge), :]
            final = out[pl.ds((f + 1) * span - edge, edge), :]
            outer[pl.ds(f * edge, edge), :] = jnp.where(odd, final, first)
            inner[pl.ds(f * edge, edge), :] = jnp.where(odd, first, final)


def last_apply_kernel(second, both, roots, *refs):
    out = refs[-1]
    core, _, block = my_place()
    parity = 1 - core if second else core
    starts = []
    for chunk in range(4):
        fj = (chunk + 16 - block) & 3
        starts.append((fj >> 1) * (WIDE * LEVELS) + (fj & 1) + (FINAL + HALO * LEVELS))
    for j in range(8):
        s = 2 * j + parity
        field = jnp.concatenate(
            [both[pl.ds(at + 2 * s, MINE, stride=LEVELS), :] for at in starts], axis=0
        )
        result = dot_split(weights_of(roots, j), split(field), turned=True)
        for g in range(GROUP):
            out[pl.ds(pl.multiple_of((g * GROUP + s) * 8, 8), 8), :] = result[g * 8 : g * 8 + 8, :]


def place_kernel(got, out, tiles):
    flip = my_place()[1]
    starts = [jnp.bitwise_xor(MEMBER_AT[k], flip) * 128 for k in range(GROUP)]
    lane = iota((16, 128), 1)
    for t in range(4):
        for n in range(8):
            rows = [got[pl.ds(starts[4 * t + p] + n, 16, stride=8), :] for p in range(4)]
            for fj in range(4):
                block = rows[(0 - fj) % 4]
                for chunk in range(1, 4):
                    block = jnp.where(lane >= 32 * chunk, rows[(chunk - fj) % 4], block)
                if fj > 0:
                    block = pltpu.roll(block, 128 - 32 * fj, 1)
                tiles[pl.ds(512 * t + (n * 2 + fj // 2) * LEVELS + fj % 2, 16, stride=2), :] = block
    for t in range(4):
        out[:, pl.ds(128 * t, 128)] = tiles[pl.ds(512 * t, 512), :]


def vmem():
    return pl.BlockSpec(memory_space=pltpu.VMEM)


def call(kernel, out, ins, name, scratch=(), aliases=None, cost=None):
    return pl.pallas_call(
        kernel,
        out_shape=out,
        in_specs=ins,
        out_specs=jax.tree.map(lambda _: vmem(), out),
        scratch_shapes=scratch,
        input_output_aliases=aliases or {},
        cost_estimate=cost,
        compiler_params=pltpu.CompilerParams(vmem_limit_bytes=VMEM_LIMIT),
        name=name,
    )


def arr(*shape, dtype=F32):
    return jax.ShapeDtypeStruct(shape, dtype)


def holder(block, hor):
    g = MEMBER_AT[block] ^ (15 * (hor & 1))
    return ((g >> 2) * 16 + hor) * 4 + (g & 3)


def block_pairs(start):
    pairs = []
    for hor in range(16):
        for block in range(start, GROUP, 2):
            after = block + 1
            pair = (holder(block, hor), holder(after % GROUP, (hor + after // GROUP) % 16))
            pairs += [pair, pair[::-1]]
    return pairs


def swap(x):
    return lax.ppermute(x, "core", [(0, 1), (1, 0)])


def exchange(x, axes):
    return lax.all_to_all(x, axes, split_axis=0, concat_axis=0, tiled=True)


def shards(ensemble, coupling, obs_column, obs_level, obs_value, obs_error, obs_live, partners):
    rows = MINE * LEVELS
    edges = 2 * HALO * LEVELS
    members = ensemble.reshape(512, COLS)
    early = pl.CostEstimate(flops=10**10, bytes_accessed=3 * 2**20, transcendentals=0)
    cost = pl.CostEstimate(flops=10**9, bytes_accessed=3 * 2**20, transcendentals=0)
    near, far = call(edges_kernel, (arr(HALO, COLS), arr(HALO, COLS)), [vmem()], "edges", cost=early)(members)
    far = lax.ppermute(far, "hor", [(i, (i - 1 + 2 * (i & 1)) % 16) for i in range(16)])
    near = lax.ppermute(near, "hor", [(i, i ^ 1) for i in range(16)])
    state, sums, mixing = call(
        prepare_kernel,
        (arr(2 * rows, 128), arr(128, 128), arr(2 * MIX, MIX, dtype=BF16)),
        [vmem()] * 8,
        "prepare",
        [pltpu.VMEM((2048, 128), F32), pltpu.VMEM((2048, 128), F32)],
    )(partners, members, obs_column, obs_level, obs_value, obs_error, obs_live, coupling)
    wide = pltpu.VMEM((WIDE * LEVELS, WIDTH), F32)
    all_levels = arr(SUBSTEPS * 2 * WIDE * LEVELS, WIDTH)
    inside = call(inner_kernel, all_levels, [vmem()] * 2, "inside", [wide], cost=cost)
    packed, _ = call(
        first_kernel,
        (arr(GROUP * 136, 128), all_levels),
        [vmem()] * 6,
        "first",
        [wide, pltpu.VMEM((4 * HALO * LEVELS, 128), F32), pltpu.VMEM((64, 128), F32)],
        aliases={0: 1},
    )(inside(state, mixing), state, near, far, sums, mixing)
    received = exchange(packed.reshape(GROUP, 136, 128), TILE).reshape(GROUP * 136, 128)
    folded = pltpu.VMEM((GROUP, FOLD, 128), F32)
    scalars = pltpu.SMEM((GROUP, 128), jnp.int32)
    keep, send, hist, table = call(
        first_gram_kernel,
        (arr(8, FOLD, 128), arr(8, FOLD, 128), arr(GROUP, 128), arr(GROUP, 128, dtype=jnp.int32)),
        [vmem()],
        "gram",
        [folded, scalars, pltpu.SemaphoreType.DMA(())],
    )(received)

    def roots(keep, send):
        parts = exchange(keep + swap(send), CHIPS)
        copies = call(root_kernel, arr(8, FOLD, 128), [vmem()], "root")(parts)
        same = exchange(copies, CHIPS)
        return same, swap(same)

    same, other = roots(keep, send)
    part = call(
        functools.partial(first_apply_kernel, False),
        arr(2 * rows, WIDTH),
        [vmem()] * 2,
        "apply",
        cost=cost,
    )(received, same)
    state, outer, inner = call(
        functools.partial(first_apply_kernel, True),
        (arr(2 * rows, WIDTH),) + (arr(edges, WIDTH),) * 2,
        [vmem()] * 3,
        "apply",
        aliases={2: 0},
    )(received, other, part)
    outer = lax.ppermute(outer, ALL, block_pairs(1))
    inner = lax.ppermute(inner, ALL, block_pairs(0))
    both, keep, send = call(
        forecast_kernel,
        (all_levels, arr(8, FOLD, 128), arr(8, FOLD, 128)),
        [vmem()] * 7,
        "forecast",
        [wide, folded, pltpu.VMEM((4 * HALO * LEVELS, 128), F32), scalars, pltpu.SemaphoreType.DMA(())],
        aliases={0: 0},
    )(inside(state, mixing), table, state, outer, inner, hist, mixing)
    same, other = roots(keep, send)
    part = call(
        functools.partial(last_apply_kernel, False),
        arr(GROUP * 128, 128),
        [vmem()] * 2,
        "analyse",
        cost=cost,
    )(both, same)
    analysed = call(
        functools.partial(last_apply_kernel, True),
        arr(GROUP * 128, 128),
        [vmem()] * 3,
        "analyse",
        aliases={2: 0},
    )(both, other, part)
    got = exchange(analysed.reshape(GROUP, 128, 128), TILE).reshape(GROUP * 128, 128)
    placed = call(place_kernel, arr(512, 512), [vmem()], "place", [pltpu.VMEM((2048, 128), F32)])(got)
    return placed.reshape(ensemble.shape)


def solution(mesh):
    fine = Mesh(mesh.devices.reshape(4, 16, 2, 2), ALL)
    group = TILE
    in_specs = (
        P(group, None, None, "hor"),
        P(),
        P(None, group, "hor", None),
        P(None, group, "hor", None),
        P(None, group, "hor", None),
        P(None, group, "hor", None),
        P(None, group, "hor", None),
        P(group, "hor", None),
    )
    out_specs = P(group, None, None, "hor")
    return jax.shard_map(shards, mesh=fine, in_specs=in_specs, out_specs=out_specs, check_vma=False)
```

```python
import functools
import math

import jax
import jax.numpy as jnp
from jax import lax
from jax.experimental import pallas as pl
from jax.experimental.pallas import tpu as pltpu
from jax.sharding import Mesh, PartitionSpec as P

SUBSTEPS = 4
ROOT_STEPS = 8
RATE = 0.5 * 0.2
MIX = 128
GROUP = 16
WIDTH = 128
LEVELS = 32
COLS = 512
MINE = COLS // GROUP
HALO = 2 * SUBSTEPS
WIDE = MINE + 2 * HALO
FINAL = (4 - 1) * 2 * WIDE * 32
FOLD = 72
F32 = jnp.float32
BF16 = jnp.bfloat16
VMEM_LIMIT = 16 * 1024 * 1024
ALL = ("mem", "hor", "zh", "core")
TILE = ("mem", "zh", "core")
CHIPS = ("mem", "zh")


def block_of(g):
    return ((g >> 1) & 1) * 8 + (g >> 2) * 2 + (g & 1)


MEMBER_AT = {block_of(g): g for g in range(GROUP)}


def my_place():
    core = lax.axis_index("core")
    flip = 15 * (lax.axis_index("hor") & 1)
    g = lax.axis_index("mem") * 4 + lax.axis_index("zh") * 2 + core
    return core, flip, block_of(jnp.bitwise_xor(g, flip))


def split(a):
    high = a.astype(BF16)
    return high, (a - high.astype(F32)).astype(BF16)


def dot_split(a, b, turned=False):
    left = jnp.concatenate([a[0], a[0], a[1]], axis=1)
    right = jnp.concatenate([b[0], b[1], b[0]], axis=1 if turned else 0)
    dims = (((1,), (1 if turned else 0,)), ((), ()))
    return lax.dot_general(left, right, dims, preferred_element_type=F32)


def iota(shape, dim):
    return lax.broadcasted_iota(jnp.int32, shape, dim)


def chunk_transpose(rows):
    lane = iota(rows[0].shape, 1)
    out = []
    for p in range(4):
        total = None
        for q in range(4):
            piece = rows[q] if p == q else pltpu.roll(rows[q], (32 * (q - p)) % 128, 1)
            total = piece if total is None else jnp.where(lane >= 32 * q, piece, total)
        out.append(total)
    return out


def edges_kernel(ens, near, far):
    first = ens[:, 0:128].T[0:HALO, :]
    last = ens[:, COLS - 128 : COLS].T[128 - HALO :, :]
    even = my_place()[1] == 0
    near[...] = jnp.where(even, last, first)
    far[...] = jnp.where(even, first, last)


def prepare_kernel(
    partner, ens, column, level, value, error, live, coupling, state, out, mixing, tiles, blocks
):
    for t in range(4):
        tiles[pl.ds(512 * t, 512), :] = ens[:, pl.ds(128 * t, 128)]
    for f in range(2):
        for t in range(4):
            for m in range(8):
                at = t * 512 + (m * 2 + f) * LEVELS
                rows = [tiles[pl.ds(at + i, 8, stride=4), :] for i in range(4)]
                for p, block in enumerate(chunk_transpose(rows)):
                    blocks[pl.ds(f * 1024 + (4 * t + p) * 8 + m, 8, stride=128), :] = block
        for four in range(8):
            turned = blocks[pl.ds(f * 1024 + four * 128, 128), :].T
            for i in range(4):
                at = f * MINE * LEVELS + 4 * four + i
                state[pl.ds(at, MINE, stride=LEVELS), :] = turned[32 * i : 32 * i + 32, :]
    member = jnp.bitwise_xor(iota((GROUP, COLS), 0), my_place()[1])
    place = ((member >> 1) & 1) * 8 + (member >> 2) * 2 + (member & 1)
    spot = iota((64, COLS), 0)
    zero = jnp.zeros((64, COLS), F32)
    for cycle in range(2):
        col = column[cycle, 0]
        weight = live[cycle, 0].astype(F32) / error[cycle, 0]
        weighted = weight * value[cycle, 0]
        here = (col >> 5) == place
        left = jnp.concatenate([jnp.where(here, weight, 0.0), jnp.where(here, weighted, 0.0)], axis=1)
        hit = jnp.where(level[cycle, 0] * 32 + (col & 31) == spot, 1.0, 0.0)
        right = jnp.concatenate(
            [jnp.concatenate([hit, zero], axis=1), jnp.concatenate([zero, hit], axis=1)], axis=0
        )
        sums = lax.dot_general(
            left, right, (((1,), (1,)), ((), ())), precision=lax.Precision.HIGHEST, preferred_element_type=F32
        )
        out[pl.ds(cycle, GROUP, stride=8), :] = sums
    lane = iota((GROUP, 128), 1)
    both = partner[0].astype(F32)
    out[pl.ds(2, GROUP, stride=8), :] = jnp.where(lane == 0, both[:, 0:1], both[:, 1:2])
    wide = jnp.concatenate([coupling[...]] * (MIX // LEVELS), axis=1)
    wide = jnp.concatenate([wide] * (MIX // LEVELS), axis=0)
    wide = jnp.where((iota((MIX, MIX), 0) >> 5) == (iota((MIX, MIX), 1) >> 5), RATE * RATE * wide, 0.0)
    high, rest = split(wide)
    mixing[pl.ds(0, MIX), :] = high
    mixing[pl.ds(MIX, MIX), :] = rest


def rows_after(sources, levels, step, f, c, count=1):
    if step == 0:
        ref, at = sources(f, c)
        return ref[pl.ds(at, count * LEVELS), :]
    return levels[pl.ds(((step - 1) * 2 + f) * WIDE * LEVELS + c * LEVELS, count * LEVELS), :]


def pressures(step, groups, sources, levels, ps, mixing):
    mix = (mixing[pl.ds(0, MIX), :], mixing[pl.ds(MIX, MIX), :])
    many = MIX // LEVELS
    for c in groups:
        block = jnp.concatenate(
            [rows_after(sources, levels, step - 1, 1, c, many), rows_after(sources, levels, step - 1, 1, c + many, many)],
            axis=1,
        )
        pressure = dot_split(mix, split(block))
        ps[pl.ds(c * LEVELS, MIX), :] = pressure[:, :128]
        ps[pl.ds(c * LEVELS + MIX, MIX), :] = pressure[:, 128:]


def sweep(step, start, stop, new, sources, levels, ps):
    last = step == SUBSTEPS

    def speed(at, c):
        value = rows_after(sources, levels, at, 0, c)
        return RATE * value if at in (0, SUBSTEPS) else value

    def slope(c):
        return ps[pl.ds(c * LEVELS, LEVELS), :]

    def put(f, c, value):
        levels[pl.ds(((step - 1) * 2 + f) * WIDE * LEVELS + c * LEVELS, LEVELS), :] = value

    flux_two, flux_one, height_one = None, None, None
    for c in range(start, stop):
        if new[0] <= c < new[1]:
            here = speed(step - 1, c)
            change = here * (speed(step - 1, c + 1) - speed(step - 1, c - 1))
            moved = (here - change) - (slope(c + 1) - slope(c - 1))
            put(0, c, moved * (1.0 / RATE) if last else moved)
        else:
            moved = speed(step, c)
        height = rows_after(sources, levels, step - 1, 1, c)
        flux = moved * height
        if c >= start + 2:
            put(1, c - 1, height_one - (flux - flux_two))
        flux_two, flux_one, height_one = flux_one, flux, height


def inner_kernel(state, mixing, levels, ps):
    span = MINE * LEVELS

    def sources(f, c):
        return state, f * span + (c - HALO) * LEVELS

    blank = jnp.zeros((LEVELS, 128), F32)
    for step in range(1, SUBSTEPS + 1):
        lo, hi = HALO + 2 * step, HALO + MINE - 2 * step
        if step < SUBSTEPS:
            for c in [*range(HALO, lo), *range(hi, HALO + MINE)]:
                levels[pl.ds(((step - 1) * 2 + 1) * WIDE * LEVELS + c * LEVELS, LEVELS), :] = blank
        pressures(step, range(HALO, HALO + MINE, 8), sources, levels, ps, mixing)
        sweep(step, lo - 1, hi + 1, (lo - 1, hi + 1), sources, levels, ps)


def outer_steps(sources, levels, ps, mixing):
    blank = jnp.zeros((LEVELS, 128), F32)
    for step in range(1, SUBSTEPS + 1):
        lo, hi = 2 * step, WIDE - 2 * step
        if step < SUBSTEPS:
            for c in [*range(lo), *range(hi, WIDE)]:
                levels[pl.ds(((step - 1) * 2 + 1) * WIDE * LEVELS + c * LEVELS, LEVELS), :] = blank
        pressures(step, (0, HALO, WIDE - 2 * HALO, WIDE - HALO), sources, levels, ps, mixing)
        sweep(step, lo - 1, lo + HALO + 1, (lo - 1, lo + HALO - 1), sources, levels, ps)
        sweep(step, hi - HALO - 1, hi + 1, (hi - HALO + 1, hi + 1), sources, levels, ps)


def four_levels(ref, at, four):
    rows = [ref[pl.ds(at + 4 * four + i, MINE, stride=LEVELS), :] for i in range(4)]
    return jnp.concatenate(rows, axis=0)


def slab_rows(ref, at, s):
    rows = [
        ref[pl.ds(f * WIDE * LEVELS + at + 2 * s + j, MINE, stride=LEVELS), :] for f in range(2) for j in range(2)
    ]
    return jnp.concatenate(rows, axis=0)


def first_kernel(levels_in, state, near, far, sums, mixing, packed, levels, ps, sides, spare):
    del levels_in
    span = MINE * LEVELS
    edge = HALO * LEVELS
    pieces = []
    flip = my_place()[1]
    even = flip == 0
    for before, after in ((far, near), (near, far)):
        for m in range(8):
            lanes = pl.ds(128 * (m // 2), 128)
            line = jnp.where(even, before[:, lanes], after[:, lanes])
            spare[pl.ds(8 * m, 8), :] = line if m % 2 == 0 else pltpu.roll(line, 64, 1)
        pieces += [spare[pl.ds(c, 8, stride=8), :] for c in range(8)]
    halo = jnp.concatenate(pieces, axis=0).T
    lane = iota((LEVELS, 128), 1)
    for f in range(2):
        line = halo[f * LEVELS : (f + 1) * LEVELS, :]
        for c in range(HALO):
            inner = pltpu.roll(state[pl.ds(f * span + (MINE - HALO + c) * LEVELS, LEVELS), :], 8, 1)
            outer = pltpu.roll(line, (128 - 8 * c) % 128, 1)
            sides[pl.ds((2 * f) * edge + c * LEVELS, LEVELS), :] = jnp.where(lane < 8, outer, inner)
            inner = pltpu.roll(state[pl.ds(f * span + c * LEVELS, LEVELS), :], 120, 1)
            outer = pltpu.roll(line, (56 - 8 * c) % 128, 1)
            sides[pl.ds((2 * f + 1) * edge + c * LEVELS, LEVELS), :] = jnp.where(lane >= 120, outer, inner)

    def sources(f, c):
        if c < HALO:
            return sides, 2 * f * edge + c * LEVELS
        if c < HALO + MINE:
            return state, f * span + (c - HALO) * LEVELS
        return sides, (2 * f + 1) * edge + (c - HALO - MINE) * LEVELS

    outer_steps(sources, levels, ps, mixing)
    starts = [jnp.bitwise_xor(MEMBER_AT[k], flip) * 136 for k in range(GROUP)]
    for s in range(GROUP):
        square = slab_rows(levels, FINAL + edge, s).T
        for k in range(GROUP):
            packed[pl.ds(starts[k] + 8 * s, 8), :] = square[8 * k : 8 * k + 8, :]
    for g in range(GROUP):
        packed[pl.ds(g * 136 + 128, 8), :] = sums[pl.ds(g * 8, 8), :]


def square_of(ref, s):
    return jnp.concatenate([ref[pl.ds(g * 136 + s * 8, 8), :] for g in range(GROUP)], axis=0)


def fold(top, bottom, vector, extra=0.0):
    row, lane = iota((64, 128), 0), iota((64, 128), 1)
    body = jnp.where((lane >= 64) | (row <= lane), top, pltpu.roll(bottom, 64, 1))
    diagonal = jnp.sum(jnp.where(lane == row + 64, bottom, 0.0), axis=0, keepdims=True)
    at = iota((8, 128), 0)
    tail = jnp.where(at == 0, diagonal, jnp.where(at == 1, vector, extra))
    return body, tail


def half_of(body, tail):
    row, lane = iota((64, 128), 0), iota((64, 128), 1)
    top = jnp.where((lane >= 64) | (row < lane), body, jnp.where(row == lane, 0.5 * body, 0.0))
    moved = pltpu.roll(body, 64, 1)
    bottom = jnp.where(row > lane - 64, moved, jnp.where(row == lane - 64, 0.5 * tail[0:1, :], 0.0))
    bottom = jnp.where(lane >= 64, bottom, 0.0)
    return jnp.concatenate([top, bottom], axis=0)


def blend(fs, table, core, keep, send):
    for j in range(GROUP // 2):
        for which, ref in ((core, keep), (1 - core, send)):
            s = 2 * j + which
            ref[j] = fs[s] + fs[table[s, 0]] + fs[table[s, 1]]


def gram_of(fs, q, anomaly, halves, mean, line, upper):
    lane = iota((1, 128), 1)
    swapped = pltpu.roll(line, 64, 1)
    mine = (lane >= 64) if upper else (lane < 64)
    weight = jnp.where(mine, swapped if upper else line, 0.0)
    pull = jnp.where(mine, line if upper else swapped, 0.0) - weight * mean
    left = jnp.concatenate([anomaly * weight, jnp.broadcast_to(pull, (8, 128))], axis=0)
    gram = dot_split(split(left), halves, turned=True)
    body, tail = fold(gram[:64], gram[64:128], gram[128:129])
    fs[q, pl.ds(0, 64), :] = body
    fs[q, pl.ds(64, 8), :] = tail


def centred(square):
    mean = jnp.mean(square, axis=0, keepdims=True)
    anomaly = square - mean
    return anomaly, split(anomaly), mean


def first_gram_kernel(got, keep, send, later, table_out, fs, table, sem):
    table_out[...] = got[pl.ds(130, GROUP, stride=136), :].astype(jnp.int32)
    copy = pltpu.make_async_copy(table_out, table, sem)
    copy.start()
    later[...] = got[pl.ds(129, GROUP, stride=136), :]
    for q in range(GROUP):
        gram_of(fs, q, *centred(square_of(got, q)), got[pl.ds(q * 136 + 128, 1), :], True)
    copy.wait()
    blend(fs, table, my_place()[0], keep, send)


def forecast_kernel(levels_in, table_in, state, outer, inner, hist, mixing, levels, keep, send, ps, fs, sides, table, sem):
    del levels_in
    edge = HALO * LEVELS
    span = MINE * LEVELS
    copy = pltpu.make_async_copy(table_in, table, sem)
    copy.start()
    odd = (my_place()[2] & 1) == 1
    for f in range(2):
        rows = pl.ds(f * edge, edge)
        sides[pl.ds(2 * f * edge, edge), :] = jnp.where(odd, inner[rows, :], outer[rows, :])
        sides[pl.ds((2 * f + 1) * edge, edge), :] = jnp.where(odd, outer[rows, :], inner[rows, :])

    def sources(f, c):
        if c < HALO:
            return sides, 2 * f * edge + c * LEVELS
        if c < HALO + MINE:
            return state, f * span + (c - HALO) * LEVELS
        return sides, (2 * f + 1) * edge + (c - HALO - MINE) * LEVELS

    outer_steps(sources, levels, ps, mixing)
    for four in range(8):
        parts = centred(four_levels(levels, FINAL + WIDE * LEVELS + edge, four).T)
        for half in range(2):
            q = 2 * four + half
            gram_of(fs, q, *parts, hist[pl.ds(q, 1), :], half == 1)
    copy.wait()
    blend(fs, table, my_place()[0], keep, send)


def root_kernel(got, out):
    total = got[0]
    for j in range(1, 8):
        total = total + got[j]
    half = half_of(total[:64], total[64:])
    gram, vector = half + half.T, total[65:66]
    eye = jnp.where(iota((WIDTH, WIDTH), 0) == iota((WIDTH, WIDTH), 1), 1.0, 0.0)
    third = 1.0 / 3.0
    blended = (WIDTH - 1.0) * eye + gram * third
    pull = vector * third
    squared = jnp.sum(jnp.sum(blended * blended, axis=0, keepdims=True), axis=1, keepdims=True)
    norm = jnp.sqrt(squared)
    a = blended / norm
    newton = 1.5 * eye - 0.5 * a
    a = dot_split(split(a), split(newton))
    z = newton
    for step in range(1, ROOT_STEPS):
        newton = 1.5 * eye - 0.5 * dot_split(split(z), split(a))
        if step < ROOT_STEPS - 1:
            both = dot_split(split(jnp.concatenate([a, z], axis=0)), split(newton))
            a, z = both[:WIDTH], both[WIDTH:]
        else:
            z = dot_split(split(z), split(newton))
    inner = jnp.sum(z * pull, axis=1, keepdims=True)
    shift = jnp.sum(z * inner, axis=0, keepdims=True) / norm
    spread = z * (math.sqrt(WIDTH - 1.0) / jnp.sqrt(norm))
    sums = jnp.sum(spread, axis=0, keepdims=True) + jnp.sum(shift, axis=1, keepdims=True)
    body, tail = fold(spread[:64], spread[64:], shift, (1.0 - sums) * (1.0 / WIDTH))
    for j in range(8):
        out[j, pl.ds(0, 64), :] = body
        out[j, pl.ds(64, 8), :] = tail


def weights_of(roots, j):
    body, tail = roots[j, pl.ds(0, 64), :], roots[j, pl.ds(64, 8), :]
    half = half_of(body, tail)
    return split((half + tail[1:2, :]) + (half + tail[2:3, :]).T)


def first_apply_kernel(second, got, roots, *refs):
    out = refs[1] if second else refs[0]
    span = MINE * LEVELS
    edge = HALO * LEVELS
    core, _, block = my_place()
    parity = 1 - core if second else core
    for j in range(8):
        s = 2 * j + parity
        square = jnp.concatenate(
            [got[pl.ds(pl.multiple_of(g * 136 + s * 8, 8), 8), :] for g in range(GROUP)], axis=0
        )
        result = dot_split(weights_of(roots, j), split(square)).T
        for fj in range(4):
            at = (fj // 2) * span + 2 * s + fj % 2
            out[pl.ds(at, MINE, stride=LEVELS), :] = result[fj * 32 : fj * 32 + 32, :]
    if second:
        outer, inner = refs[2:]
        odd = (block & 1) == 1
        for f in range(2):
            first = out[pl.ds(f * span, edge), :]
            final = out[pl.ds((f + 1) * span - edge, edge), :]
            outer[pl.ds(f * edge, edge), :] = jnp.where(odd, final, first)
            inner[pl.ds(f * edge, edge), :] = jnp.where(odd, first, final)


def last_apply_kernel(second, both, roots, *refs):
    out = refs[-1]
    core, _, block = my_place()
    parity = 1 - core if second else core
    starts = []
    for chunk in range(4):
        fj = (chunk + 16 - block) & 3
        starts.append((fj >> 1) * (WIDE * LEVELS) + (fj & 1) + (FINAL + HALO * LEVELS))
    for j in range(8):
        s = 2 * j + parity
        field = jnp.concatenate(
            [both[pl.ds(at + 2 * s, MINE, stride=LEVELS), :] for at in starts], axis=0
        )
        result = dot_split(weights_of(roots, j), split(field), turned=True)
        for g in range(GROUP):
            out[pl.ds(pl.multiple_of((g * GROUP + s) * 8, 8), 8), :] = result[g * 8 : g * 8 + 8, :]


def place_kernel(got, out, tiles):
    flip = my_place()[1]
    starts = [jnp.bitwise_xor(MEMBER_AT[k], flip) * 128 for k in range(GROUP)]
    lane = iota((16, 128), 1)
    for t in range(4):
        for n in range(8):
            rows = [got[pl.ds(starts[4 * t + p] + n, 16, stride=8), :] for p in range(4)]
            for fj in range(4):
                block = rows[(0 - fj) % 4]
                for chunk in range(1, 4):
                    block = jnp.where(lane >= 32 * chunk, rows[(chunk - fj) % 4], block)
                if fj > 0:
                    block = pltpu.roll(block, 128 - 32 * fj, 1)
                tiles[pl.ds(512 * t + (n * 2 + fj // 2) * LEVELS + fj % 2, 16, stride=2), :] = block
    for t in range(4):
        out[:, pl.ds(128 * t, 128)] = tiles[pl.ds(512 * t, 512), :]


def vmem():
    return pl.BlockSpec(memory_space=pltpu.VMEM)


def call(kernel, out, ins, name, scratch=(), aliases=None, cost=None):
    return pl.pallas_call(
        kernel,
        out_shape=out,
        in_specs=ins,
        out_specs=jax.tree.map(lambda _: vmem(), out),
        scratch_shapes=scratch,
        input_output_aliases=aliases or {},
        cost_estimate=cost,
        compiler_params=pltpu.CompilerParams(vmem_limit_bytes=VMEM_LIMIT),
        name=name,
    )


def arr(*shape, dtype=F32):
    return jax.ShapeDtypeStruct(shape, dtype)


def holder(block, hor):
    g = MEMBER_AT[block] ^ (15 * (hor & 1))
    return ((g >> 2) * 16 + hor) * 4 + (g & 3)


def block_pairs(start):
    pairs = []
    for hor in range(16):
        for block in range(start, GROUP, 2):
            after = block + 1
            pair = (holder(block, hor), holder(after % GROUP, (hor + after // GROUP) % 16))
            pairs += [pair, pair[::-1]]
    return pairs


def swap(x):
    return lax.ppermute(x, "core", [(0, 1), (1, 0)])


def exchange(x, axes):
    return lax.all_to_all(x, axes, split_axis=0, concat_axis=0, tiled=True)


def shards(ensemble, coupling, obs_column, obs_level, obs_value, obs_error, obs_live, partners):
    rows = MINE * LEVELS
    edges = 2 * HALO * LEVELS
    members = ensemble.reshape(512, COLS)
    early = pl.CostEstimate(flops=10**10, bytes_accessed=3 * 2**20, transcendentals=0)
    cost = pl.CostEstimate(flops=10**9, bytes_accessed=3 * 2**20, transcendentals=0)
    near, far = call(edges_kernel, (arr(HALO, COLS), arr(HALO, COLS)), [vmem()], "edges", cost=early)(members)
    far = lax.ppermute(far, "hor", [(i, (i - 1 + 2 * (i & 1)) % 16) for i in range(16)])
    near = lax.ppermute(near, "hor", [(i, i ^ 1) for i in range(16)])
    state, sums, mixing = call(
        prepare_kernel,
        (arr(2 * rows, 128), arr(128, 128), arr(2 * MIX, MIX, dtype=BF16)),
        [vmem()] * 8,
        "prepare",
        [pltpu.VMEM((2048, 128), F32), pltpu.VMEM((2048, 128), F32)],
    )(partners, members, obs_column, obs_level, obs_value, obs_error, obs_live, coupling)
    wide = pltpu.VMEM((WIDE * LEVELS, WIDTH), F32)
    all_levels = arr(SUBSTEPS * 2 * WIDE * LEVELS, WIDTH)
    inside = call(inner_kernel, all_levels, [vmem()] * 2, "inside", [wide], cost=cost)
    packed, _ = call(
        first_kernel,
        (arr(GROUP * 136, 128), all_levels),
        [vmem()] * 6,
        "first",
        [wide, pltpu.VMEM((4 * HALO * LEVELS, 128), F32), pltpu.VMEM((64, 128), F32)],
        aliases={0: 1},
    )(inside(state, mixing), state, near, far, sums, mixing)
    received = exchange(packed.reshape(GROUP, 136, 128), TILE).reshape(GROUP * 136, 128)
    folded = pltpu.VMEM((GROUP, FOLD, 128), F32)
    scalars = pltpu.SMEM((GROUP, 128), jnp.int32)
    keep, send, hist, table = call(
        first_gram_kernel,
        (arr(8, FOLD, 128), arr(8, FOLD, 128), arr(GROUP, 128), arr(GROUP, 128, dtype=jnp.int32)),
        [vmem()],
        "gram",
        [folded, scalars, pltpu.SemaphoreType.DMA(())],
    )(received)

    def roots(keep, send):
        parts = exchange(keep + swap(send), CHIPS)
        copies = call(root_kernel, arr(8, FOLD, 128), [vmem()], "root")(parts)
        same = exchange(copies, CHIPS)
        return same, swap(same)

    same, other = roots(keep, send)
    part = call(
        functools.partial(first_apply_kernel, False),
        arr(2 * rows, WIDTH),
        [vmem()] * 2,
        "apply",
        cost=cost,
    )(received, same)
    state, outer, inner = call(
        functools.partial(first_apply_kernel, True),
        (arr(2 * rows, WIDTH),) + (arr(edges, WIDTH),) * 2,
        [vmem()] * 3,
        "apply",
        aliases={2: 0},
    )(received, other, part)
    outer = lax.ppermute(outer, ALL, block_pairs(1))
    inner = lax.ppermute(inner, ALL, block_pairs(0))
    both, keep, send = call(
        forecast_kernel,
        (all_levels, arr(8, FOLD, 128), arr(8, FOLD, 128)),
        [vmem()] * 7,
        "forecast",
        [wide, folded, pltpu.VMEM((4 * HALO * LEVELS, 128), F32), scalars, pltpu.SemaphoreType.DMA(())],
        aliases={0: 0},
    )(inside(state, mixing), table, state, outer, inner, hist, mixing)
    same, other = roots(keep, send)
    part = call(
        functools.partial(last_apply_kernel, False),
        arr(GROUP * 128, 128),
        [vmem()] * 2,
        "analyse",
        cost=cost,
    )(both, same)
    analysed = call(
        functools.partial(last_apply_kernel, True),
        arr(GROUP * 128, 128),
        [vmem()] * 3,
        "analyse",
        aliases={2: 0},
    )(both, other, part)
    got = exchange(analysed.reshape(GROUP, 128, 128), TILE).reshape(GROUP * 128, 128)
    placed = call(place_kernel, arr(512, 512), [vmem()], "place", [pltpu.VMEM((2048, 128), F32)])(got)
    return placed.reshape(ensemble.shape)


def solution(mesh):
    fine = Mesh(mesh.devices.reshape(4, 16, 2, 2), ALL)
    group = TILE
    in_specs = (
        P(group, None, None, "hor"),
        P(),
        P(None, group, "hor", None),
        P(None, group, "hor", None),
        P(None, group, "hor", None),
        P(None, group, "hor", None),
        P(None, group, "hor", None),
        P(group, "hor", None),
    )
    out_specs = P(group, None, None, "hor")
    return jax.shard_map(shards, mesh=fine, in_specs=in_specs, out_specs=out_specs, check_vma=False)
```

```python
import functools
import math

import jax
import jax.numpy as jnp
from jax import lax
from jax.experimental import pallas as pl
from jax.experimental.pallas import tpu as pltpu
from jax.sharding import Mesh, PartitionSpec as P

SUBSTEPS = 4
ROOT_STEPS = 8
RATE = 0.5 * 0.2
MIX = 128
GROUP = 16
WIDTH = 128
LEVELS = 32
COLS = 512
MINE = COLS // GROUP
HALO = 2 * SUBSTEPS
WIDE = MINE + 2 * HALO
FINAL = (4 - 1) * 2 * WIDE * 32
FOLD = 72
F32 = jnp.float32
BF16 = jnp.bfloat16
VMEM_LIMIT = 16 * 1024 * 1024
ALL = ("mem", "hor", "zh", "core")
TILE = ("mem", "zh", "core")
CHIPS = ("mem", "zh")


def block_of(g):
    return ((g >> 1) & 1) * 8 + (g >> 2) * 2 + (g & 1)


MEMBER_AT = {block_of(g): g for g in range(GROUP)}


def my_place():
    core = lax.axis_index("core")
    flip = 15 * (lax.axis_index("hor") & 1)
    g = lax.axis_index("mem") * 4 + lax.axis_index("zh") * 2 + core
    return core, flip, block_of(jnp.bitwise_xor(g, flip))


def split(a):
    high = a.astype(BF16)
    return high, (a - high.astype(F32)).astype(BF16)


def dot_split(a, b, turned=False):
    left = jnp.concatenate([a[0], a[0], a[1]], axis=1)
    right = jnp.concatenate([b[0], b[1], b[0]], axis=1 if turned else 0)
    dims = (((1,), (1 if turned else 0,)), ((), ()))
    return lax.dot_general(left, right, dims, preferred_element_type=F32)


def iota(shape, dim):
    return lax.broadcasted_iota(jnp.int32, shape, dim)


def chunk_transpose(rows):
    lane = iota(rows[0].shape, 1)
    out = []
    for p in range(4):
        total = None
        for q in range(4):
            piece = rows[q] if p == q else pltpu.roll(rows[q], (32 * (q - p)) % 128, 1)
            total = piece if total is None else jnp.where(lane >= 32 * q, piece, total)
        out.append(total)
    return out


def edges_kernel(ens, near, far):
    first = ens[:, 0:128].T[0:HALO, :]
    last = ens[:, COLS - 128 : COLS].T[128 - HALO :, :]
    even = my_place()[1] == 0
    near[...] = jnp.where(even, last, first)
    far[...] = jnp.where(even, first, last)


def prepare_kernel(
    partner, ens, column, level, value, error, live, coupling, state, out, mixing, tiles, blocks
):
    for t in range(4):
        tiles[pl.ds(512 * t, 512), :] = ens[:, pl.ds(128 * t, 128)]
    for f in range(2):
        for t in range(4):
            for m in range(8):
                at = t * 512 + (m * 2 + f) * LEVELS
                rows = [tiles[pl.ds(at + i, 8, stride=4), :] for i in range(4)]
                for p, block in enumerate(chunk_transpose(rows)):
                    blocks[pl.ds(f * 1024 + (4 * t + p) * 8 + m, 8, stride=128), :] = block
        for four in range(8):
            turned = blocks[pl.ds(f * 1024 + four * 128, 128), :].T
            for i in range(4):
                at = f * MINE * LEVELS + 4 * four + i
                state[pl.ds(at, MINE, stride=LEVELS), :] = turned[32 * i : 32 * i + 32, :]
    member = jnp.bitwise_xor(iota((GROUP, COLS), 0), my_place()[1])
    place = ((member >> 1) & 1) * 8 + (member >> 2) * 2 + (member & 1)
    spot = iota((64, COLS), 0)
    zero = jnp.zeros((64, COLS), F32)
    for cycle in range(2):
        col = column[cycle, 0]
        weight = live[cycle, 0].astype(F32) / error[cycle, 0]
        weighted = weight * value[cycle, 0]
        here = (col >> 5) == place
        left = jnp.concatenate([jnp.where(here, weight, 0.0), jnp.where(here, weighted, 0.0)], axis=1)
        hit = jnp.where(level[cycle, 0] * 32 + (col & 31) == spot, 1.0, 0.0)
        right = jnp.concatenate(
            [jnp.concatenate([hit, zero], axis=1), jnp.concatenate([zero, hit], axis=1)], axis=0
        )
        sums = lax.dot_general(
            left, right, (((1,), (1,)), ((), ())), precision=lax.Precision.HIGHEST, preferred_element_type=F32
        )
        out[pl.ds(cycle, GROUP, stride=8), :] = sums
    lane = iota((GROUP, 128), 1)
    both = partner[0].astype(F32)
    out[pl.ds(2, GROUP, stride=8), :] = jnp.where(lane == 0, both[:, 0:1], both[:, 1:2])
    wide = jnp.concatenate([coupling[...]] * (MIX // LEVELS), axis=1)
    wide = jnp.concatenate([wide] * (MIX // LEVELS), axis=0)
    wide = jnp.where((iota((MIX, MIX), 0) >> 5) == (iota((MIX, MIX), 1) >> 5), RATE * RATE * wide, 0.0)
    high, rest = split(wide)
    mixing[pl.ds(0, MIX), :] = high
    mixing[pl.ds(MIX, MIX), :] = rest


def rows_after(sources, levels, step, f, c, count=1):
    if step == 0:
        ref, at = sources(f, c)
        return ref[pl.ds(at, count * LEVELS), :]
    return levels[pl.ds(((step - 1) * 2 + f) * WIDE * LEVELS + c * LEVELS, count * LEVELS), :]


def pressures(step, groups, sources, levels, ps, mixing):
    mix = (mixing[pl.ds(0, MIX), :], mixing[pl.ds(MIX, MIX), :])
    many = MIX // LEVELS
    for c in groups:
        block = jnp.concatenate(
            [rows_after(sources, levels, step - 1, 1, c, many), rows_after(sources, levels, step - 1, 1, c + many, many)],
            axis=1,
        )
        pressure = dot_split(mix, split(block))
        ps[pl.ds(c * LEVELS, MIX), :] = pressure[:, :128]
        ps[pl.ds(c * LEVELS + MIX, MIX), :] = pressure[:, 128:]


def sweep(step, start, stop, new, sources, levels, ps):
    last = step == SUBSTEPS

    def speed(at, c):
        value = rows_after(sources, levels, at, 0, c)
        return RATE * value if at in (0, SUBSTEPS) else value

    def slope(c):
        return ps[pl.ds(c * LEVELS, LEVELS), :]

    def put(f, c, value):
        levels[pl.ds(((step - 1) * 2 + f) * WIDE * LEVELS + c * LEVELS, LEVELS), :] = value

    flux_two, flux_one, height_one = None, None, None
    for c in range(start, stop):
        if new[0] <= c < new[1]:
            here = speed(step - 1, c)
            change = here * (speed(step - 1, c + 1) - speed(step - 1, c - 1))
            moved = (here - change) - (slope(c + 1) - slope(c - 1))
            put(0, c, moved * (1.0 / RATE) if last else moved)
        else:
            moved = speed(step, c)
        height = rows_after(sources, levels, step - 1, 1, c)
        flux = moved * height
        if c >= start + 2:
            put(1, c - 1, height_one - (flux - flux_two))
        flux_two, flux_one, height_one = flux_one, flux, height


def inner_kernel(state, mixing, levels, ps):
    span = MINE * LEVELS

    def sources(f, c):
        return state, f * span + (c - HALO) * LEVELS

    blank = jnp.zeros((LEVELS, 128), F32)
    for step in range(1, SUBSTEPS + 1):
        lo, hi = HALO + 2 * step, HALO + MINE - 2 * step
        if step < SUBSTEPS:
            for c in [*range(HALO, lo), *range(hi, HALO + MINE)]:
                levels[pl.ds(((step - 1) * 2 + 1) * WIDE * LEVELS + c * LEVELS, LEVELS), :] = blank
        pressures(step, range(HALO, HALO + MINE, 8), sources, levels, ps, mixing)
        sweep(step, lo - 1, hi + 1, (lo - 1, hi + 1), sources, levels, ps)


def outer_steps(sources, levels, ps, mixing):
    blank = jnp.zeros((LEVELS, 128), F32)
    for step in range(1, SUBSTEPS + 1):
        lo, hi = 2 * step, WIDE - 2 * step
        if step < SUBSTEPS:
            for c in [*range(lo), *range(hi, WIDE)]:
                levels[pl.ds(((step - 1) * 2 + 1) * WIDE * LEVELS + c * LEVELS, LEVELS), :] = blank
        pressures(step, (0, HALO, WIDE - 2 * HALO, WIDE - HALO), sources, levels, ps, mixing)
        sweep(step, lo - 1, lo + HALO + 1, (lo - 1, lo + HALO - 1), sources, levels, ps)
        sweep(step, hi - HALO - 1, hi + 1, (hi - HALO + 1, hi + 1), sources, levels, ps)


def four_levels(ref, at, four):
    rows = [ref[pl.ds(at + 4 * four + i, MINE, stride=LEVELS), :] for i in range(4)]
    return jnp.concatenate(rows, axis=0)


def slab_rows(ref, at, s):
    rows = [
        ref[pl.ds(f * WIDE * LEVELS + at + 2 * s + j, MINE, stride=LEVELS), :] for f in range(2) for j in range(2)
    ]
    return jnp.concatenate(rows, axis=0)


def first_kernel(levels_in, state, near, far, sums, mixing, packed, levels, ps, sides, spare):
    del levels_in
    span = MINE * LEVELS
    edge = HALO * LEVELS
    pieces = []
    flip = my_place()[1]
    even = flip == 0
    for before, after in ((far, near), (near, far)):
        for m in range(8):
            lanes = pl.ds(128 * (m // 2), 128)
            line = jnp.where(even, before[:, lanes], after[:, lanes])
            spare[pl.ds(8 * m, 8), :] = line if m % 2 == 0 else pltpu.roll(line, 64, 1)
        pieces += [spare[pl.ds(c, 8, stride=8), :] for c in range(8)]
    halo = jnp.concatenate(pieces, axis=0).T
    lane = iota((LEVELS, 128), 1)
    for f in range(2):
        line = halo[f * LEVELS : (f + 1) * LEVELS, :]
        for c in range(HALO):
            inner = pltpu.roll(state[pl.ds(f * span + (MINE - HALO + c) * LEVELS, LEVELS), :], 8, 1)
            outer = pltpu.roll(line, (128 - 8 * c) % 128, 1)
            sides[pl.ds((2 * f) * edge + c * LEVELS, LEVELS), :] = jnp.where(lane < 8, outer, inner)
            inner = pltpu.roll(state[pl.ds(f * span + c * LEVELS, LEVELS), :], 120, 1)
            outer = pltpu.roll(line, (56 - 8 * c) % 128, 1)
            sides[pl.ds((2 * f + 1) * edge + c * LEVELS, LEVELS), :] = jnp.where(lane >= 120, outer, inner)

    def sources(f, c):
        if c < HALO:
            return sides, 2 * f * edge + c * LEVELS
        if c < HALO + MINE:
            return state, f * span + (c - HALO) * LEVELS
        return sides, (2 * f + 1) * edge + (c - HALO - MINE) * LEVELS

    outer_steps(sources, levels, ps, mixing)
    starts = [jnp.bitwise_xor(MEMBER_AT[k], flip) * 136 for k in range(GROUP)]
    for s in range(GROUP):
        square = slab_rows(levels, FINAL + edge, s).T
        for k in range(GROUP):
            packed[pl.ds(starts[k] + 8 * s, 8), :] = square[8 * k : 8 * k + 8, :]
    for g in range(GROUP):
        packed[pl.ds(g * 136 + 128, 8), :] = sums[pl.ds(g * 8, 8), :]


def square_of(ref, s):
    return jnp.concatenate([ref[pl.ds(g * 136 + s * 8, 8), :] for g in range(GROUP)], axis=0)


def fold(top, bottom, vector, extra=0.0):
    row, lane = iota((64, 128), 0), iota((64, 128), 1)
    body = jnp.where((lane >= 64) | (row <= lane), top, pltpu.roll(bottom, 64, 1))
    diagonal = jnp.sum(jnp.where(lane == row + 64, bottom, 0.0), axis=0, keepdims=True)
    at = iota((8, 128), 0)
    tail = jnp.where(at == 0, diagonal, jnp.where(at == 1, vector, extra))
    return body, tail


def half_of(body, tail):
    row, lane = iota((64, 128), 0), iota((64, 128), 1)
    top = jnp.where((lane >= 64) | (row < lane), body, jnp.where(row == lane, 0.5 * body, 0.0))
    moved = pltpu.roll(body, 64, 1)
    bottom = jnp.where(row > lane - 64, moved, jnp.where(row == lane - 64, 0.5 * tail[0:1, :], 0.0))
    bottom = jnp.where(lane >= 64, bottom, 0.0)
    return jnp.concatenate([top, bottom], axis=0)


def blend(fs, table, core, keep, send):
    for j in range(GROUP // 2):
        for which, ref in ((core, keep), (1 - core, send)):
            s = 2 * j + which
            ref[j] = fs[s] + fs[table[s, 0]] + fs[table[s, 1]]


def gram_of(fs, q, anomaly, halves, mean, line, upper):
    lane = iota((1, 128), 1)
    swapped = pltpu.roll(line, 64, 1)
    mine = (lane >= 64) if upper else (lane < 64)
    weight = jnp.where(mine, swapped if upper else line, 0.0)
    pull = jnp.where(mine, line if upper else swapped, 0.0) - weight * mean
    left = jnp.concatenate([anomaly * weight, jnp.broadcast_to(pull, (8, 128))], axis=0)
    gram = dot_split(split(left), halves, turned=True)
    body, tail = fold(gram[:64], gram[64:128], gram[128:129])
    fs[q, pl.ds(0, 64), :] = body
    fs[q, pl.ds(64, 8), :] = tail


def centred(square):
    mean = jnp.mean(square, axis=0, keepdims=True)
    anomaly = square - mean
    return anomaly, split(anomaly), mean


def first_gram_kernel(got, keep, send, later, table_out, fs, table, sem):
    table_out[...] = got[pl.ds(130, GROUP, stride=136), :].astype(jnp.int32)
    copy = pltpu.make_async_copy(table_out, table, sem)
    copy.start()
    later[...] = got[pl.ds(129, GROUP, stride=136), :]
    for q in range(GROUP):
        gram_of(fs, q, *centred(square_of(got, q)), got[pl.ds(q * 136 + 128, 1), :], True)
    copy.wait()
    blend(fs, table, my_place()[0], keep, send)


def forecast_kernel(levels_in, table_in, state, outer, inner, hist, mixing, levels, keep, send, ps, fs, sides, table, sem):
    del levels_in
    edge = HALO * LEVELS
    span = MINE * LEVELS
    copy = pltpu.make_async_copy(table_in, table, sem)
    copy.start()
    odd = (my_place()[2] & 1) == 1
    for f in range(2):
        rows = pl.ds(f * edge, edge)
        sides[pl.ds(2 * f * edge, edge), :] = jnp.where(odd, inner[rows, :], outer[rows, :])
        sides[pl.ds((2 * f + 1) * edge, edge), :] = jnp.where(odd, outer[rows, :], inner[rows, :])

    def sources(f, c):
        if c < HALO:
            return sides, 2 * f * edge + c * LEVELS
        if c < HALO + MINE:
            return state, f * span + (c - HALO) * LEVELS
        return sides, (2 * f + 1) * edge + (c - HALO - MINE) * LEVELS

    outer_steps(sources, levels, ps, mixing)
    for four in range(8):
        parts = centred(four_levels(levels, FINAL + WIDE * LEVELS + edge, four).T)
        for half in range(2):
            q = 2 * four + half
            gram_of(fs, q, *parts, hist[pl.ds(q, 1), :], half == 1)
    copy.wait()
    blend(fs, table, my_place()[0], keep, send)


def root_kernel(got, out):
    total = got[0]
    for j in range(1, 8):
        total = total + got[j]
    half = half_of(total[:64], total[64:])
    gram, vector = half + half.T, total[65:66]
    eye = jnp.where(iota((WIDTH, WIDTH), 0) == iota((WIDTH, WIDTH), 1), 1.0, 0.0)
    third = 1.0 / 3.0
    blended = (WIDTH - 1.0) * eye + gram * third
    pull = vector * third
    squared = jnp.sum(jnp.sum(blended * blended, axis=0, keepdims=True), axis=1, keepdims=True)
    norm = jnp.sqrt(squared)
    a = blended / norm
    newton = 1.5 * eye - 0.5 * a
    a = dot_split(split(a), split(newton))
    z = newton
    for step in range(1, ROOT_STEPS):
        newton = 1.5 * eye - 0.5 * dot_split(split(z), split(a))
        if step < ROOT_STEPS - 1:
            both = dot_split(split(jnp.concatenate([a, z], axis=0)), split(newton))
            a, z = both[:WIDTH], both[WIDTH:]
        else:
            z = dot_split(split(z), split(newton))
    inner = jnp.sum(z * pull, axis=1, keepdims=True)
    shift = jnp.sum(z * inner, axis=0, keepdims=True) / norm
    spread = z * (math.sqrt(WIDTH - 1.0) / jnp.sqrt(norm))
    sums = jnp.sum(spread, axis=0, keepdims=True) + jnp.sum(shift, axis=1, keepdims=True)
    body, tail = fold(spread[:64], spread[64:], shift, (1.0 - sums) * (1.0 / WIDTH))
    for j in range(8):
        out[j, pl.ds(0, 64), :] = body
        out[j, pl.ds(64, 8), :] = tail


def weights_of(roots, j):
    body, tail = roots[j, pl.ds(0, 64), :], roots[j, pl.ds(64, 8), :]
    half = half_of(body, tail)
    return split((half + tail[1:2, :]) + (half + tail[2:3, :]).T)


def keep_halves(ready, j, halves):
    ready[j, pl.ds(0, 128), :] = halves[0]
    ready[j, pl.ds(128, 128), :] = halves[1]


def kept_halves(ready, j):
    return ready[j, pl.ds(0, 128), :], ready[j, pl.ds(128, 128), :]


def first_apply_kernel(second, roots, *refs):
    core, _, block = my_place()
    if second:
        _, ready, out, outer, inner = refs
    else:
        got, out, ready = refs
    span = MINE * LEVELS
    edge = HALO * LEVELS

    def square(s):
        return jnp.concatenate(
            [got[pl.ds(pl.multiple_of(g * 136 + s * 8, 8), 8), :] for g in range(GROUP)], axis=0
        )

    for j in range(8):
        s = 2 * j + (1 - core if second else core)
        halves = kept_halves(ready, j) if second else split(square(s))
        result = dot_split(weights_of(roots, j), halves).T
        for fj in range(4):
            at = (fj // 2) * span + 2 * s + fj % 2
            out[pl.ds(at, MINE, stride=LEVELS), :] = result[fj * 32 : fj * 32 + 32, :]
        if not second:
            keep_halves(ready, j, split(square(2 * j + 1 - core)))
    if second:
        odd = (block & 1) == 1
        for f in range(2):
            first = out[pl.ds(f * span, edge), :]
            final = out[pl.ds((f + 1) * span - edge, edge), :]
            outer[pl.ds(f * edge, edge), :] = jnp.where(odd, final, first)
            inner[pl.ds(f * edge, edge), :] = jnp.where(odd, first, final)


def last_apply_kernel(second, roots, *refs):
    core, _, block = my_place()
    if second:
        _, ready, out = refs
    else:
        both, out, ready = refs
    starts = []
    for chunk in range(4):
        fj = (chunk + 16 - block) & 3
        starts.append((fj >> 1) * (WIDE * LEVELS) + (fj & 1) + (FINAL + HALO * LEVELS))

    def field(s):
        return jnp.concatenate([both[pl.ds(at + 2 * s, MINE, stride=LEVELS), :] for at in starts], axis=0)

    for j in range(8):
        s = 2 * j + (1 - core if second else core)
        halves = kept_halves(ready, j) if second else split(field(s))
        result = dot_split(weights_of(roots, j), halves, turned=True)
        for g in range(GROUP):
            out[pl.ds(pl.multiple_of((g * GROUP + s) * 8, 8), 8), :] = result[g * 8 : g * 8 + 8, :]
        if not second:
            keep_halves(ready, j, split(field(2 * j + 1 - core)))


def place_kernel(got, out, tiles):
    flip = my_place()[1]
    starts = [jnp.bitwise_xor(MEMBER_AT[k], flip) * 128 for k in range(GROUP)]
    lane = iota((16, 128), 1)
    for t in range(4):
        for n in range(8):
            rows = [got[pl.ds(starts[4 * t + p] + n, 16, stride=8), :] for p in range(4)]
            for fj in range(4):
                block = rows[(0 - fj) % 4]
                for chunk in range(1, 4):
                    block = jnp.where(lane >= 32 * chunk, rows[(chunk - fj) % 4], block)
                if fj > 0:
                    block = pltpu.roll(block, 128 - 32 * fj, 1)
                tiles[pl.ds(512 * t + (n * 2 + fj // 2) * LEVELS + fj % 2, 16, stride=2), :] = block
    for t in range(4):
        out[:, pl.ds(128 * t, 128)] = tiles[pl.ds(512 * t, 512), :]


def vmem():
    return pl.BlockSpec(memory_space=pltpu.VMEM)


def call(kernel, out, ins, name, scratch=(), aliases=None, cost=None):
    return pl.pallas_call(
        kernel,
        out_shape=out,
        in_specs=ins,
        out_specs=jax.tree.map(lambda _: vmem(), out),
        scratch_shapes=scratch,
        input_output_aliases=aliases or {},
        cost_estimate=cost,
        compiler_params=pltpu.CompilerParams(vmem_limit_bytes=VMEM_LIMIT),
        name=name,
    )


def arr(*shape, dtype=F32):
    return jax.ShapeDtypeStruct(shape, dtype)


def holder(block, hor):
    g = MEMBER_AT[block] ^ (15 * (hor & 1))
    return ((g >> 2) * 16 + hor) * 4 + (g & 3)


def block_pairs(start):
    pairs = []
    for hor in range(16):
        for block in range(start, GROUP, 2):
            after = block + 1
            pair = (holder(block, hor), holder(after % GROUP, (hor + after // GROUP) % 16))
            pairs += [pair, pair[::-1]]
    return pairs


def swap(x):
    return lax.ppermute(x, "core", [(0, 1), (1, 0)])


def exchange(x, axes):
    return lax.all_to_all(x, axes, split_axis=0, concat_axis=0, tiled=True)


def shards(ensemble, coupling, obs_column, obs_level, obs_value, obs_error, obs_live, partners):
    rows = MINE * LEVELS
    edges = 2 * HALO * LEVELS
    members = ensemble.reshape(512, COLS)
    early = pl.CostEstimate(flops=10**10, bytes_accessed=3 * 2**20, transcendentals=0)
    cost = pl.CostEstimate(flops=10**9, bytes_accessed=3 * 2**20, transcendentals=0)
    near, far = call(edges_kernel, (arr(HALO, COLS), arr(HALO, COLS)), [vmem()], "edges", cost=early)(members)
    far = lax.ppermute(far, "hor", [(i, (i - 1 + 2 * (i & 1)) % 16) for i in range(16)])
    near = lax.ppermute(near, "hor", [(i, i ^ 1) for i in range(16)])
    state, sums, mixing = call(
        prepare_kernel,
        (arr(2 * rows, 128), arr(128, 128), arr(2 * MIX, MIX, dtype=BF16)),
        [vmem()] * 8,
        "prepare",
        [pltpu.VMEM((2048, 128), F32), pltpu.VMEM((2048, 128), F32)],
    )(partners, members, obs_column, obs_level, obs_value, obs_error, obs_live, coupling)
    wide = pltpu.VMEM((WIDE * LEVELS, WIDTH), F32)
    all_levels = arr(SUBSTEPS * 2 * WIDE * LEVELS, WIDTH)
    inside = call(inner_kernel, all_levels, [vmem()] * 2, "inside", [wide], cost=cost)
    packed, _ = call(
        first_kernel,
        (arr(GROUP * 136, 128), all_levels),
        [vmem()] * 6,
        "first",
        [wide, pltpu.VMEM((4 * HALO * LEVELS, 128), F32), pltpu.VMEM((64, 128), F32)],
        aliases={0: 1},
    )(inside(state, mixing), state, near, far, sums, mixing)
    received = exchange(packed.reshape(GROUP, 136, 128), TILE).reshape(GROUP * 136, 128)
    folded = pltpu.VMEM((GROUP, FOLD, 128), F32)
    scalars = pltpu.SMEM((GROUP, 128), jnp.int32)
    keep, send, hist, table = call(
        first_gram_kernel,
        (arr(8, FOLD, 128), arr(8, FOLD, 128), arr(GROUP, 128), arr(GROUP, 128, dtype=jnp.int32)),
        [vmem()],
        "gram",
        [folded, scalars, pltpu.SemaphoreType.DMA(())],
    )(received)

    def roots(keep, send):
        parts = exchange(keep + swap(send), CHIPS)
        copies = call(root_kernel, arr(8, FOLD, 128), [vmem()], "root")(parts)
        same = exchange(copies, CHIPS)
        return same, swap(same)

    same, other = roots(keep, send)
    ready = arr(8, 256, 128, dtype=BF16)
    part, halves = call(
        functools.partial(first_apply_kernel, False),
        (arr(2 * rows, WIDTH), ready),
        [vmem()] * 2,
        "apply",
        cost=cost,
    )(same, received)
    state, outer, inner = call(
        functools.partial(first_apply_kernel, True),
        (arr(2 * rows, WIDTH),) + (arr(edges, WIDTH),) * 2,
        [vmem()] * 3,
        "apply",
        aliases={1: 0},
    )(other, part, halves)
    outer = lax.ppermute(outer, ALL, block_pairs(1))
    inner = lax.ppermute(inner, ALL, block_pairs(0))
    both, keep, send = call(
        forecast_kernel,
        (all_levels, arr(8, FOLD, 128), arr(8, FOLD, 128)),
        [vmem()] * 7,
        "forecast",
        [wide, folded, pltpu.VMEM((4 * HALO * LEVELS, 128), F32), scalars, pltpu.SemaphoreType.DMA(())],
        aliases={0: 0},
    )(inside(state, mixing), table, state, outer, inner, hist, mixing)
    same, other = roots(keep, send)
    part, halves = call(
        functools.partial(last_apply_kernel, False),
        (arr(GROUP * 128, 128), ready),
        [vmem()] * 2,
        "analyse",
        cost=cost,
    )(same, both)
    analysed = call(
        functools.partial(last_apply_kernel, True),
        arr(GROUP * 128, 128),
        [vmem()] * 3,
        "analyse",
        aliases={1: 0},
    )(other, part, halves)
    got = exchange(analysed.reshape(GROUP, 128, 128), TILE).reshape(GROUP * 128, 128)
    placed = call(place_kernel, arr(512, 512), [vmem()], "place", [pltpu.VMEM((2048, 128), F32)])(got)
    return placed.reshape(ensemble.shape)


def solution(mesh):
    fine = Mesh(mesh.devices.reshape(4, 16, 2, 2), ALL)
    group = TILE
    in_specs = (
        P(group, None, None, "hor"),
        P(),
        P(None, group, "hor", None),
        P(None, group, "hor", None),
        P(None, group, "hor", None),
        P(None, group, "hor", None),
        P(None, group, "hor", None),
        P(group, "hor", None),
    )
    out_specs = P(group, None, None, "hor")
    return jax.shard_map(shards, mesh=fine, in_specs=in_specs, out_specs=out_specs, check_vma=False)
```
